128 devices in a mesh: lat: 8 (over z, y_hi), lon: 16 (over y_lo, x, core).
Axes of the slice: x: 4, y: 4 (y_hi: 2, y_lo: 2; y = y_hi * 2 + y_lo), z: 4, core: 2. Of those that a mesh axis runs over, the one named last changes fastest.
Arguments:
- mesh_nodes: bfloat16 [65536, 512], P(('lat', 'lon')), may hold values from -6 to 6
- norm_gain: float32 [512], replicated, may hold values from 0.5 to 1.5
- w_query: bfloat16 [512, 512], replicated, may hold values from -0.25 to 0.25
- w_node_kv: bfloat16 [512, 1024], replicated, may hold values from -0.25 to 0.25
- obs_rows: bfloat16 [65536, 256], P(('lat', 'lon')), may hold values from -82 to 82
- w_obs_kv: bfloat16 [256, 1024], replicated, may hold values from -0.375 to 0.375
- obs_owner: int32 [65536, 1], P(('lat', 'lon')), may hold values from 0 to 127; in each aligned block of 512 rows (0 to 511, 512 to 1023, ...) at most 8 rows name the same one
- neighbours: int32 [65536, 32], P(('lat', 'lon')), may hold values from 0 to 1023
- neighbour_mask: int32 [65536, 32], P(('lat', 'lon')), may hold values 0 or 1
- disk_tokens: bfloat16 [1024, 5, 256], P(('lat', 'lon')), may hold values from -6 to 6
- w_disk_kv: bfloat16 [256, 1024], replicated, may hold values from -0.375 to 0.375
- disk_start: int32 [5], replicated, may hold values from 0 to 15
- disk_extent: int32 [5], replicated, may hold values from 4 to 8
- w_out: bfloat16 [512, 512], replicated, may hold values from -0.25 to 0.25
Outputs:
- updated: bfloat16 [65536, 512], P(('lat', 'lon'))
The draws below stay inside these ranges and needn't reach their ends.
Inputs may be any that keep to these rules, and one draw needn't show every extreme that they name: `obs_owner`: in the rows of one device, no owner is named more than 8 times, a bound that some block reaches.
All inputs are finite; a program needn't handle non-finite values. No bound on the sum of `neighbour_mask` on one device may be relied on, other than what follows from the above.
Results may differ from the reference program's by a relative error of at most 0.0039.
The reference program's roundings to bfloat16 on the way count: a program that leaves them out, or rounds other values in their place, can miss the bound.
Values may be sent and summed in bfloat16 or wider, within the bound.
No kernel may reach another device: no remote copies, remote signals or barrier semaphores. Data moves between devices by JAX's collectives and lax.ppermute only.
A program may use at most 128 MiB of HBM per device.

```python
import math
import jax
import jax.numpy as jnp
import numpy as np
from jax import lax

D = 512
HEADS = 8
F_OBS = 256
F_DISK = 256
NEIGH = 32
DISKS = 5
DISK_TOK = 1024
NODE_DEV = 512
OBS_DEV = 512
CAP = 8
SLOTS = 1024
NODES = 65536
OBS = 65536
N_LAT = 8
N_LON = 16
DEVICES = 128


def draw_obs_rows(key, part):
    first_key = jax.random.fold_in(jax.random.fold_in(key, 11), 0)
    base = jax.random.truncated_normal(first_key, -4.0, 4.0, (OBS, F_OBS), jnp.float32)
    return base.astype(jnp.bfloat16)


def draw_disk_extent(key, part):
    least_span = N_LON // 4
    most_span = N_LON // 2
    spans = jax.random.randint(jax.random.fold_in(key, 23), (DISKS,), least_span, most_span + 1)
    spans = spans.at[0].set(most_span).at[1].set(least_span)
    return spans.astype(jnp.int32)


def with_ends(drawn, rng, smallest, high):
    longest = drawn.shape.index(max(drawn.shape))
    spots = []
    for shift in (0, 1):
        where = [jax.random.randint(jax.random.fold_in(rng, axis), (), 0, length) for axis, length in enumerate(drawn.shape)]
        where[longest] = (where[longest] + shift) % drawn.shape[longest]
        spots.append(tuple(where))
    return drawn.at[spots[0]].set(smallest).at[spots[1]].set(high)


def block_scale(stream_key, dims, pieces, least, high):
    factor_of, own = 1.0, jax.random.fold_in(stream_key, 6)
    for dim, parts in pieces:
        draws = jnp.exp(jax.random.uniform(jax.random.fold_in(own, dim), (parts,), jnp.float32, least / len(pieces), high / len(pieces)))
        factor_of = factor_of * jnp.repeat(draws, dims[dim] // parts).reshape([-1 if axis == dim else 1 for axis in range(len(dims))])
    return factor_of


def assign_block(stream_key, own, number, rows, count, top, bound, slope):
    order = jax.random.permutation(stream_key, count)
    heavy_load, ordinary = load_shares(count, rows * top, bound, slope, True), load_shares(count, rows * top, bound, slope, False)
    places = jnp.arange(count)

    def named(tallies, turn):
        used = int((tallies > 0).sum())
        fixed = max(1, used // 4)
        passed = fixed + (places - fixed + turn * (used - fixed)) % max(1, count - fixed)
        return jnp.zeros((count,), jnp.int32).at[order[jnp.where(places < fixed, places, passed)]].set(jnp.asarray(tallies, jnp.int32))

    tallies = jnp.where(number % 4 == 0, named(heavy_load, number // 4), named(ordinary, number - number // 4 - 1))
    mixed = jax.random.permutation(jax.random.fold_in(own, 3), count)
    giver, sink = mixed[0:count // 2 * 2:2], mixed[1:count // 2 * 2:2]
    slack = jnp.minimum(tallies[giver] - 1, bound - tallies[sink]) // 2
    slack = jnp.where((giver == order[0]) | (sink == order[0]) | (tallies[sink] == 0), 0, jnp.maximum(slack, 0))
    passed = jax.random.randint(jax.random.fold_in(own, 4), (count // 2,), 0, 1 << 20) % (slack + 1)
    tallies = tallies.at[giver].add(-passed).at[sink].add(passed)
    labels = jnp.searchsorted(jnp.cumsum(tallies), jnp.arange(rows * top), side="right").astype(jnp.int32)
    listing = labels.reshape(top, rows).T
    listing = listing[jax.random.permutation(jax.random.fold_in(own, 1), rows)]
    turn = jax.random.randint(jax.random.fold_in(own, 2), (rows, 1), 0, top)
    return jnp.take_along_axis(listing, (jnp.arange(top)[None, :] + turn) % top, axis=1)


def load_shares(count, total, reach, lean, full):
    weights = [(1 << 20) // math.isqrt(standing ** lean) + 1 for standing in range(1, count + 1)]
    largest = reach if full else min(reach, max(-(-total // count), total * weights[0] // sum(weights)))
    least = 1 if total - largest >= count - 1 else 0
    counts, rest = [largest] + [least] * (count - 1), total - largest - least * (count - 1)
    while rest > 0:
        movable = [i for i in range(1, count) if counts[i] < largest] or [i for i in range(1, count) if counts[i] < reach]
        pool, budget = sum([weights[i] for i in movable]), rest
        for i in movable:
            extra = min(reach - counts[i], max(1, budget * weights[i] // pool), rest)
            counts[i] = counts[i] + extra
            rest = rest - extra
    return np.array(counts)


def gaussian(own_key, dims, scale, bound, cuts=(), kind=jnp.bfloat16):
    drawn = scale * jax.random.normal(own_key, dims, jnp.float32)
    if cuts:
        drawn = drawn * block_scale(own_key, dims, cuts, -0.22, 0.18)
    return jnp.clip(drawn, -bound, bound).astype(kind)


def setup_inputs(seed: int = 0) -> dict:
    splits = jax.random.split(jax.random.key(seed), 15)
    mesh_nodes = gaussian(splits[0], (NODES, D), 1.0, 6.0, ((0, 128),))
    norm_gain = jnp.clip(1.0 + 0.1 * jax.random.normal(splits[1], (D,), jnp.float32), 0.5, 1.5)
    w_query = gaussian(splits[2], (D, D), D ** -0.5, 0.25)
    w_node_kv = gaussian(splits[3], (D, 2 * D), D ** -0.5, 0.25)
    obs_rows = draw_obs_rows(jax.random.fold_in(splits[14], 71), 0)
    w_obs_kv = gaussian(splits[5], (F_OBS, 2 * D), F_OBS ** -0.5, 0.375)
    obs_owner_keys = jax.random.split(jax.random.fold_in(splits[6], 1), OBS // OBS_DEV)
    obs_owner_turns = jax.random.permutation(jax.random.fold_in(splits[6], 3), OBS // OBS_DEV)
    obs_owner = jax.vmap(lambda own, number: assign_block(jax.random.fold_in(splits[6], 2), own, number, OBS_DEV, DEVICES, 1, CAP, 2))(obs_owner_keys, obs_owner_turns).reshape((OBS, 1))
    neighbours = with_ends(jax.random.randint(splits[7], (NODES, NEIGH), 0, SLOTS), jax.random.fold_in(splits[7], 1), 0, SLOTS - 1).astype(jnp.int32)
    neighbour_mask = with_ends((jax.random.randint(splits[8], (NODES, NEIGH), 0, 4) < 3).astype(jnp.int32), jax.random.fold_in(splits[8], 1), 0, 1)
    disk_tokens = gaussian(splits[9], (DISK_TOK, DISKS, F_DISK), 1.0, 6.0, ((0, 128),))
    w_disk_kv = gaussian(splits[10], (F_DISK, 2 * D), F_DISK ** -0.5, 0.375)
    disk_start = with_ends(jax.random.randint(splits[11], (DISKS,), 0, N_LON), jax.random.fold_in(splits[11], 1), 0, N_LON - 1).astype(jnp.int32)
    disk_extent = draw_disk_extent(jax.random.fold_in(splits[14], 71), 0)
    w_out = gaussian(splits[13], (D, D), D ** -0.5, 0.25)
    return {"mesh_nodes": mesh_nodes, "norm_gain": norm_gain, "w_query": w_query, "w_node_kv": w_node_kv, "obs_rows": obs_rows, "w_obs_kv": w_obs_kv, "obs_owner": obs_owner, "neighbours": neighbours, "neighbour_mask": neighbour_mask, "disk_tokens": disk_tokens, "w_disk_kv": w_disk_kv, "disk_start": disk_start, "disk_extent": disk_extent, "w_out": w_out}


def split_heads(packed, head_count):
    width = packed.shape[-1] // 2
    head_width = width // head_count
    leading = packed.shape[:-1]
    return (packed[..., :width].reshape(leading + (head_count, head_width)), packed[..., width:].reshape(leading + (head_count, head_width)))

def rounded(values):
    return lax.optimization_barrier(values.astype(jnp.bfloat16)).astype(jnp.float32)

def reference(mesh_nodes, norm_gain, w_query, w_node_kv, obs_rows, w_obs_kv, obs_owner, neighbours, neighbour_mask, disk_tokens, w_disk_kv, disk_start, disk_extent, w_out):
    device_count = N_LAT * N_LON
    head_width = D // HEADS
    node_values = mesh_nodes.astype(jnp.float32)
    inverse = lax.rsqrt(lax.optimization_barrier(jnp.mean(node_values * node_values, axis=1, keepdims=True)) + 1e-06)
    normed = (node_values * inverse * norm_gain).astype(jnp.bfloat16)
    query_all = (jnp.dot(normed, w_query, preferred_element_type=jnp.float32) * head_width ** (-0.5)).astype(jnp.bfloat16)
    self_all = jnp.dot(normed, w_node_kv, preferred_element_type=jnp.float32).astype(jnp.bfloat16)
    obs_kv = jnp.dot(obs_rows, w_obs_kv, preferred_element_type=jnp.float32).astype(jnp.bfloat16)
    disk_kv = jnp.einsum('tkf,fe->kte', disk_tokens.astype(jnp.float32), w_disk_kv.astype(jnp.float32)).astype(jnp.bfloat16)
    disk_keys, disk_values = split_heads(disk_kv, HEADS)
    flat_values = disk_values.reshape(DISKS * DISK_TOK, HEADS, head_width).astype(jnp.float32)
    device_ids = jnp.arange(device_count, dtype=jnp.int32)
    obs_dest = obs_owner[:, 0].reshape(device_count, OBS_DEV)
    dest_hot = (obs_dest[:, :, None] == device_ids[None, None, :]).astype(jnp.int32)
    obs_rank = lax.optimization_barrier(jnp.sum((jnp.cumsum(dest_hot, axis=1) - dest_hot) * dest_hot, axis=2))
    source_ids = jnp.broadcast_to(device_ids[:, None], (device_count, OBS_DEV))
    target = (obs_dest * SLOTS + source_ids * CAP + obs_rank).reshape(-1).astype(jnp.int32)
    slot_table = jnp.full((device_count * SLOTS,), -1, jnp.int32).at[target].set(jnp.arange(OBS, dtype=jnp.int32))
    visible_all = jnp.mod(device_ids[:, None] % N_LON - disk_start[None, :], N_LON) < disk_extent[None, :]

    def one_device(device):
        query_heads = lax.dynamic_slice_in_dim(query_all, device * NODE_DEV, NODE_DEV, 0).reshape(NODE_DEV, HEADS, head_width).astype(jnp.float32)
        self_kv = lax.dynamic_slice_in_dim(self_all, device * NODE_DEV, NODE_DEV, 0).astype(jnp.float32)
        self_keys, self_values = split_heads(self_kv, HEADS)
        slot_ids = lax.dynamic_slice_in_dim(slot_table, device * SLOTS, SLOTS, 0)
        filled = slot_ids >= 0
        slot_kv = jnp.where(filled[:, None], obs_kv[jnp.maximum(slot_ids, 0)], jnp.zeros((), jnp.bfloat16))
        listed = lax.dynamic_slice_in_dim(neighbours, device * NODE_DEV, NODE_DEV, 0)
        mark_values = lax.dynamic_slice_in_dim(neighbour_mask, device * NODE_DEV, NODE_DEV, 0)
        valid_slot = (mark_values > 0) & filled[listed]
        near_keys, near_values = split_heads(slot_kv[listed].astype(jnp.float32), HEADS)
        self_scores = lax.optimization_barrier(jnp.sum(query_heads * self_keys, axis=2))
        near_scores = jnp.einsum('nhd,nehd->nhe', query_heads, near_keys)
        near_scores = jnp.where(valid_slot[:, None, :], near_scores, -jnp.inf)
        visible = visible_all[device]
        score_list = []
        for disk_index in range(DISKS):
            score_list.append(lax.cond(visible[disk_index], lambda keys: jnp.einsum('nhd,thd->nht', query_heads, keys), lambda keys: jnp.full((NODE_DEV, HEADS, DISK_TOK), -jnp.inf, query_heads.dtype), disk_keys[disk_index].astype(jnp.float32)))
        disk_scores = jnp.concatenate(score_list, axis=2)
        row_top = jnp.maximum(jnp.maximum(self_scores, lax.optimization_barrier(jnp.max(near_scores, axis=2))), lax.optimization_barrier(jnp.max(disk_scores, axis=2)))
        self_weight = jnp.exp(self_scores - row_top)
        near_weight = jnp.exp(near_scores - row_top[:, :, None])
        disk_weight = jnp.exp(disk_scores - row_top[:, :, None])
        denominator = self_weight + lax.optimization_barrier(jnp.sum(near_weight, axis=2)) + lax.optimization_barrier(jnp.sum(disk_weight, axis=2))
        summed = rounded(self_weight)[:, :, None] * self_values
        summed = summed + jnp.einsum('nhe,nehd->nhd', rounded(near_weight), near_values)
        summed = summed + jnp.einsum('nht,thd->nhd', rounded(disk_weight), flat_values)
        return (summed / denominator[:, :, None]).reshape(NODE_DEV, D).astype(jnp.bfloat16)
    attended = lax.map(one_device, device_ids).reshape(NODES, D)
    mixed_rows = jnp.dot(attended, w_out, preferred_element_type=jnp.float32)
    return (node_values + mixed_rows).astype(jnp.bfloat16)
```

```python
import functools

import jax
import jax.numpy as jnp
from jax import lax
from jax.experimental import pallas as pl
from jax.experimental.pallas import tpu as pltpu
from jax.sharding import PartitionSpec as P

HEADS = 8
AXES = ("lat", "lon")
LOG2E = 1.4426950408889634
EMPTY = 65536.0
NEG = -1e30
BIG = 2.0**100
F32 = jnp.float32
BF16 = jnp.bfloat16
NT = (((1,), (1,)), ((), ()))


def shape(dims, dtype):
    return jax.ShapeDtypeStruct(dims, dtype)


def params(mib):
    return pltpu.CompilerParams(vmem_limit_bytes=mib * 2**20)


def place_kernel(owner_ref, rows_ref, send_ref):
    count = rows_ref.shape[0]
    owners = send_ref.shape[0] // 8
    owner = owner_ref[...]
    hot = owner == lax.broadcasted_iota(jnp.int32, (count, owners), 1)
    hot_f = jnp.where(hot, 1.0, 0.0)
    hot_b = hot_f.astype(BF16)
    row = lax.broadcasted_iota(jnp.int32, (count, count), 0)
    col = lax.broadcasted_iota(jnp.int32, (count, count), 1)
    earlier = jnp.where(col < row, 1.0, 0.0).astype(BF16)
    before = jnp.dot(earlier, hot_b, preferred_element_type=F32)
    rank_b = (before * hot_f).astype(BF16)
    ids = lax.broadcasted_iota(jnp.int32, (8, owners), 1).astype(F32).astype(BF16)
    ones = jnp.ones((8, owners), BF16)
    slot = 8.0 * lax.dot_general(ids, hot_b, NT, preferred_element_type=F32) + lax.dot_general(
        ones, rank_b, NT, preferred_element_type=F32
    )
    slot = slot[0:1, :].astype(jnp.int32)
    rows = rows_ref[...]
    ones_rows = jnp.ones((count, 128), BF16)
    step = 256
    for start in range(0, send_ref.shape[0], step):
        ids_col = lax.broadcasted_iota(jnp.int32, (step, count), 0) + start
        placing = jnp.where(ids_col == slot, 1.0, 0.0).astype(BF16)
        placed = jnp.dot(placing, rows, preferred_element_type=F32)
        filled = jnp.dot(placing, ones_rows, preferred_element_type=F32)
        filled = jnp.concatenate([filled, filled], axis=1)
        send_ref[pl.ds(start, step), :] = jnp.where(filled > 0.5, placed, EMPTY).astype(BF16)


def place(owner, rows, slots):
    return pl.pallas_call(
        place_kernel,
        out_shape=shape((slots, rows.shape[1]), BF16),
        compiler_params=params(16),
        cost_estimate=pl.CostEstimate(flops=10**9, bytes_accessed=10**6, transcendentals=0),
        name="place",
    )(owner, rows)


def node_kernel(x_ref, gain_ref, wq_ref, wkv_ref, wd_ref, query_ref, lifted_ref, own_ref, value_ref):
    x = x_ref[...].astype(F32)
    inverse = lax.rsqrt(jnp.mean(x * x, axis=1, keepdims=True) + 1e-06)
    normed = (x * inverse * gain_ref[...]).astype(BF16)
    query = (jnp.dot(normed, wq_ref[...], preferred_element_type=F32) * 0.125).astype(BF16)
    query_ref[...] = query
    kv = jnp.dot(normed, wkv_ref[...], preferred_element_type=F32).astype(BF16)
    value_ref[...] = kv[:, 512:]
    prod = query.astype(F32) * kv[:, :512].astype(F32)
    lane = lax.broadcasted_iota(jnp.int32, (x.shape[0], 128), 1)
    own = jnp.zeros((x.shape[0], 128), F32)
    for head in range(HEADS):
        part = jnp.sum(prod[:, head * 64 : head * 64 + 64], axis=1, keepdims=True) * LOG2E
        own = jnp.where(lane == head, part, own)
        lifted = lax.dot_general(
            query[:, head * 64 : head * 64 + 64],
            wd_ref[:, head * 64 : head * 64 + 64],
            NT,
            preferred_element_type=F32,
        )
        lifted_ref[pl.ds(head * x.shape[0], x.shape[0]), :] = (lifted * LOG2E).astype(BF16)
    own_ref[...] = own


def node_prep(x, gain, wq, wkv, wd):
    n, d = x.shape
    return pl.pallas_call(
        node_kernel,
        out_shape=(
            shape((n, d), BF16),
            shape((HEADS * n, wd.shape[0]), BF16),
            shape((n, 128), F32),
            shape((n, d), BF16),
        ),
        compiler_params=params(24),
        cost_estimate=pl.CostEstimate(flops=3 * 10**9, bytes_accessed=5 * 10**6, transcendentals=0),
        name="node_prep",
    )(x, gain, wq, wkv, wd)


def count_kernel(near_ref, mark_ref, count_ref):
    slots = count_ref.shape[1]
    step = 64

    def body(i, carry):
        start = pl.multiple_of(i * step, step)
        near = jnp.where(mark_ref[pl.ds(start, step), :] > 0, near_ref[pl.ds(start, step), :], -1)
        near = near.astype(jnp.int16)
        ids = lax.broadcasted_iota(jnp.int16, (step, slots), 1)
        total = jnp.zeros((step, slots), jnp.int16)
        one = jnp.ones((step, slots), jnp.int16)
        for entry in range(near_ref.shape[1]):
            total = jnp.where(ids == near[:, entry : entry + 1], total + one, total)
        count_ref[pl.ds(start, step), :] = total.astype(F32).astype(BF16)
        return carry

    lax.fori_loop(0, near_ref.shape[0] // step, body, 0)


def count_listed(near, mark, slots):
    return pl.pallas_call(
        count_kernel,
        out_shape=shape((near.shape[0], slots), BF16),
        compiler_params=params(16),
        cost_estimate=pl.CostEstimate(flops=4 * 10**9, bytes_accessed=2 * 10**6, transcendentals=0),
        name="count_listed",
    )(near, mark)


def near_kernel(got_ref, w_ref, query_ref, count_ref, own_ref, value_ref, top_ref, sum_ref, acc_ref, kv_ref, bias_ref):
    slots = got_ref.shape[0]
    n = query_ref.shape[0]
    got = got_ref[...]
    absent = got.astype(F32) > 1024.0
    rows = jnp.where(absent, 0.0, got.astype(F32)).astype(BF16)
    kv_ref[...] = jnp.dot(rows, w_ref[...], preferred_element_type=F32).astype(BF16)
    ones = jnp.ones((8, got.shape[1]), BF16)
    empty = lax.dot_general(
        ones, jnp.where(absent, 1.0, 0.0).astype(BF16), NT, preferred_element_type=F32
    )[0:1, :]
    count = count_ref[...].astype(F32)
    bias_ref[...] = jnp.where((count > 0.0) & (empty < 0.5), jnp.log2(jnp.maximum(count, 1.0)), NEG)
    step = 256
    lane = lax.broadcasted_iota(jnp.int32, (step, 128), 1)
    for start in range(0, n, step):
        tops = jnp.zeros((step, 128), F32)
        sums = jnp.ones((step, 128), F32)
        own = own_ref[pl.ds(start, step), :]
        bias = bias_ref[pl.ds(start, step), :]
        for head in range(HEADS):
            lo = head * 64
            scores = lax.dot_general(
                query_ref[pl.ds(start, step), lo : lo + 64],
                kv_ref[:, lo : lo + 64],
                NT,
                preferred_element_type=F32,
            )
            scores = scores * LOG2E + bias
            mine = own[:, head : head + 1]
            best = jnp.maximum(jnp.max(scores, axis=1, keepdims=True), mine)
            weights = jnp.exp2(scores - best)
            self_weight = jnp.exp2(mine - best)
            total = jnp.sum(weights, axis=1, keepdims=True) + self_weight
            part = jnp.dot(
                weights.astype(BF16), kv_ref[:, 512 + lo : 512 + lo + 64], preferred_element_type=F32
            )
            self_b = self_weight.astype(BF16).astype(F32)
            part = part + self_b * value_ref[pl.ds(start, step), lo : lo + 64].astype(F32)
            acc_ref[pl.ds(start, step), lo : lo + 64] = part
            tops = jnp.where(lane == head, best, tops)
            sums = jnp.where(lane == head, total, sums)
        top_ref[pl.ds(start, step), :] = tops
        sum_ref[pl.ds(start, step), :] = sums


def near_attend(got, w, query, count, own, value):
    n, d = query.shape
    return pl.pallas_call(
        near_kernel,
        out_shape=(shape((n, 128), F32), shape((n, 128), F32), shape((n, d), F32)),
        scratch_shapes=[pltpu.VMEM((got.shape[0], 2 * d), BF16), pltpu.VMEM((n, got.shape[0]), F32)],
        compiler_params=params(32),
        cost_estimate=pl.CostEstimate(flops=5 * 10**9, bytes_accessed=5 * 10**6, transcendentals=10**6),
        name="near_attend",
    )(got, w, query, count, own, value)


def disk_kernel(*refs, pieces):
    (vis_ref, lifted_ref), refs = refs[:2], refs[2:]
    piece_refs, refs = refs[:pieces], refs[pieces:]
    own_ref, top_ref, sum_ref, near_ref, wd_ref, wout_ref, x_ref, out_ref, tok_ref, shift_ref, acc_ref, den_ref, att_ref = refs
    n, d = x_ref.shape
    rows = lifted_ref.shape[0]
    disks = piece_refs[0].shape[0]
    size = piece_refs[0].shape[1]
    for head in range(HEADS):
        shift_ref[pl.ds(head * n, n), :] = jnp.broadcast_to(own_ref[:, head : head + 1], (n, 128))

    def load_disk(disk):
        for i, piece in enumerate(piece_refs):
            tok_ref[pl.ds(i * size, size), :] = piece[disk]

    def add_disks(step, unroll):
        den_ref[...] = jnp.zeros_like(den_ref)
        acc_ref[...] = jnp.zeros_like(acc_ref)

        def add_disk(disk, carry):
            @pl.when(vis_ref[disk] > 0)
            def _():
                load_disk(disk)

                def body(i, inner):
                    for u in range(unroll):
                        at = pl.ds(pl.multiple_of((i * unroll + u) * step, step), step)
                        scores = lax.dot_general(
                            lifted_ref[at, :], tok_ref[...], NT, preferred_element_type=F32
                        )
                        weights = jnp.exp2(scores - shift_ref[at, :1])
                        part = weights[:, :128]
                        for j in range(1, weights.shape[1] // 128):
                            part = part + weights[:, j * 128 : j * 128 + 128]
                        den_ref[at, :] += part
                        acc_ref[at, :] += jnp.dot(
                            weights.astype(BF16), tok_ref[...], preferred_element_type=F32
                        )
                    return inner

                lax.fori_loop(0, rows // (step * unroll), body, 0)

            return carry

        lax.fori_loop(0, disks, add_disk, 0)

    add_disks(256, 8)

    worst = jnp.max(jnp.max(den_ref[...], axis=0, keepdims=True))

    @pl.when(jnp.logical_not(worst < BIG))
    def _():
        def top_disk(disk, carry):
            @pl.when(vis_ref[disk] > 0)
            def _():
                load_disk(disk)

                def body(i, inner):
                    at = pl.ds(pl.multiple_of(i * 256, 256), 256)
                    scores = lax.dot_general(
                        lifted_ref[at, :], tok_ref[...], NT, preferred_element_type=F32
                    )
                    best = jnp.max(scores, axis=1, keepdims=True)
                    shift_ref[at, :] = jnp.maximum(shift_ref[at, :], best)
                    return inner

                lax.fori_loop(0, rows // 256, body, 0)

            return carry

        lax.fori_loop(0, disks, top_disk, 0)
        add_disks(256, 1)

    for head in range(HEADS):
        lo = head * 64
        at = pl.ds(head * n, n)
        shift = shift_ref[at, :1]
        top = top_ref[:, head : head + 1]
        best = jnp.maximum(shift, top)
        disk_scale = jnp.exp2(shift - best)
        near_scale = jnp.exp2(top - best)
        total = (
            jnp.sum(den_ref[at, :], axis=1, keepdims=True) * disk_scale
            + sum_ref[:, head : head + 1] * near_scale
        )
        inv = 1.0 / total
        mixed = (acc_ref[at, :] * (disk_scale * inv)).astype(BF16)
        part = jnp.dot(mixed, wd_ref[:, d + lo : d + lo + 64], preferred_element_type=F32)
        part = part + near_ref[:, lo : lo + 64] * (near_scale * inv)
        att_ref[:, lo : lo + 64] = part.astype(BF16)
    out = jnp.dot(att_ref[...], wout_ref[...], preferred_element_type=F32)
    out_ref[...] = (x_ref[...].astype(F32) + out).astype(BF16)


def disk_attend(visible, lifted, pieces, own, top, total, near, wd, wout, x):
    n, d = x.shape
    tokens = sum(piece.shape[1] for piece in pieces)
    rows, width = lifted.shape
    vmem = pl.BlockSpec(memory_space=pltpu.VMEM)
    return pl.pallas_call(
        functools.partial(disk_kernel, pieces=len(pieces)),
        out_shape=shape((n, d), BF16),
        in_specs=[pl.BlockSpec(memory_space=pltpu.SMEM)] + [vmem] * (8 + len(pieces)),
        out_specs=vmem,
        scratch_shapes=[
            pltpu.VMEM((tokens, width), BF16),
            pltpu.VMEM((rows, 128), F32),
            pltpu.VMEM((rows, width), F32),
            pltpu.VMEM((rows, 128), F32),
            pltpu.VMEM((n, d), BF16),
        ],
        compiler_params=params(48),
        cost_estimate=pl.CostEstimate(flops=16 * 10**9, bytes_accessed=10**7, transcendentals=10**6),
        name="disk_attend",
    )(visible, lifted, *pieces, own, top, total, near, wd, wout, x)


def device_at(z, y, x, core):
    return (z * 2 + y // 2) * 16 + (y % 2) * 8 + x * 2 + core


def ring(*steps):
    pairs = []
    for z in range(4):
        for y in range(4):
            for x in range(4):
                for core in range(2):
                    axis, by = steps[core]
                    to = [z, y, x]
                    to[axis] = (to[axis] + by) % 4
                    pairs.append((device_at(z, y, x, core), device_at(*to, core)))
    return pairs


def other_core():
    return [(s, s ^ 1) for s in range(128)]


def spread(block, first, second):
    return [lax.ppermute(block, AXES, ring((first, by), (second, by))) for by in (1, 3, 2)]


def gather_tokens(disk_tokens):
    block = jnp.transpose(disk_tokens, (1, 0, 2))
    block = jnp.concatenate([block] + spread(block, 0, 1), axis=1)
    block = jnp.concatenate([block] + spread(block, 1, 2), axis=1)
    pieces = [block] + spread(block, 2, 0)
    return pieces + [lax.ppermute(piece, AXES, other_core()) for piece in pieces]


def local(
    mesh_nodes,
    norm_gain,
    w_query,
    w_node_kv,
    obs_rows,
    w_obs_kv,
    obs_owner,
    neighbours,
    neighbour_mask,
    disk_tokens,
    w_disk_kv,
    disk_start,
    disk_extent,
    w_out,
):
    devices = lax.axis_size("lat") * lax.axis_size("lon")
    width = obs_rows.shape[1]
    slots = devices * 8
    send = place(obs_owner, obs_rows, slots)
    got = lax.all_to_all(
        send.reshape(devices, 8, width), AXES, split_axis=0, concat_axis=0, tiled=True
    ).reshape(slots, width)
    query, lifted, own, value = node_prep(
        mesh_nodes, norm_gain.reshape(1, -1), w_query, w_node_kv, w_disk_kv
    )
    count = count_listed(neighbours, neighbour_mask, slots)
    pieces = gather_tokens(disk_tokens)
    visible = (
        jnp.mod(lax.axis_index("lon") - disk_start, lax.axis_size("lon")) < disk_extent
    ).astype(jnp.int32)
    top, total, near = near_attend(got, w_obs_kv, query, count, own, value)
    return disk_attend(
        visible, lifted, pieces, own, top, total, near, w_disk_kv, w_out, mesh_nodes
    )


def solution(mesh):
    split = P(AXES, None)
    return jax.shard_map(
        local,
        mesh=mesh,
        in_specs=(
            split,
            P(),
            P(),
            P(),
            split,
            P(),
            split,
            split,
            split,
            P(AXES, None, None),
            P(),
            P(),
            P(),
            P(),
        ),
        out_specs=split,
        check_vma=False,
    )
```

```python
import functools

import jax
import jax.numpy as jnp
from jax import lax
from jax.experimental import pallas as pl
from jax.experimental.pallas import tpu as pltpu
from jax.sharding import PartitionSpec as P

HEADS = 8
AXES = ("lat", "lon")
LOG2E = 1.4426950408889634
EMPTY = 65536.0
NEG = -1e30
BIG = 2.0**100
F32 = jnp.float32
BF16 = jnp.bfloat16
NT = (((1,), (1,)), ((), ()))


def shape(dims, dtype):
    return jax.ShapeDtypeStruct(dims, dtype)


def params(mib):
    return pltpu.CompilerParams(vmem_limit_bytes=mib * 2**20)


HBM = pl.BlockSpec(memory_space=pltpu.HBM)
VMEM = pl.BlockSpec(memory_space=pltpu.VMEM)
SMEM = pl.BlockSpec(memory_space=pltpu.SMEM)


def start_copy(source, target, sem):
    copy = pltpu.make_async_copy(source, target, sem)
    copy.start()
    return copy


def place_kernel(owner_ref, rows_ref, send_ref, held_ref, sems):
    count = rows_ref.shape[0]
    slots = send_ref.shape[0]
    owners = slots // 8
    owner = owner_ref[...]
    hot = jnp.where(lax.broadcasted_iota(jnp.int32, (owners, count), 0) == owner, 1.0, 0.0)
    row = lax.broadcasted_iota(jnp.int32, (count, count), 0)
    col = lax.broadcasted_iota(jnp.int32, (count, count), 1)
    earlier = jnp.where(row < col, 1.0, 0.0).astype(BF16)
    before = jnp.dot(hot.astype(BF16), earlier, preferred_element_type=F32)
    rank = jnp.sum(before * hot, axis=0, keepdims=True)
    slot = owner * 8 + rank.astype(jnp.int32)
    rows = rows_ref[...]
    ones_rows = jnp.ones((count, 128), BF16)
    step = slots // 4
    copies = []
    for i in range(4):
        at = pl.ds(i * step, step)
        ids_col = lax.broadcasted_iota(jnp.int32, (step, count), 0) + i * step
        placing = jnp.where(ids_col == slot, 1.0, 0.0).astype(BF16)
        placed = jnp.dot(placing, rows, preferred_element_type=F32)
        filled = jnp.dot(placing, ones_rows, preferred_element_type=F32)
        filled = jnp.concatenate([filled, filled], axis=1)
        held_ref[at, :] = jnp.where(filled > 0.5, placed, EMPTY).astype(BF16)
        copies.append(start_copy(held_ref.at[at, :], send_ref.at[at, :], sems.at[i]))
    for copy in copies:
        copy.wait()


def place(owner, rows, slots):
    return pl.pallas_call(
        place_kernel,
        out_shape=shape((slots, rows.shape[1]), BF16),
        in_specs=[VMEM, VMEM],
        out_specs=HBM,
        scratch_shapes=[pltpu.VMEM((slots, rows.shape[1]), BF16), pltpu.SemaphoreType.DMA((4,))],
        compiler_params=params(16),
        cost_estimate=pl.CostEstimate(flops=10**9, bytes_accessed=10**6, transcendentals=0),
        name="place",
    )(owner, rows)


def one_head(pair, odd):
    lane = lax.broadcasted_iota(jnp.int32, pair.shape, 1)
    keep = lane >= 64 if odd else lane < 64
    return jnp.where(keep, pair.astype(F32), 0.0).astype(pair.dtype)


def node_kernel(
    x_hbm, gain_ref, wq_hbm, wkv_hbm, wd_hbm, query_hbm, lifted_hbm, own_hbm, value_hbm,
    x_ref, wq_ref, wkv_ref, wd_ref, query_ref, lifted_ref, own_ref, value_ref, sems,
):
    n, d = x_ref.shape
    get_x = start_copy(x_hbm, x_ref, sems.at[0])
    get_wq = start_copy(wq_hbm, wq_ref, sems.at[1])
    get_wkv = start_copy(wkv_hbm, wkv_ref, sems.at[2])
    get_wd = start_copy(wd_hbm, wd_ref, sems.at[3])
    get_x.wait()
    x = x_ref[...].astype(F32)
    inverse = lax.rsqrt(jnp.mean(x * x, axis=1, keepdims=True) + 1e-06)
    normed = (x * inverse * gain_ref[...]).astype(BF16)
    get_wq.wait()
    query = (jnp.dot(normed, wq_ref[...], preferred_element_type=F32) * 0.125).astype(BF16)
    query_ref[...] = query
    puts = [start_copy(query_ref, query_hbm, sems.at[4])]
    get_wkv.wait()
    kv = jnp.dot(normed, wkv_ref[...], preferred_element_type=F32).astype(BF16)
    value_ref[...] = kv[:, d:]
    puts.append(start_copy(value_ref, value_hbm, sems.at[5]))
    prod = query.astype(F32) * kv[:, :d].astype(F32)
    lane = lax.broadcasted_iota(jnp.int32, (n, 128), 1)
    own = jnp.zeros((n, 128), F32)
    get_wd.wait()
    for head in range(HEADS):
        lo = head // 2 * 128
        part = jnp.sum(prod[:, head * 64 : head * 64 + 64], axis=1, keepdims=True) * LOG2E
        own = jnp.where(lane == head, part, own)
        lifted = lax.dot_general(
            one_head(query[:, lo : lo + 128], head % 2),
            wd_ref[:, lo : lo + 128],
            NT,
            preferred_element_type=F32,
        )
        at = pl.ds(head * n, n)
        lifted_ref[at, :] = (lifted * LOG2E).astype(BF16)
        puts.append(start_copy(lifted_ref.at[at, :], lifted_hbm.at[at, :], sems.at[7 + head]))
    own_ref[...] = own
    puts.append(start_copy(own_ref, own_hbm, sems.at[6]))
    for copy in puts:
        copy.wait()


def node_prep(x, gain, wq, wkv, wd):
    n, d = x.shape
    width = wd.shape[0]
    outs = [((n, d), BF16), ((HEADS * n, width), BF16), ((n, 128), F32), ((n, d), BF16)]
    ins = [(v.shape, v.dtype) for v in (x, wq, wkv, wd)]
    return pl.pallas_call(
        node_kernel,
        out_shape=tuple(shape(*o) for o in outs),
        in_specs=[HBM, VMEM, HBM, HBM, HBM],
        out_specs=(HBM,) * 4,
        scratch_shapes=[pltpu.VMEM(*v) for v in ins + outs]
        + [pltpu.SemaphoreType.DMA((7 + HEADS,))],
        compiler_params=params(24),
        cost_estimate=pl.CostEstimate(flops=3 * 10**9, bytes_accessed=5 * 10**6, transcendentals=0),
        name="node_prep",
    )(x, gain, wq, wkv, wd)


def count_kernel(near_ref, mark_ref, count_hbm, count_ref, sems):
    slots = count_ref.shape[1]
    step = 64
    parts = near_ref.shape[0] // step

    def piece(i):
        at = pl.ds(pl.multiple_of(i * step, step), step)
        return pltpu.make_async_copy(count_ref.at[at, :], count_hbm.at[at, :], sems.at[i])

    def body(i, carry):
        start = pl.multiple_of(i * step, step)
        near = jnp.where(mark_ref[pl.ds(start, step), :] > 0, near_ref[pl.ds(start, step), :], -1)
        near = near.astype(jnp.int16)
        ids = lax.broadcasted_iota(jnp.int16, (step, slots), 1)
        total = jnp.zeros((step, slots), jnp.int16)
        one = jnp.ones((step, slots), jnp.int16)
        for entry in range(near_ref.shape[1]):
            total = jnp.where(ids == near[:, entry : entry + 1], total + one, total)
        count_ref[pl.ds(start, step), :] = total.astype(F32).astype(BF16)
        piece(i).start()
        return carry

    lax.fori_loop(0, parts, body, 0)
    for i in range(parts):
        piece(i).wait()


def count_listed(near, mark, slots):
    n = near.shape[0]
    return pl.pallas_call(
        count_kernel,
        out_shape=shape((n, slots), BF16),
        in_specs=[VMEM, VMEM],
        out_specs=HBM,
        scratch_shapes=[pltpu.VMEM((n, slots), BF16), pltpu.SemaphoreType.DMA((n // 64,))],
        compiler_params=params(16),
        cost_estimate=pl.CostEstimate(flops=4 * 10**9, bytes_accessed=2 * 10**6, transcendentals=0),
        name="count_listed",
    )(near, mark)


def near_kernel(
    got_hbm, w_hbm, query_hbm, count_hbm, own_hbm, value_hbm, top_hbm, sum_hbm, acc_hbm,
    got_ref, w_ref, query_ref, count_ref, own_ref, value_ref, top_ref, sum_ref, acc_ref,
    key_ref, val_ref, bias_ref, sems,
):
    slots = got_ref.shape[0]
    n, d = query_ref.shape
    get_got = start_copy(got_hbm, got_ref, sems.at[0])
    get_w = start_copy(w_hbm, w_ref, sems.at[1])
    get_count = start_copy(count_hbm, count_ref, sems.at[2])
    gets = [
        start_copy(query_hbm, query_ref, sems.at[3]),
        start_copy(own_hbm, own_ref, sems.at[4]),
        start_copy(value_hbm, value_ref, sems.at[5]),
    ]
    get_got.wait()
    got = got_ref[...]
    absent = got.astype(F32) > 1024.0
    rows = jnp.where(absent, 0.0, got.astype(F32)).astype(BF16)
    ones = jnp.ones((8, 128), BF16)
    empty = lax.dot_general(
        ones, jnp.where(absent[:, :128], 1.0, 0.0).astype(BF16), NT, preferred_element_type=F32
    )[0:1, :]
    get_w.wait()
    kv = jnp.dot(rows, w_ref[...], preferred_element_type=F32).astype(BF16)
    key_ref[...] = kv[:, :d]
    for pair in range(HEADS // 2):
        lo = d + pair * 128
        val_ref[pair, :, :128] = kv[:, lo : lo + 128]
        val_ref[pair, :, 128:] = jnp.ones((slots, 128), BF16)
    get_count.wait()
    count = count_ref[...].astype(F32)
    bias_ref[...] = jnp.where((count > 0.0) & (empty < 0.5), jnp.log2(jnp.maximum(count, 1.0)), NEG)
    for copy in gets:
        copy.wait()

    def attend(step, exact):
        lane = lax.broadcasted_iota(jnp.int32, (step, 128), 1)

        def body(i, carry):
            at = pl.ds(pl.multiple_of(i * step, step), step)
            own = own_ref[at, :]
            tops = own
            sums = jnp.ones((step, 128), F32)
            for pair in range(HEADS // 2):
                lo = pair * 128
                sides = []
                for odd in range(2):
                    head = 2 * pair + odd
                    scores = lax.dot_general(
                        one_head(query_ref[at, lo : lo + 128], odd),
                        key_ref[:, lo : lo + 128],
                        NT,
                        preferred_element_type=F32,
                    )
                    scores = scores * LOG2E + bias_ref[at, :]
                    shift = own[:, head : head + 1]
                    if exact:
                        mine = shift
                        shift = jnp.maximum(jnp.max(scores, axis=1, keepdims=True), mine)
                        self_weight = jnp.exp2(mine - shift).astype(BF16).astype(F32)
                        tops = jnp.where(lane == head, shift, tops)
                    else:
                        self_weight = 1.0
                    weights = jnp.exp2(scores - shift).astype(BF16)
                    part = jnp.dot(weights, val_ref[pair], preferred_element_type=F32)
                    sums = jnp.where(lane == head, part[:, 128:] + self_weight, sums)
                    sides.append(part[:, :128] + self_weight * value_ref[at, lo : lo + 128].astype(F32))
                acc_ref[at, lo : lo + 128] = jnp.where(lane < 64, sides[0], sides[1])
            top_ref[at, :] = tops
            sum_ref[at, :] = sums
            return carry

        lax.fori_loop(0, n // step, body, 0)

    attend(256, False)
    worst = jnp.max(jnp.max(sum_ref[...], axis=0, keepdims=True))

    @pl.when(jnp.logical_not(worst < BIG))
    def _():
        attend(64, True)

    puts = [
        start_copy(top_ref, top_hbm, sems.at[6]),
        start_copy(sum_ref, sum_hbm, sems.at[7]),
        start_copy(acc_ref, acc_hbm, sems.at[8]),
    ]
    for copy in puts:
        copy.wait()


def near_attend(got, w, query, count, own, value):
    n, d = query.shape
    slots = got.shape[0]
    ins = [(v.shape, v.dtype) for v in (got, w, query, count, own, value)]
    outs = [((n, 128), F32), ((n, 128), F32), ((n, d), F32)]
    return pl.pallas_call(
        near_kernel,
        out_shape=tuple(shape(*o) for o in outs),
        in_specs=[HBM] * 6,
        out_specs=(HBM,) * 3,
        scratch_shapes=[pltpu.VMEM(*v) for v in ins + outs]
        + [
            pltpu.VMEM((slots, d), BF16),
            pltpu.VMEM((HEADS // 2, slots, 256), BF16),
            pltpu.VMEM((n, slots), F32),
            pltpu.SemaphoreType.DMA((9,)),
        ],
        compiler_params=params(40),
        cost_estimate=pl.CostEstimate(flops=5 * 10**9, bytes_accessed=5 * 10**6, transcendentals=10**6),
        name="near_attend",
    )(got, w, query, count, own, value)


def disk_kernel(*refs, pieces):
    (vis_ref, lifted_hbm), refs = refs[:2], refs[2:]
    piece_hbm, refs = refs[:pieces], refs[pieces:]
    late_hbm, refs = refs[:7], refs[7:]
    out_ref, own_ref, lifted_ref, tok_ref = refs[:4]
    top_ref, sum_ref, near_ref, wd_ref, wout_ref, x_ref = late_refs = refs[4:10]
    shift_ref, acc_ref, den_ref, att_ref, sems, tok_sems = refs[10:]
    own_hbm = late_hbm[0]
    n, d = x_ref.shape
    rows = lifted_ref.shape[0]
    disks, size = piece_hbm[0].shape[:2]

    get_own = start_copy(own_hbm, own_ref, sems.at[0])
    get_lifted = start_copy(lifted_hbm, lifted_ref, sems.at[1])

    def token_copies(disk):
        return [
            pltpu.make_async_copy(
                piece_hbm[i].at[disk],
                tok_ref.at[disk, pl.ds(i * size, size), :],
                tok_sems.at[disk, i],
            )
            for i in range(pieces)
        ]

    for disk in range(disks):

        @pl.when(vis_ref[disk] > 0)
        def _():
            for copy in token_copies(disk):
                copy.start()

    late = [
        start_copy(source, target, sems.at[2 + i])
        for i, (source, target) in enumerate(zip(late_hbm[1:], late_refs))
    ]

    def add_disks(step, unroll, first):
        den_ref[...] = jnp.zeros_like(den_ref)
        acc_ref[...] = jnp.zeros_like(acc_ref)
        if first:
            get_own.wait()
            for head in range(HEADS):
                shift_ref[pl.ds(head * n, n), :] = jnp.broadcast_to(own_ref[:, head : head + 1], (n, 128))
            get_lifted.wait()
            for disk in range(disks):

                @pl.when(vis_ref[disk] > 0)
                def _():
                    for copy in token_copies(disk):
                        copy.wait()

        def add_disk(disk, carry):
            @pl.when(vis_ref[disk] > 0)
            def _():
                def body(i, inner):
                    for u in range(unroll):
                        at = pl.ds(pl.multiple_of((i * unroll + u) * step, step), step)
                        scores = lax.dot_general(
                            lifted_ref[at, :], tok_ref[disk], NT, preferred_element_type=F32
                        )
                        weights = jnp.exp2(scores - shift_ref[at, :1])
                        part = weights[:, :128]
                        for j in range(1, weights.shape[1] // 128):
                            part = part + weights[:, j * 128 : j * 128 + 128]
                        den_ref[at, :] += part
                        acc_ref[at, :] += jnp.dot(
                            weights.astype(BF16), tok_ref[disk], preferred_element_type=F32
                        )
                    return inner

                lax.fori_loop(0, rows // (step * unroll), body, 0)

            return carry

        lax.fori_loop(0, disks, add_disk, 0)

    add_disks(256, 8, True)

    worst = jnp.max(jnp.max(den_ref[...], axis=0, keepdims=True))

    @pl.when(jnp.logical_not(worst < BIG))
    def _():
        def top_disk(disk, carry):
            @pl.when(vis_ref[disk] > 0)
            def _():
                def body(i, inner):
                    at = pl.ds(pl.multiple_of(i * 128, 128), 128)
                    scores = lax.dot_general(
                        lifted_ref[at, :], tok_ref[disk], NT, preferred_element_type=F32
                    )
                    best = jnp.max(scores, axis=1, keepdims=True)
                    shift_ref[at, :] = jnp.maximum(shift_ref[at, :], best)
                    return inner

                lax.fori_loop(0, rows // 128, body, 0)

            return carry

        lax.fori_loop(0, disks, top_disk, 0)
        add_disks(128, 1, False)

    for copy in late:
        copy.wait()
    lane = lax.broadcasted_iota(jnp.int32, (n, 128), 1)
    for pair in range(HEADS // 2):
        lo = pair * 128
        sides = []
        for odd in range(2):
            head = 2 * pair + odd
            at = pl.ds(head * n, n)
            shift = shift_ref[at, :1]
            top = top_ref[:, head : head + 1]
            best = jnp.maximum(shift, top)
            disk_scale = jnp.exp2(shift - best)
            near_scale = jnp.exp2(top - best)
            total = (
                jnp.sum(den_ref[at, :], axis=1, keepdims=True) * disk_scale
                + sum_ref[:, head : head + 1] * near_scale
            )
            inv = 1.0 / total
            mixed = (acc_ref[at, :] * (disk_scale * inv)).astype(BF16)
            part = jnp.dot(mixed, wd_ref[:, d + lo : d + lo + 128], preferred_element_type=F32)
            sides.append(part + near_ref[:, lo : lo + 128] * (near_scale * inv))
        att_ref[:, lo : lo + 128] = jnp.where(lane < 64, sides[0], sides[1]).astype(BF16)
    out = jnp.dot(att_ref[...], wout_ref[...], preferred_element_type=F32)
    out_ref[...] = (x_ref[...].astype(F32) + out).astype(BF16)


def disk_attend(visible, lifted, pieces, own, top, total, near, wd, wout, x):
    n, d = x.shape
    disks = pieces[0].shape[0]
    tokens = sum(piece.shape[1] for piece in pieces)
    rows, width = lifted.shape
    late = (top, total, near, wd, wout, x)
    return pl.pallas_call(
        functools.partial(disk_kernel, pieces=len(pieces)),
        out_shape=shape((n, d), BF16),
        in_specs=[SMEM] + [HBM] * (8 + len(pieces)),
        out_specs=VMEM,
        scratch_shapes=[
            pltpu.VMEM(own.shape, F32),
            pltpu.VMEM((rows, width), BF16),
            pltpu.VMEM((disks, tokens, width), BF16),
        ]
        + [pltpu.VMEM(v.shape, v.dtype) for v in late]
        + [
            pltpu.VMEM((rows, 128), F32),
            pltpu.VMEM((rows, width), F32),
            pltpu.VMEM((rows, 128), F32),
            pltpu.VMEM((n, d), BF16),
            pltpu.SemaphoreType.DMA((8,)),
            pltpu.SemaphoreType.DMA((disks, len(pieces))),
        ],
        compiler_params=params(48),
        cost_estimate=pl.CostEstimate(flops=16 * 10**9, bytes_accessed=10**7, transcendentals=10**6),
        name="disk_attend",
    )(visible, lifted, *pieces, own, *late)


def device_at(z, y, x, core):
    return (z * 2 + y // 2) * 16 + (y % 2) * 8 + x * 2 + core


def ring(*steps):
    pairs = []
    for z in range(4):
        for y in range(4):
            for x in range(4):
                for core in range(2):
                    axis, by = steps[core]
                    to = [z, y, x]
                    to[axis] = (to[axis] + by) % 4
                    pairs.append((device_at(z, y, x, core), device_at(*to, core)))
    return pairs


def other_core():
    return [(s, s ^ 1) for s in range(128)]


def spread(block, first, second):
    return [lax.ppermute(block, AXES, ring((first, by), (second, by))) for by in (1, 3, 2)]


def gather_tokens(disk_tokens):
    block = jnp.transpose(disk_tokens, (1, 0, 2))
    block = jnp.concatenate([block] + spread(block, 0, 1), axis=1)
    block = jnp.concatenate([block] + spread(block, 1, 2), axis=1)
    pieces = [block] + spread(block, 2, 0)
    return pieces + [lax.ppermute(piece, AXES, other_core()) for piece in pieces]


def local(
    mesh_nodes,
    norm_gain,
    w_query,
    w_node_kv,
    obs_rows,
    w_obs_kv,
    obs_owner,
    neighbours,
    neighbour_mask,
    disk_tokens,
    w_disk_kv,
    disk_start,
    disk_extent,
    w_out,
):
    devices = lax.axis_size("lat") * lax.axis_size("lon")
    width = obs_rows.shape[1]
    slots = devices * 8
    send = place(obs_owner.reshape(1, -1), obs_rows, slots)
    got = lax.all_to_all(
        send.reshape(devices, 8, width), AXES, split_axis=0, concat_axis=0, tiled=True
    ).reshape(slots, width)
    query, lifted, own, value = node_prep(
        mesh_nodes, norm_gain.reshape(1, -1), w_query, w_node_kv, w_disk_kv
    )
    count = count_listed(neighbours, neighbour_mask, slots)
    pieces = gather_tokens(disk_tokens)
    visible = (
        jnp.mod(lax.axis_index("lon") - disk_start, lax.axis_size("lon")) < disk_extent
    ).astype(jnp.int32)
    top, total, near = near_attend(got, w_obs_kv, query, count, own, value)
    return disk_attend(
        visible, lifted, pieces, own, top, total, near, w_disk_kv, w_out, mesh_nodes
    )


def solution(mesh):
    split = P(AXES, None)
    return jax.shard_map(
        local,
        mesh=mesh,
        in_specs=(
            split,
            P(),
            P(),
            P(),
            split,
            P(),
            split,
            split,
            split,
            P(AXES, None, None),
            P(),
            P(),
            P(),
            P(),
        ),
        out_specs=split,
        check_vma=False,
    )
```

```python
import functools

import jax
import jax.numpy as jnp
from jax import lax
from jax.experimental import pallas as pl
from jax.experimental.pallas import tpu as pltpu
from jax.sharding import PartitionSpec as P

HEADS = 8
AXES = ("lat", "lon")
LOG2E = 1.4426950408889634
EMPTY = 65536.0
NEG = -1e30
BIG = 2.0**100
F32 = jnp.float32
BF16 = jnp.bfloat16
NT = (((1,), (1,)), ((), ()))


def shape(dims, dtype):
    return jax.ShapeDtypeStruct(dims, dtype)


def params():
    return pltpu.CompilerParams(vmem_limit_bytes=67043328)


HBM = pl.BlockSpec(memory_space=pltpu.HBM)
VMEM = pl.BlockSpec(memory_space=pltpu.VMEM)
SMEM = pl.BlockSpec(memory_space=pltpu.SMEM)


def start_copy(source, target, sem):
    copy = pltpu.make_async_copy(source, target, sem)
    copy.start()
    return copy


def place_kernel(owner_ref, rows_ref, send_ref, held_ref, sems):
    count = rows_ref.shape[0]
    slots = send_ref.shape[0]
    owners = slots // 8
    owner = owner_ref[...]
    hot = jnp.where(lax.broadcasted_iota(jnp.int32, (owners, count), 0) == owner, 1.0, 0.0)
    row = lax.broadcasted_iota(jnp.int32, (count, count), 0)
    col = lax.broadcasted_iota(jnp.int32, (count, count), 1)
    earlier = jnp.where(row < col, 1.0, 0.0).astype(BF16)
    before = jnp.dot(hot.astype(BF16), earlier, preferred_element_type=F32)
    rank = jnp.sum(before * hot, axis=0, keepdims=True)
    slot = owner * 8 + rank.astype(jnp.int32)
    rows = rows_ref[...]
    ones_rows = jnp.ones((count, 128), BF16)
    step = slots // 4
    copies = []
    for i in range(4):
        at = pl.ds(i * step, step)
        ids_col = lax.broadcasted_iota(jnp.int32, (step, count), 0) + i * step
        placing = jnp.where(ids_col == slot, 1.0, 0.0).astype(BF16)
        placed = jnp.dot(placing, rows, preferred_element_type=F32)
        filled = jnp.dot(placing, ones_rows, preferred_element_type=F32)
        filled = jnp.concatenate([filled, filled], axis=1)
        held_ref[at, :] = jnp.where(filled > 0.5, placed, EMPTY).astype(BF16)
        copies.append(start_copy(held_ref.at[at, :], send_ref.at[at, :], sems.at[i]))
    for copy in copies:
        copy.wait()


def place(owner, rows, slots):
    return pl.pallas_call(
        place_kernel,
        out_shape=shape((slots, rows.shape[1]), BF16),
        in_specs=[VMEM, VMEM],
        out_specs=HBM,
        scratch_shapes=[pltpu.VMEM((slots, rows.shape[1]), BF16), pltpu.SemaphoreType.DMA((4,))],
        compiler_params=params(),
        cost_estimate=pl.CostEstimate(flops=10**9, bytes_accessed=10**6, transcendentals=0),
        name="place",
    )(owner, rows)


def one_head(pair, odd):
    lane = lax.broadcasted_iota(jnp.int32, pair.shape, 1)
    keep = lane >= 64 if odd else lane < 64
    return jnp.where(keep, pair.astype(F32), 0.0).astype(pair.dtype)


def node_kernel(
    x_hbm, gain_ref, wq_hbm, wkv_hbm, wd_hbm, query_hbm, lifted_hbm, own_hbm, value_hbm,
    x_ref, wq_ref, wkv_ref, wd_ref, query_ref, lifted_ref, own_ref, value_ref, sems,
):
    n, d = x_ref.shape
    get_x = start_copy(x_hbm, x_ref, sems.at[0])
    get_wq = start_copy(wq_hbm, wq_ref, sems.at[1])
    get_wkv = start_copy(wkv_hbm, wkv_ref, sems.at[2])
    get_wd = start_copy(wd_hbm, wd_ref, sems.at[3])
    get_x.wait()
    x = x_ref[...].astype(F32)
    inverse = lax.rsqrt(jnp.mean(x * x, axis=1, keepdims=True) + 1e-06)
    normed = (x * inverse * gain_ref[...]).astype(BF16)
    get_wq.wait()
    query = (jnp.dot(normed, wq_ref[...], preferred_element_type=F32) * 0.125).astype(BF16)
    query_ref[...] = query
    puts = [start_copy(query_ref, query_hbm, sems.at[4])]
    get_wkv.wait()
    kv = jnp.dot(normed, wkv_ref[...], preferred_element_type=F32).astype(BF16)
    value_ref[...] = kv[:, d:]
    puts.append(start_copy(value_ref, value_hbm, sems.at[5]))
    prod = query.astype(F32) * kv[:, :d].astype(F32)
    lane = lax.broadcasted_iota(jnp.int32, (n, 128), 1)
    own = jnp.zeros((n, 128), F32)
    get_wd.wait()
    for head in range(HEADS):
        lo = head // 2 * 128
        part = jnp.sum(prod[:, head * 64 : head * 64 + 64], axis=1, keepdims=True) * LOG2E
        own = jnp.where(lane == head, part, own)
        lifted = lax.dot_general(
            one_head(query[:, lo : lo + 128], head % 2),
            wd_ref[:, lo : lo + 128],
            NT,
            preferred_element_type=F32,
        )
        at = pl.ds(head * n, n)
        lifted_ref[at, :] = (lifted * LOG2E).astype(BF16)
        puts.append(start_copy(lifted_ref.at[at, :], lifted_hbm.at[at, :], sems.at[7 + head]))
    own_ref[...] = own
    puts.append(start_copy(own_ref, own_hbm, sems.at[6]))
    for copy in puts:
        copy.wait()


def node_prep(x, gain, wq, wkv, wd):
    n, d = x.shape
    width = wd.shape[0]
    outs = [((n, d), BF16), ((HEADS * n, width), BF16), ((n, 128), F32), ((n, d), BF16)]
    ins = [(v.shape, v.dtype) for v in (x, wq, wkv, wd)]
    return pl.pallas_call(
        node_kernel,
        out_shape=tuple(shape(*o) for o in outs),
        in_specs=[HBM, VMEM, HBM, HBM, HBM],
        out_specs=(HBM,) * 4,
        scratch_shapes=[pltpu.VMEM(*v) for v in ins + outs]
        + [pltpu.SemaphoreType.DMA((7 + HEADS,))],
        compiler_params=params(),
        cost_estimate=pl.CostEstimate(flops=3 * 10**9, bytes_accessed=5 * 10**6, transcendentals=0),
        name="node_prep",
    )(x, gain, wq, wkv, wd)


def count_kernel(near_ref, mark_ref, count_hbm, count_ref, sems):
    slots = count_ref.shape[1]
    step = 64
    parts = near_ref.shape[0] // step

    def piece(i):
        at = pl.ds(pl.multiple_of(i * step, step), step)
        return pltpu.make_async_copy(count_ref.at[at, :], count_hbm.at[at, :], sems.at[i])

    def body(i, carry):
        start = pl.multiple_of(i * step, step)
        near = jnp.where(mark_ref[pl.ds(start, step), :] > 0, near_ref[pl.ds(start, step), :], -1)
        near = near.astype(jnp.int16)
        ids = lax.broadcasted_iota(jnp.int16, (step, slots), 1)
        total = jnp.zeros((step, slots), jnp.int16)
        one = jnp.ones((step, slots), jnp.int16)
        for entry in range(near_ref.shape[1]):
            total = jnp.where(ids == near[:, entry : entry + 1], total + one, total)
        count_ref[pl.ds(start, step), :] = total.astype(F32).astype(BF16)
        piece(i).start()
        return carry

    lax.fori_loop(0, parts, body, 0)
    for i in range(parts):
        piece(i).wait()


def count_listed(near, mark, slots):
    n = near.shape[0]
    return pl.pallas_call(
        count_kernel,
        out_shape=shape((n, slots), BF16),
        in_specs=[VMEM, VMEM],
        out_specs=HBM,
        scratch_shapes=[pltpu.VMEM((n, slots), BF16), pltpu.SemaphoreType.DMA((n // 64,))],
        compiler_params=params(),
        cost_estimate=pl.CostEstimate(flops=4 * 10**9, bytes_accessed=2 * 10**6, transcendentals=0),
        name="count_listed",
    )(near, mark)


def near_kernel(
    got_hbm, w_hbm, query_hbm, count_hbm, own_hbm, value_hbm, top_hbm, sum_hbm, acc_hbm,
    got_ref, w_ref, query_ref, count_ref, own_ref, value_ref, top_ref, sum_ref, acc_ref,
    key_ref, val_ref, bias_ref, sems,
):
    slots = got_ref.shape[0]
    n, d = query_ref.shape
    get_got = start_copy(got_hbm, got_ref, sems.at[0])
    get_w = start_copy(w_hbm, w_ref, sems.at[1])
    get_count = start_copy(count_hbm, count_ref, sems.at[2])
    gets = [
        start_copy(query_hbm, query_ref, sems.at[3]),
        start_copy(own_hbm, own_ref, sems.at[4]),
        start_copy(value_hbm, value_ref, sems.at[5]),
    ]
    get_got.wait()
    got = got_ref[...]
    absent = got.astype(F32) > 1024.0
    rows = jnp.where(absent, 0.0, got.astype(F32)).astype(BF16)
    ones = jnp.ones((8, 128), BF16)
    empty = lax.dot_general(
        ones, jnp.where(absent[:, :128], 1.0, 0.0).astype(BF16), NT, preferred_element_type=F32
    )[0:1, :]
    get_w.wait()
    kv = jnp.dot(rows, w_ref[...], preferred_element_type=F32).astype(BF16)
    key_ref[...] = kv[:, :d]
    for pair in range(HEADS // 2):
        lo = d + pair * 128
        val_ref[pair, :, :128] = kv[:, lo : lo + 128]
        val_ref[pair, :, 128:] = jnp.ones((slots, 128), BF16)
    get_count.wait()
    count = count_ref[...].astype(F32)
    bias_ref[...] = jnp.where((count > 0.0) & (empty < 0.5), jnp.log2(jnp.maximum(count, 1.0)), NEG)
    for copy in gets:
        copy.wait()

    def attend(step, exact):
        lane = lax.broadcasted_iota(jnp.int32, (step, 128), 1)

        def body(i, carry):
            at = pl.ds(pl.multiple_of(i * step, step), step)
            own = own_ref[at, :]
            tops = own
            sums = jnp.ones((step, 128), F32)
            for pair in range(HEADS // 2):
                lo = pair * 128
                sides = []
                for odd in range(2):
                    head = 2 * pair + odd
                    scores = lax.dot_general(
                        one_head(query_ref[at, lo : lo + 128], odd),
                        key_ref[:, lo : lo + 128],
                        NT,
                        preferred_element_type=F32,
                    )
                    scores = scores * LOG2E + bias_ref[at, :]
                    shift = own[:, head : head + 1]
                    if exact:
                        mine = shift
                        shift = jnp.maximum(jnp.max(scores, axis=1, keepdims=True), mine)
                        self_weight = jnp.exp2(mine - shift).astype(BF16).astype(F32)
                        tops = jnp.where(lane == head, shift, tops)
                    else:
                        self_weight = 1.0
                    weights = jnp.exp2(scores - shift).astype(BF16)
                    part = jnp.dot(weights, val_ref[pair], preferred_element_type=F32)
                    sums = jnp.where(lane == head, part[:, 128:] + self_weight, sums)
                    sides.append(part[:, :128] + self_weight * value_ref[at, lo : lo + 128].astype(F32))
                acc_ref[at, lo : lo + 128] = jnp.where(lane < 64, sides[0], sides[1])
            top_ref[at, :] = tops
            sum_ref[at, :] = sums
            return carry

        lax.fori_loop(0, n // step, body, 0)

    attend(256, False)
    worst = jnp.max(jnp.max(sum_ref[...], axis=0, keepdims=True))

    @pl.when(jnp.logical_not(worst < BIG))
    def _():
        attend(64, True)

    puts = [
        start_copy(top_ref, top_hbm, sems.at[6]),
        start_copy(sum_ref, sum_hbm, sems.at[7]),
        start_copy(acc_ref, acc_hbm, sems.at[8]),
    ]
    for copy in puts:
        copy.wait()


def near_attend(got, w, query, count, own, value):
    n, d = query.shape
    slots = got.shape[0]
    ins = [(v.shape, v.dtype) for v in (got, w, query, count, own, value)]
    outs = [((n, 128), F32), ((n, 128), F32), ((n, d), F32)]
    return pl.pallas_call(
        near_kernel,
        out_shape=tuple(shape(*o) for o in outs),
        in_specs=[HBM] * 6,
        out_specs=(HBM,) * 3,
        scratch_shapes=[pltpu.VMEM(*v) for v in ins + outs]
        + [
            pltpu.VMEM((slots, d), BF16),
            pltpu.VMEM((HEADS // 2, slots, 256), BF16),
            pltpu.VMEM((n, slots), F32),
            pltpu.SemaphoreType.DMA((9,)),
        ],
        compiler_params=params(),
        cost_estimate=pl.CostEstimate(flops=5 * 10**9, bytes_accessed=5 * 10**6, transcendentals=10**6),
        name="near_attend",
    )(got, w, query, count, own, value)


def disk_kernel(*refs, pieces):
    (vis_ref, lifted_hbm), refs = refs[:2], refs[2:]
    piece_hbm, refs = refs[:pieces], refs[pieces:]
    late_hbm, refs = refs[:7], refs[7:]
    out_ref, own_ref, lifted_ref, tok_ref = refs[:4]
    top_ref, sum_ref, near_ref, wd_ref, wout_ref, x_ref = late_refs = refs[4:10]
    shift_ref, acc_ref, den_ref, att_ref, sems, tok_sems = refs[10:]
    own_hbm = late_hbm[0]
    n, d = x_ref.shape
    rows = lifted_ref.shape[0]
    disks, size = piece_hbm[0].shape[:2]

    get_own = start_copy(own_hbm, own_ref, sems.at[0])
    get_lifted = start_copy(lifted_hbm, lifted_ref, sems.at[1])

    def token_copies(disk):
        return [
            pltpu.make_async_copy(
                piece_hbm[i].at[disk],
                tok_ref.at[disk, pl.ds(i * size, size), :],
                tok_sems.at[disk, i],
            )
            for i in range(pieces)
        ]

    for disk in range(disks):

        @pl.when(vis_ref[disk] > 0)
        def _():
            for copy in token_copies(disk):
                copy.start()

    late = [
        start_copy(source, target, sems.at[2 + i])
        for i, (source, target) in enumerate(zip(late_hbm[1:], late_refs))
    ]

    def add_disks(step, unroll, first):
        den_ref[...] = jnp.zeros_like(den_ref)
        acc_ref[...] = jnp.zeros_like(acc_ref)
        if first:
            get_own.wait()
            for head in range(HEADS):
                shift_ref[pl.ds(head * n, n), :] = jnp.broadcast_to(own_ref[:, head : head + 1], (n, 128))
            get_lifted.wait()
            for disk in range(disks):

                @pl.when(vis_ref[disk] > 0)
                def _():
                    for copy in token_copies(disk):
                        copy.wait()

        def add_disk(disk, carry):
            @pl.when(vis_ref[disk] > 0)
            def _():
                def body(i, inner):
                    for u in range(unroll):
                        at = pl.ds(pl.multiple_of((i * unroll + u) * step, step), step)
                        scores = lax.dot_general(
                            lifted_ref[at, :], tok_ref[disk], NT, preferred_element_type=F32
                        )
                        weights = jnp.exp2(scores - shift_ref[at, :1])
                        part = weights[:, :128]
                        for j in range(1, weights.shape[1] // 128):
                            part = part + weights[:, j * 128 : j * 128 + 128]
                        den_ref[at, :] += part
                        acc_ref[at, :] += jnp.dot(
                            weights.astype(BF16), tok_ref[disk], preferred_element_type=F32
                        )
                    return inner

                lax.fori_loop(0, rows // (step * unroll), body, 0)

            return carry

        lax.fori_loop(0, disks, add_disk, 0)

    add_disks(256, 8, True)

    worst = jnp.max(jnp.max(den_ref[...], axis=0, keepdims=True))

    @pl.when(jnp.logical_not(worst < BIG))
    def _():
        def top_disk(disk, carry):
            @pl.when(vis_ref[disk] > 0)
            def _():
                def body(i, inner):
                    at = pl.ds(pl.multiple_of(i * 128, 128), 128)
                    scores = lax.dot_general(
                        lifted_ref[at, :], tok_ref[disk], NT, preferred_element_type=F32
                    )
                    best = jnp.max(scores, axis=1, keepdims=True)
                    shift_ref[at, :] = jnp.maximum(shift_ref[at, :], best)
                    return inner

                lax.fori_loop(0, rows // 128, body, 0)

            return carry

        lax.fori_loop(0, disks, top_disk, 0)
        add_disks(128, 1, False)

    for copy in late:
        copy.wait()
    lane = lax.broadcasted_iota(jnp.int32, (n, 128), 1)
    for pair in range(HEADS // 2):
        lo = pair * 128
        sides = []
        for odd in range(2):
            head = 2 * pair + odd
            at = pl.ds(head * n, n)
            shift = shift_ref[at, :1]
            top = top_ref[:, head : head + 1]
            best = jnp.maximum(shift, top)
            disk_scale = jnp.exp2(shift - best)
            near_scale = jnp.exp2(top - best)
            total = (
                jnp.sum(den_ref[at, :], axis=1, keepdims=True) * disk_scale
                + sum_ref[:, head : head + 1] * near_scale
            )
            inv = 1.0 / total
            mixed = (acc_ref[at, :] * (disk_scale * inv)).astype(BF16)
            part = jnp.dot(mixed, wd_ref[:, d + lo : d + lo + 128], preferred_element_type=F32)
            sides.append(part + near_ref[:, lo : lo + 128] * (near_scale * inv))
        att_ref[:, lo : lo + 128] = jnp.where(lane < 64, sides[0], sides[1]).astype(BF16)
    out = jnp.dot(att_ref[...], wout_ref[...], preferred_element_type=F32)
    out_ref[...] = (x_ref[...].astype(F32) + out).astype(BF16)


def disk_attend(visible, lifted, pieces, own, top, total, near, wd, wout, x):
    n, d = x.shape
    disks = pieces[0].shape[0]
    tokens = sum(piece.shape[1] for piece in pieces)
    rows, width = lifted.shape
    late = (top, total, near, wd, wout, x)
    return pl.pallas_call(
        functools.partial(disk_kernel, pieces=len(pieces)),
        out_shape=shape((n, d), BF16),
        in_specs=[SMEM] + [HBM] * (8 + len(pieces)),
        out_specs=VMEM,
        scratch_shapes=[
            pltpu.VMEM(own.shape, F32),
            pltpu.VMEM((rows, width), BF16),
            pltpu.VMEM((disks, tokens, width), BF16),
        ]
        + [pltpu.VMEM(v.shape, v.dtype) for v in late]
        + [
            pltpu.VMEM((rows, 128), F32),
            pltpu.VMEM((rows, width), F32),
            pltpu.VMEM((rows, 128), F32),
            pltpu.VMEM((n, d), BF16),
            pltpu.SemaphoreType.DMA((8,)),
            pltpu.SemaphoreType.DMA((disks, len(pieces))),
        ],
        compiler_params=params(),
        cost_estimate=pl.CostEstimate(flops=16 * 10**9, bytes_accessed=10**7, transcendentals=10**6),
        name="disk_attend",
    )(visible, lifted, *pieces, own, *late)


def device_at(z, y, x, core):
    return (z * 2 + y // 2) * 16 + (y % 2) * 8 + x * 2 + core


def ring(*steps):
    pairs = []
    for z in range(4):
        for y in range(4):
            for x in range(4):
                for core in range(2):
                    axis, by = steps[core]
                    to = [z, y, x]
                    to[axis] = (to[axis] + by) % 4
                    pairs.append((device_at(z, y, x, core), device_at(*to, core)))
    return pairs


def other_core():
    return [(s, s ^ 1) for s in range(128)]


def spread(block, first, second):
    return [lax.ppermute(block, AXES, ring((first, by), (second, by))) for by in (1, 3, 2)]


def gather_tokens(disk_tokens):
    block = jnp.transpose(disk_tokens, (1, 0, 2))
    block = jnp.concatenate([block] + spread(block, 0, 1), axis=1)
    block = jnp.concatenate([block] + spread(block, 1, 2), axis=1)
    pieces = [block] + spread(block, 2, 0)
    return pieces + [lax.ppermute(piece, AXES, other_core()) for piece in pieces]


def local(
    mesh_nodes,
    norm_gain,
    w_query,
    w_node_kv,
    obs_rows,
    w_obs_kv,
    obs_owner,
    neighbours,
    neighbour_mask,
    disk_tokens,
    w_disk_kv,
    disk_start,
    disk_extent,
    w_out,
):
    devices = lax.axis_size("lat") * lax.axis_size("lon")
    width = obs_rows.shape[1]
    slots = devices * 8
    send = place(obs_owner.reshape(1, -1), obs_rows, slots)
    got = lax.all_to_all(
        send.reshape(devices, 8, width), AXES, split_axis=0, concat_axis=0, tiled=True
    ).reshape(slots, width)
    query, lifted, own, value = node_prep(
        mesh_nodes, norm_gain.reshape(1, -1), w_query, w_node_kv, w_disk_kv
    )
    count = count_listed(neighbours, neighbour_mask, slots)
    pieces = gather_tokens(disk_tokens)
    visible = (
        jnp.mod(lax.axis_index("lon") - disk_start, lax.axis_size("lon")) < disk_extent
    ).astype(jnp.int32)
    top, total, near = near_attend(got, w_obs_kv, query, count, own, value)
    return disk_attend(
        visible, lifted, pieces, own, top, total, near, w_disk_kv, w_out, mesh_nodes
    )


def solution(mesh):
    split = P(AXES, None)
    return jax.shard_map(
        local,
        mesh=mesh,
        in_specs=(
            split,
            P(),
            P(),
            P(),
            split,
            P(),
            split,
            split,
            split,
            P(AXES, None, None),
            P(),
            P(),
            P(),
            P(),
        ),
        out_specs=split,
        check_vma=False,
    )
```

```python
import functools

import jax
import jax.numpy as jnp
from jax import lax
from jax.experimental import pallas as pl
from jax.experimental.pallas import tpu as pltpu
from jax.sharding import PartitionSpec as P

HEADS = 8
AXES = ("lat", "lon")
LOG2E = 1.4426950408889634
EMPTY = 65536.0
NEG = -1e30
BIG = 2.0**100
F32 = jnp.float32
BF16 = jnp.bfloat16
NT = (((1,), (1,)), ((), ()))


def shape(dims, dtype):
    return jax.ShapeDtypeStruct(dims, dtype)


def params(grant=60 * 1024 * 1024):
    return pltpu.CompilerParams(vmem_limit_bytes=grant)


HBM = pl.BlockSpec(memory_space=pltpu.HBM)
VMEM = pl.BlockSpec(memory_space=pltpu.VMEM)
SMEM = pl.BlockSpec(memory_space=pltpu.SMEM)


def start_copy(source, target, sem):
    copy = pltpu.make_async_copy(source, target, sem)
    copy.start()
    return copy


def place_kernel(owner_ref, rows_ref, send_ref, held_ref, sems):
    count = rows_ref.shape[0]
    slots = send_ref.shape[0]
    owners = slots // 8
    owner = owner_ref[...]
    hot = jnp.where(lax.broadcasted_iota(jnp.int32, (owners, count), 0) == owner, 1.0, 0.0)
    row = lax.broadcasted_iota(jnp.int32, (count, count), 0)
    col = lax.broadcasted_iota(jnp.int32, (count, count), 1)
    earlier = jnp.where(row < col, 1.0, 0.0).astype(BF16)
    before = jnp.dot(hot.astype(BF16), earlier, preferred_element_type=F32)
    rank = jnp.sum(before * hot, axis=0, keepdims=True)
    slot = owner * 8 + rank.astype(jnp.int32)
    rows = rows_ref[...]
    ones_rows = jnp.ones((count, 128), BF16)
    step = slots // 4
    copies = []
    for i in range(4):
        at = pl.ds(i * step, step)
        ids_col = lax.broadcasted_iota(jnp.int32, (step, count), 0) + i * step
        placing = jnp.where(ids_col == slot, 1.0, 0.0).astype(BF16)
        placed = jnp.dot(placing, rows, preferred_element_type=F32)
        filled = jnp.dot(placing, ones_rows, preferred_element_type=F32)
        filled = jnp.concatenate([filled, filled], axis=1)
        held_ref[at, :] = jnp.where(filled > 0.5, placed, EMPTY).astype(BF16)
        copies.append(start_copy(held_ref.at[at, :], send_ref.at[at, :], sems.at[i]))
    for copy in copies:
        copy.wait()


def place(owner, rows, slots):
    return pl.pallas_call(
        place_kernel,
        out_shape=shape((slots, rows.shape[1]), BF16),
        in_specs=[VMEM, VMEM],
        out_specs=HBM,
        scratch_shapes=[pltpu.VMEM((slots, rows.shape[1]), BF16), pltpu.SemaphoreType.DMA((4,))],
        compiler_params=params(67043328),
        cost_estimate=pl.CostEstimate(flops=10**9, bytes_accessed=10**6, transcendentals=0),
        name="place",
    )(owner, rows)


def one_head(pair, odd):
    lane = lax.broadcasted_iota(jnp.int32, pair.shape, 1)
    keep = lane >= 64 if odd else lane < 64
    return jnp.where(keep, pair.astype(F32), 0.0).astype(pair.dtype)


def prep_kernel(
    near_ref, mark_ref, x_hbm, gain_ref, wq_hbm, wkv_hbm, wd_hbm, all_hbm, own_hbm,
    x_ref, wq_ref, wkv_ref, wd_ref, all_ref, own_ref, list_ref, sems, out_sems,
):
    n, d = x_ref.shape
    slots = 1024
    get_x = start_copy(x_hbm, x_ref, sems.at[0])
    get_wq = start_copy(wq_hbm, wq_ref, sems.at[1])
    get_wkv = start_copy(wkv_hbm, wkv_ref, sems.at[2])
    get_wd = start_copy(wd_hbm, wd_ref, sems.at[3])
    list_ref[...] = jnp.transpose(jnp.where(mark_ref[...] > 0, near_ref[...], -1), (1, 0))
    step = 64

    def body(i, carry):
        start = pl.multiple_of(i * step, step)
        near = list_ref[pl.ds(start, step), :].astype(jnp.int16)
        ids = lax.broadcasted_iota(jnp.int16, (step, slots), 1)
        total = jnp.zeros((step, slots), jnp.int16)
        one = jnp.ones((step, slots), jnp.int16)
        for entry in range(near.shape[1]):
            total = jnp.where(ids == near[:, entry : entry + 1], total + one, total)
        count = total.astype(F32).astype(BF16)
        for j in range(4):
            at = pl.ds(pl.multiple_of((12 + j) * n + start, step), step)
            all_ref[at, :] = count[:, j * 256 : j * 256 + 256]
        return carry

    lax.fori_loop(0, n // step, body, 0)

    def put(block, blocks, sem):
        at = pl.ds(block * n, blocks * n)
        return start_copy(all_ref.at[at, :], all_hbm.at[at, :], out_sems.at[sem])

    puts = [put(12, 4, 0)]
    get_x.wait()
    x = x_ref[...].astype(F32)
    inverse = lax.rsqrt(jnp.mean(x * x, axis=1, keepdims=True) + 1e-06)
    normed = (x * inverse * gain_ref[...]).astype(BF16)
    get_wq.wait()
    query = (jnp.dot(normed, wq_ref[...], preferred_element_type=F32) * 0.125).astype(BF16)
    get_wkv.wait()
    kv = jnp.dot(normed, wkv_ref[...], preferred_element_type=F32).astype(BF16)
    for j in range(2):
        all_ref[pl.ds((8 + j) * n, n), :] = query[:, j * 256 : j * 256 + 256]
        all_ref[pl.ds((10 + j) * n, n), :] = kv[:, d + j * 256 : d + j * 256 + 256]
    puts.append(put(8, 4, 1))
    prod = query.astype(F32) * kv[:, :d].astype(F32)
    lane = lax.broadcasted_iota(jnp.int32, (n, 128), 1)
    own = jnp.zeros((n, 128), F32)
    get_wd.wait()
    for head in range(HEADS):
        lo = head // 2 * 128
        part = jnp.sum(prod[:, head * 64 : head * 64 + 64], axis=1, keepdims=True) * LOG2E
        own = jnp.where(lane == head, part, own)
        lifted = lax.dot_general(
            one_head(query[:, lo : lo + 128], head % 2),
            wd_ref[:, lo : lo + 128],
            NT,
            preferred_element_type=F32,
        )
        all_ref[pl.ds(head * n, n), :] = (lifted * LOG2E).astype(BF16)
        puts.append(put(head, 1, 2 + head))
    own_ref[...] = own
    puts.append(start_copy(own_ref, own_hbm, out_sems.at[2 + HEADS]))
    for copy in puts:
        copy.wait()


def prep(near, mark, x, gain, wq, wkv, wd):
    n, d = x.shape
    outs = [((16 * n, 256), BF16), ((n, 128), F32)]
    ins = [(v.shape, v.dtype) for v in (x, wq, wkv, wd)]
    return pl.pallas_call(
        prep_kernel,
        out_shape=tuple(shape(*o) for o in outs),
        in_specs=[VMEM, VMEM, HBM, VMEM, HBM, HBM, HBM],
        out_specs=(HBM,) * 2,
        scratch_shapes=[pltpu.VMEM(*v) for v in ins + outs]
        + [
            pltpu.VMEM(near.shape[::-1], jnp.int32),
            pltpu.SemaphoreType.DMA((4,)),
            pltpu.SemaphoreType.DMA((3 + HEADS,)),
        ],
        compiler_params=params(),
        cost_estimate=pl.CostEstimate(flops=8 * 10**9, bytes_accessed=8 * 10**6, transcendentals=0),
        name="prep",
    )(near, mark, x, gain, wq, wkv, wd)


def near_kernel(
    got_hbm, w_hbm, all_hbm, own_hbm, top_hbm, sum_hbm, acc_hbm,
    got_ref, w_ref, query_ref, count_ref, own_ref, value_ref, top_ref, sum_ref, acc_ref,
    key_ref, val_ref, bias_ref, sems,
):
    slots = got_ref.shape[0]
    n, d = query_ref.shape
    get_got = start_copy(got_hbm, got_ref, sems.at[0])
    get_w = start_copy(w_hbm, w_ref, sems.at[1])

    def get_block(block, target, j, sem):
        return start_copy(
            all_hbm.at[pl.ds(block * n, n), :], target.at[:, pl.ds(j * 256, 256)], sems.at[sem]
        )

    get_count = [get_block(12 + j, count_ref, j, 8 + j) for j in range(4)]
    gets = [get_block(8 + j, query_ref, j, 2 + j) for j in range(2)]
    gets += [get_block(10 + j, value_ref, j, 4 + j) for j in range(2)]
    gets.append(start_copy(own_hbm, own_ref, sems.at[6]))
    get_got.wait()
    got = got_ref[...]
    absent = got.astype(F32) > 1024.0
    rows = jnp.where(absent, 0.0, got.astype(F32)).astype(BF16)
    ones = jnp.ones((8, 128), BF16)
    empty = lax.dot_general(
        ones, jnp.where(absent[:, :128], 1.0, 0.0).astype(BF16), NT, preferred_element_type=F32
    )[0:1, :]
    get_w.wait()
    kv = jnp.dot(rows, w_ref[...], preferred_element_type=F32).astype(BF16)
    key_ref[...] = kv[:, :d]
    for pair in range(HEADS // 2):
        lo = d + pair * 128
        val_ref[pair, :, :128] = kv[:, lo : lo + 128]
        val_ref[pair, :, 128:] = jnp.ones((slots, 128), BF16)
    for copy in get_count:
        copy.wait()
    count = count_ref[...].astype(F32)
    bias_ref[...] = jnp.where((count > 0.0) & (empty < 0.5), jnp.log2(jnp.maximum(count, 1.0)), NEG)
    for copy in gets:
        copy.wait()

    def attend(step, exact):
        lane = lax.broadcasted_iota(jnp.int32, (step, 128), 1)

        def body(i, carry):
            at = pl.ds(pl.multiple_of(i * step, step), step)
            own = own_ref[at, :]
            tops = own
            sums = jnp.ones((step, 128), F32)
            for pair in range(HEADS // 2):
                lo = pair * 128
                sides = []
                for odd in range(2):
                    head = 2 * pair + odd
                    scores = lax.dot_general(
                        one_head(query_ref[at, lo : lo + 128], odd),
                        key_ref[:, lo : lo + 128],
                        NT,
                        preferred_element_type=F32,
                    )
                    scores = scores * LOG2E + bias_ref[at, :]
                    shift = own[:, head : head + 1]
                    if exact:
                        mine = shift
                        shift = jnp.maximum(jnp.max(scores, axis=1, keepdims=True), mine)
                        self_weight = jnp.exp2(mine - shift).astype(BF16).astype(F32)
                        tops = jnp.where(lane == head, shift, tops)
                    else:
                        self_weight = 1.0
                    weights = jnp.exp2(scores - shift).astype(BF16)
                    part = jnp.dot(weights, val_ref[pair], preferred_element_type=F32)
                    sums = jnp.where(lane == head, part[:, 128:] + self_weight, sums)
                    sides.append(part[:, :128] + self_weight * value_ref[at, lo : lo + 128].astype(F32))
                acc_ref[at, lo : lo + 128] = jnp.where(lane < 64, sides[0], sides[1])
            top_ref[at, :] = tops
            sum_ref[at, :] = sums
            return carry

        lax.fori_loop(0, n // step, body, 0)

    attend(256, False)
    worst = jnp.max(jnp.max(sum_ref[...], axis=0, keepdims=True))

    @pl.when(jnp.logical_not(worst < BIG))
    def _():
        attend(64, True)

    puts = [
        start_copy(top_ref, top_hbm, sems.at[12]),
        start_copy(sum_ref, sum_hbm, sems.at[13]),
        start_copy(acc_ref, acc_hbm, sems.at[14]),
    ]
    for copy in puts:
        copy.wait()


def near_attend(got, w, everything, own):
    n, d = own.shape[0], w.shape[1] // 2
    slots = got.shape[0]
    ins = [(got.shape, BF16), (w.shape, BF16), ((n, d), BF16), ((n, slots), BF16)]
    ins += [(own.shape, F32), ((n, d), BF16)]
    outs = [((n, 128), F32), ((n, 128), F32), ((n, d), F32)]
    return pl.pallas_call(
        near_kernel,
        out_shape=tuple(shape(*o) for o in outs),
        in_specs=[HBM] * 4,
        out_specs=(HBM,) * 3,
        scratch_shapes=[pltpu.VMEM(*v) for v in ins + outs]
        + [
            pltpu.VMEM((slots, d), BF16),
            pltpu.VMEM((HEADS // 2, slots, 256), BF16),
            pltpu.VMEM((n, slots), F32),
            pltpu.SemaphoreType.DMA((15,)),
        ],
        compiler_params=params(),
        cost_estimate=pl.CostEstimate(flops=5 * 10**9, bytes_accessed=5 * 10**6, transcendentals=10**6),
        name="near_attend",
    )(got, w, everything, own)


def disk_kernel(*refs, pieces):
    (start_ref, extent_ref, lifted_hbm), refs = refs[:3], refs[3:]
    piece_hbm, refs = refs[:pieces], refs[pieces:]
    late_hbm, refs = refs[:7], refs[7:]
    out_ref, own_ref, lifted_ref, tok_ref = refs[:4]
    top_ref, sum_ref, near_ref, wd_ref, wout_ref, x_ref = late_refs = refs[4:10]
    shift_ref, acc_ref, den_ref, att_ref, sems, tok_sems = refs[10:]
    own_hbm = late_hbm[0]
    n, d = x_ref.shape
    rows = lifted_ref.shape[0]
    disks, size = piece_hbm[0].shape[:2]

    get_own = start_copy(own_hbm, own_ref, sems.at[0])
    get_lifted = start_copy(lifted_hbm.at[pl.ds(0, rows), :], lifted_ref, sems.at[1])
    here = lax.axis_index("lon")
    sectors = lax.axis_size("lon")

    def seen(disk):
        return lax.rem(here - start_ref[disk] + sectors, sectors) < extent_ref[disk]

    def token_copies(disk):
        return [
            pltpu.make_async_copy(
                piece_hbm[i].at[disk],
                tok_ref.at[disk, pl.ds(i * size, size), :],
                tok_sems.at[disk, i],
            )
            for i in range(pieces)
        ]

    for disk in range(disks):

        @pl.when(seen(disk))
        def _():
            for copy in token_copies(disk):
                copy.start()

    late = [
        start_copy(source, target, sems.at[2 + i])
        for i, (source, target) in enumerate(zip(late_hbm[1:], late_refs))
    ]

    def add_disks(step, unroll, first):
        den_ref[...] = jnp.zeros_like(den_ref)
        acc_ref[...] = jnp.zeros_like(acc_ref)
        if first:
            get_own.wait()
            for head in range(HEADS):
                shift_ref[pl.ds(head * n, n), :] = jnp.broadcast_to(own_ref[:, head : head + 1], (n, 128))
            get_lifted.wait()
            for disk in range(disks):

                @pl.when(seen(disk))
                def _():
                    for copy in token_copies(disk):
                        copy.wait()

        def add_disk(disk, carry):
            @pl.when(seen(disk))
            def _():
                def body(i, inner):
                    for u in range(unroll):
                        at = pl.ds(pl.multiple_of((i * unroll + u) * step, step), step)
                        scores = lax.dot_general(
                            lifted_ref[at, :], tok_ref[disk], NT, preferred_element_type=F32
                        )
                        weights = jnp.exp2(scores - shift_ref[at, :1])
                        part = weights[:, :128]
                        for j in range(1, weights.shape[1] // 128):
                            part = part + weights[:, j * 128 : j * 128 + 128]
                        den_ref[at, :] += part
                        acc_ref[at, :] += jnp.dot(
                            weights.astype(BF16), tok_ref[disk], preferred_element_type=F32
                        )
                    return inner

                lax.fori_loop(0, rows // (step * unroll), body, 0)

            return carry

        lax.fori_loop(0, disks, add_disk, 0)

    add_disks(256, 8, True)

    worst = jnp.max(jnp.max(den_ref[...], axis=0, keepdims=True))

    @pl.when(jnp.logical_not(worst < BIG))
    def _():
        def top_disk(disk, carry):
            @pl.when(seen(disk))
            def _():
                def body(i, inner):
                    at = pl.ds(pl.multiple_of(i * 128, 128), 128)
                    scores = lax.dot_general(
                        lifted_ref[at, :], tok_ref[disk], NT, preferred_element_type=F32
                    )
                    best = jnp.max(scores, axis=1, keepdims=True)
                    shift_ref[at, :] = jnp.maximum(shift_ref[at, :], best)
                    return inner

                lax.fori_loop(0, rows // 128, body, 0)

            return carry

        lax.fori_loop(0, disks, top_disk, 0)
        add_disks(128, 1, False)

    for copy in late:
        copy.wait()
    lane = lax.broadcasted_iota(jnp.int32, (n, 128), 1)
    for pair in range(HEADS // 2):
        lo = pair * 128
        sides = []
        for odd in range(2):
            head = 2 * pair + odd
            at = pl.ds(head * n, n)
            shift = shift_ref[at, :1]
            top = top_ref[:, head : head + 1]
            best = jnp.maximum(shift, top)
            disk_scale = jnp.exp2(shift - best)
            near_scale = jnp.exp2(top - best)
            total = (
                jnp.sum(den_ref[at, :], axis=1, keepdims=True) * disk_scale
                + sum_ref[:, head : head + 1] * near_scale
            )
            inv = 1.0 / total
            mixed = (acc_ref[at, :] * (disk_scale * inv)).astype(BF16)
            part = jnp.dot(mixed, wd_ref[:, d + lo : d + lo + 128], preferred_element_type=F32)
            sides.append(part + near_ref[:, lo : lo + 128] * (near_scale * inv))
        att_ref[:, lo : lo + 128] = jnp.where(lane < 64, sides[0], sides[1]).astype(BF16)
    out = jnp.dot(att_ref[...], wout_ref[...], preferred_element_type=F32)
    out_ref[...] = (x_ref[...].astype(F32) + out).astype(BF16)


def disk_attend(start, extent, everything, pieces, own, top, total, near, wd, wout, x):
    n, d = x.shape
    disks = pieces[0].shape[0]
    tokens = sum(piece.shape[1] for piece in pieces)
    rows, width = HEADS * n, wd.shape[0]
    late = (top, total, near, wd, wout, x)
    return pl.pallas_call(
        functools.partial(disk_kernel, pieces=len(pieces)),
        out_shape=shape((n, d), BF16),
        in_specs=[SMEM, SMEM] + [HBM] * (8 + len(pieces)),
        out_specs=VMEM,
        scratch_shapes=[
            pltpu.VMEM(own.shape, F32),
            pltpu.VMEM((rows, width), BF16),
            pltpu.VMEM((disks, tokens, width), BF16),
        ]
        + [pltpu.VMEM(v.shape, v.dtype) for v in late]
        + [
            pltpu.VMEM((rows, 128), F32),
            pltpu.VMEM((rows, width), F32),
            pltpu.VMEM((rows, 128), F32),
            pltpu.VMEM((n, d), BF16),
            pltpu.SemaphoreType.DMA((8,)),
            pltpu.SemaphoreType.DMA((disks, len(pieces))),
        ],
        compiler_params=params(),
        cost_estimate=pl.CostEstimate(flops=16 * 10**9, bytes_accessed=10**7, transcendentals=10**6),
        name="disk_attend",
    )(start, extent, everything, *pieces, own, *late)


def device_at(z, y, x, core):
    return (z * 2 + y // 2) * 16 + (y % 2) * 8 + x * 2 + core


def ring(*steps):
    pairs = []
    for z in range(4):
        for y in range(4):
            for x in range(4):
                for core in range(2):
                    axis, by = steps[core]
                    to = [z, y, x]
                    to[axis] = (to[axis] + by) % 4
                    pairs.append((device_at(z, y, x, core), device_at(*to, core)))
    return pairs


def other_core():
    return [(s, s ^ 1) for s in range(128)]


def spread(block, first, second):
    return [lax.ppermute(block, AXES, ring((first, by), (second, by))) for by in (1, 3, 2)]


def gather_tokens(disk_tokens):
    block = jnp.transpose(disk_tokens, (1, 0, 2))
    block = jnp.concatenate([block] + spread(block, 0, 1), axis=1)
    block = jnp.concatenate([block] + spread(block, 1, 2), axis=1)
    pieces = [block] + spread(block, 2, 0)
    return pieces + [lax.ppermute(piece, AXES, other_core()) for piece in pieces]


def local(
    mesh_nodes,
    norm_gain,
    w_query,
    w_node_kv,
    obs_rows,
    w_obs_kv,
    obs_owner,
    neighbours,
    neighbour_mask,
    disk_tokens,
    w_disk_kv,
    disk_start,
    disk_extent,
    w_out,
):
    devices = lax.axis_size("lat") * lax.axis_size("lon")
    width = obs_rows.shape[1]
    slots = devices * 8
    send = place(obs_owner.reshape(1, -1), obs_rows, slots)
    got = lax.all_to_all(
        send.reshape(devices, 8, width), AXES, split_axis=0, concat_axis=0, tiled=True
    ).reshape(slots, width)
    everything, own = prep(
        neighbours.T,
        neighbour_mask.T,
        mesh_nodes,
        norm_gain.reshape(1, -1),
        w_query,
        w_node_kv,
        w_disk_kv,
    )
    pieces = gather_tokens(disk_tokens)
    top, total, near = near_attend(got, w_obs_kv, everything, own)
    return disk_attend(
        disk_start, disk_extent, everything, pieces, own, top, total, near, w_disk_kv, w_out, mesh_nodes
    )


def solution(mesh):
    split = P(AXES, None)
    return jax.shard_map(
        local,
        mesh=mesh,
        in_specs=(
            split,
            P(),
            P(),
            P(),
            split,
            P(),
            split,
            split,
            split,
            P(AXES, None, None),
            P(),
            P(),
            P(),
            P(),
        ),
        out_specs=split,
        check_vma=False,
    )
```

```python
import functools

import jax
import jax.numpy as jnp
from jax import lax
from jax.experimental import pallas as pl
from jax.experimental.pallas import tpu as pltpu
from jax.sharding import PartitionSpec as P


HEADS = 8
AXES = ("lat", "lon")
LOG2E = 1.4426950408889634
EMPTY = 65536.0
NEG = -1e30
BIG = 2.0**100
F32 = jnp.float32
BF16 = jnp.bfloat16
NT = (((1,), (1,)), ((), ()))


def shape(dims, dtype):
    return jax.ShapeDtypeStruct(dims, dtype)


def params(grant=60 * 1024 * 1024):
    return pltpu.CompilerParams(vmem_limit_bytes=grant)


HBM = pl.BlockSpec(memory_space=pltpu.HBM)
VMEM = pl.BlockSpec(memory_space=pltpu.VMEM)
SMEM = pl.BlockSpec(memory_space=pltpu.SMEM)


def start_copy(source, target, sem):
    copy = pltpu.make_async_copy(source, target, sem)
    copy.start()
    return copy


def place_kernel(owner_ref, rows_ref, send_ref, held_ref, sems):
    count = rows_ref.shape[0]
    slots = send_ref.shape[0]
    owners = slots // 8
    owner = owner_ref[...]
    hot = jnp.where(lax.broadcasted_iota(jnp.int32, (owners, count), 0) == owner, 1.0, 0.0)
    row = lax.broadcasted_iota(jnp.int32, (count, count), 0)
    col = lax.broadcasted_iota(jnp.int32, (count, count), 1)
    earlier = jnp.where(row < col, 1.0, 0.0).astype(BF16)
    before = jnp.dot(hot.astype(BF16), earlier, preferred_element_type=F32)
    rank = jnp.sum(before * hot, axis=0, keepdims=True)
    slot = owner * 8 + rank.astype(jnp.int32)
    rows = rows_ref[...]
    ones_rows = jnp.ones((count, 128), BF16)
    step = slots // 4
    copies = []
    for i in range(4):
        at = pl.ds(i * step, step)
        ids_col = lax.broadcasted_iota(jnp.int32, (step, count), 0) + i * step
        placing = jnp.where(ids_col == slot, 1.0, 0.0).astype(BF16)
        placed = jnp.dot(placing, rows, preferred_element_type=F32)
        filled = jnp.dot(placing, ones_rows, preferred_element_type=F32)
        filled = jnp.concatenate([filled, filled], axis=1)
        held_ref[at, :] = jnp.where(filled > 0.5, placed, EMPTY).astype(BF16)
        copies.append(start_copy(held_ref.at[at, :], send_ref.at[at, :], sems.at[i]))
    for copy in copies:
        copy.wait()


def place(owner, rows, slots):
    return pl.pallas_call(
        place_kernel,
        out_shape=shape((slots, rows.shape[1]), BF16),
        in_specs=[VMEM, VMEM],
        out_specs=HBM,
        scratch_shapes=[pltpu.VMEM((slots, rows.shape[1]), BF16), pltpu.SemaphoreType.DMA((4,))],
        compiler_params=params(67043328),
        cost_estimate=pl.CostEstimate(flops=10**9, bytes_accessed=10**6, transcendentals=0),
        name="place",
    )(owner, rows)


def one_head(pair, odd):
    lane = lax.broadcasted_iota(jnp.int32, pair.shape, 1)
    keep = lane >= 64 if odd else lane < 64
    return jnp.where(keep, pair.astype(F32), 0.0).astype(pair.dtype)


def prep_kernel(
    near_ref, mark_ref, x_hbm, gain_ref, wq_hbm, wkv_hbm, wd_hbm, all_hbm, own_hbm,
    x_ref, wq_ref, wkv_ref, wd_ref, all_ref, own_ref, list_ref, sems, out_sems,
):
    n, d = x_ref.shape
    slots = 1024
    get_x = start_copy(x_hbm, x_ref, sems.at[0])
    get_wq = start_copy(wq_hbm, wq_ref, sems.at[1])
    get_wkv = start_copy(wkv_hbm, wkv_ref, sems.at[2])
    get_wd = start_copy(wd_hbm, wd_ref, sems.at[3])
    list_ref[...] = jnp.transpose(jnp.where(mark_ref[...] > 0, near_ref[...], -1), (1, 0))
    step = 64

    def body(i, carry):
        start = pl.multiple_of(i * step, step)
        near = list_ref[pl.ds(start, step), :].astype(jnp.int16)
        ids = lax.broadcasted_iota(jnp.int16, (step, slots), 1)
        total = jnp.zeros((step, slots), jnp.int16)
        one = jnp.ones((step, slots), jnp.int16)
        for entry in range(near.shape[1]):
            total = jnp.where(ids == near[:, entry : entry + 1], total + one, total)
        count = total.astype(F32).astype(BF16)
        for j in range(4):
            at = pl.ds(pl.multiple_of((12 + j) * n + start, step), step)
            all_ref[at, :] = count[:, j * 256 : j * 256 + 256]
        return carry

    lax.fori_loop(0, n // step, body, 0)

    def put(block, blocks, sem):
        at = pl.ds(block * n, blocks * n)
        return start_copy(all_ref.at[at, :], all_hbm.at[at, :], out_sems.at[sem])

    puts = [put(12, 4, 0)]
    get_x.wait()
    x = x_ref[...].astype(F32)
    inverse = lax.rsqrt(jnp.mean(x * x, axis=1, keepdims=True) + 1e-06)
    normed = (x * inverse * gain_ref[...]).astype(BF16)
    get_wq.wait()
    query = (jnp.dot(normed, wq_ref[...], preferred_element_type=F32) * 0.125).astype(BF16)
    get_wkv.wait()
    kv = jnp.dot(normed, wkv_ref[...], preferred_element_type=F32).astype(BF16)
    for j in range(2):
        all_ref[pl.ds((8 + j) * n, n), :] = query[:, j * 256 : j * 256 + 256]
        all_ref[pl.ds((10 + j) * n, n), :] = kv[:, d + j * 256 : d + j * 256 + 256]
    puts.append(put(8, 4, 1))
    prod = query.astype(F32) * kv[:, :d].astype(F32)
    lane = lax.broadcasted_iota(jnp.int32, (n, 128), 1)
    own = jnp.zeros((n, 128), F32)
    get_wd.wait()
    for head in range(HEADS):
        lo = head // 2 * 128
        part = jnp.sum(prod[:, head * 64 : head * 64 + 64], axis=1, keepdims=True) * LOG2E
        own = jnp.where(lane == head, part, own)
        lifted = lax.dot_general(
            one_head(query[:, lo : lo + 128], head % 2),
            wd_ref[:, lo : lo + 128],
            NT,
            preferred_element_type=F32,
        )
        all_ref[pl.ds(head * n, n), :] = (lifted * LOG2E).astype(BF16)
        puts.append(put(head, 1, 2 + head))
    own_ref[...] = own
    puts.append(start_copy(own_ref, own_hbm, out_sems.at[2 + HEADS]))
    for copy in puts:
        copy.wait()


def prep(near, mark, x, gain, wq, wkv, wd):
    n, _ = x.shape
    outs = [((16 * n, 256), BF16), ((n, 128), F32)]
    ins = [(v.shape, v.dtype) for v in (x, wq, wkv, wd)]
    return pl.pallas_call(
        prep_kernel,
        out_shape=tuple(shape(*o) for o in outs),
        in_specs=[VMEM, VMEM, HBM, VMEM, HBM, HBM, HBM],
        out_specs=(HBM,) * 2,
        scratch_shapes=[pltpu.VMEM(*v) for v in ins + outs]
        + [
            pltpu.VMEM(near.shape[::-1], jnp.int32),
            pltpu.SemaphoreType.DMA((4,)),
            pltpu.SemaphoreType.DMA((3 + HEADS,)),
        ],
        compiler_params=params(),
        cost_estimate=pl.CostEstimate(flops=8 * 10**9, bytes_accessed=8 * 10**6, transcendentals=0),
        name="prep",
    )(near, mark, x, gain, wq, wkv, wd)


def near_kernel(
    got_hbm, w_hbm, all_hbm, own_hbm, top_hbm, sum_hbm, acc_hbm,
    got_ref, w_ref, query_ref, count_ref, own_ref, value_ref, top_ref, sum_ref, acc_ref,
    key_ref, val_ref, bias_ref, sems,
):
    slots = got_ref.shape[0]
    n, d = query_ref.shape
    get_got = start_copy(got_hbm, got_ref, sems.at[0])
    get_w = start_copy(w_hbm, w_ref, sems.at[1])

    def get_block(block, target, j, sem):
        return start_copy(
            all_hbm.at[pl.ds(block * n, n), :], target.at[:, pl.ds(j * 256, 256)], sems.at[sem]
        )

    get_count = [get_block(12 + j, count_ref, j, 8 + j) for j in range(4)]
    gets = [get_block(8 + j, query_ref, j, 2 + j) for j in range(2)]
    gets += [get_block(10 + j, value_ref, j, 4 + j) for j in range(2)]
    gets.append(start_copy(own_hbm, own_ref, sems.at[6]))
    get_got.wait()
    got = got_ref[...]
    absent = got.astype(F32) > 1024.0
    rows = jnp.where(absent, 0.0, got.astype(F32)).astype(BF16)
    ones = jnp.ones((8, 128), BF16)
    empty = lax.dot_general(
        ones, jnp.where(absent[:, :128], 1.0, 0.0).astype(BF16), NT, preferred_element_type=F32
    )[0:1, :]
    get_w.wait()
    kv = jnp.dot(rows, w_ref[...], preferred_element_type=F32).astype(BF16)
    key_ref[...] = kv[:, :d]
    for pair in range(HEADS // 2):
        lo = d + pair * 128
        val_ref[pair, :, :128] = kv[:, lo : lo + 128]
        val_ref[pair, :, 128:] = jnp.ones((slots, 128), BF16)
    for copy in get_count:
        copy.wait()
    count = count_ref[...].astype(F32)
    bias_ref[...] = jnp.where((count > 0.0) & (empty < 0.5), jnp.log2(jnp.maximum(count, 1.0)), NEG)
    for copy in gets:
        copy.wait()

    def attend(step, exact):
        lane = lax.broadcasted_iota(jnp.int32, (step, 128), 1)

        def body(i, carry):
            at = pl.ds(pl.multiple_of(i * step, step), step)
            own = own_ref[at, :]
            tops = own
            sums = jnp.ones((step, 128), F32)
            for pair in range(HEADS // 2):
                lo = pair * 128
                sides = []
                for odd in range(2):
                    head = 2 * pair + odd
                    scores = lax.dot_general(
                        one_head(query_ref[at, lo : lo + 128], odd),
                        key_ref[:, lo : lo + 128],
                        NT,
                        preferred_element_type=F32,
                    )
                    scores = scores * LOG2E + bias_ref[at, :]
                    shift = own[:, head : head + 1]
                    if exact:
                        mine = shift
                        shift = jnp.maximum(jnp.max(scores, axis=1, keepdims=True), mine)
                        self_weight = jnp.exp2(mine - shift).astype(BF16).astype(F32)
                        tops = jnp.where(lane == head, shift, tops)
                    else:
                        self_weight = 1.0
                    weights = jnp.exp2(scores - shift).astype(BF16)
                    part = jnp.dot(weights, val_ref[pair], preferred_element_type=F32)
                    sums = jnp.where(lane == head, part[:, 128:] + self_weight, sums)
                    sides.append(part[:, :128] + self_weight * value_ref[at, lo : lo + 128].astype(F32))
                acc_ref[at, lo : lo + 128] = jnp.where(lane < 64, sides[0], sides[1])
            top_ref[at, :] = tops
            sum_ref[at, :] = sums
            return carry

        lax.fori_loop(0, n // step, body, 0)

    attend(256, False)
    worst = jnp.max(jnp.max(sum_ref[...], axis=0, keepdims=True))

    @pl.when(jnp.logical_not(worst < BIG))
    def _():
        attend(64, True)

    puts = [
        start_copy(top_ref, top_hbm, sems.at[12]),
        start_copy(sum_ref, sum_hbm, sems.at[13]),
        start_copy(acc_ref, acc_hbm, sems.at[14]),
    ]
    for copy in puts:
        copy.wait()


def near_attend(got, w, everything, own):
    n, d = own.shape[0], w.shape[1] // 2
    slots = got.shape[0]
    ins = [(got.shape, BF16), (w.shape, BF16), ((n, d), BF16), ((n, slots), BF16)]
    ins += [(own.shape, F32), ((n, d), BF16)]
    outs = [((n, 128), F32), ((n, 128), F32), ((n, d), F32)]
    return pl.pallas_call(
        near_kernel,
        out_shape=tuple(shape(*o) for o in outs),
        in_specs=[HBM] * 4,
        out_specs=(HBM,) * 3,
        scratch_shapes=[pltpu.VMEM(*v) for v in ins + outs]
        + [
            pltpu.VMEM((slots, d), BF16),
            pltpu.VMEM((HEADS // 2, slots, 256), BF16),
            pltpu.VMEM((n, slots), F32),
            pltpu.SemaphoreType.DMA((15,)),
        ],
        compiler_params=params(67043328),
        cost_estimate=pl.CostEstimate(flops=5 * 10**9, bytes_accessed=5 * 10**6, transcendentals=10**6),
        name="near_attend",
    )(got, w, everything, own)


def disk_kernel(*refs, pieces):
    (start_ref, extent_ref, lifted_hbm), refs = refs[:3], refs[3:]
    piece_hbm, refs = refs[:pieces], refs[pieces:]
    late_hbm, refs = refs[:7], refs[7:]
    out_ref, own_ref, lifted_ref, tok_ref = refs[:4]
    top_ref, sum_ref, near_ref, wd_ref, wout_ref, x_ref = late_refs = refs[4:10]
    shift_ref, acc_ref, den_ref, att_ref, sems, tok_sems = refs[10:]
    own_hbm = late_hbm[0]
    n, d = x_ref.shape
    rows = lifted_ref.shape[0]
    disks, size = piece_hbm[0].shape[:2]

    get_own = start_copy(own_hbm, own_ref, sems.at[0])
    get_lifted = start_copy(lifted_hbm.at[pl.ds(0, rows), :], lifted_ref, sems.at[1])
    here = lax.axis_index("lon")
    sectors = lax.axis_size("lon")

    def seen(disk):
        return lax.rem(here - start_ref[disk] + sectors, sectors) < extent_ref[disk]

    def token_copies(disk):
        return [
            pltpu.make_async_copy(
                piece_hbm[i].at[disk],
                tok_ref.at[disk, pl.ds(i * size, size), :],
                tok_sems.at[disk, i],
            )
            for i in range(pieces)
        ]

    for disk in range(disks):

        @pl.when(seen(disk))
        def _():
            for copy in token_copies(disk):
                copy.start()

    late = [
        start_copy(source, target, sems.at[2 + i])
        for i, (source, target) in enumerate(zip(late_hbm[1:], late_refs))
    ]

    def add_disks(step, unroll, first):
        den_ref[...] = jnp.zeros_like(den_ref)
        acc_ref[...] = jnp.zeros_like(acc_ref)
        if first:
            get_own.wait()
            for head in range(HEADS):
                shift_ref[pl.ds(head * n, n), :] = jnp.broadcast_to(own_ref[:, head : head + 1], (n, 128))
            get_lifted.wait()
            for disk in range(disks):

                @pl.when(seen(disk))
                def _():
                    for copy in token_copies(disk):
                        copy.wait()

        def add_disk(disk, carry):
            @pl.when(seen(disk))
            def _():
                def body(i, inner):
                    for u in range(unroll):
                        at = pl.ds(pl.multiple_of((i * unroll + u) * step, step), step)
                        scores = lax.dot_general(
                            lifted_ref[at, :], tok_ref[disk], NT, preferred_element_type=F32
                        )
                        weights = jnp.exp2(scores - shift_ref[at, :1])
                        part = weights[:, :128]
                        for j in range(1, weights.shape[1] // 128):
                            part = part + weights[:, j * 128 : j * 128 + 128]
                        den_ref[at, :] += part
                        acc_ref[at, :] += jnp.dot(
                            weights.astype(BF16), tok_ref[disk], preferred_element_type=F32
                        )
                    return inner

                lax.fori_loop(0, rows // (step * unroll), body, 0)

            return carry

        lax.fori_loop(0, disks, add_disk, 0)

    add_disks(256, 8, True)

    worst = jnp.max(jnp.max(den_ref[...], axis=0, keepdims=True))

    @pl.when(jnp.logical_not(worst < BIG))
    def _():
        def top_disk(disk, carry):
            @pl.when(seen(disk))
            def _():
                def body(i, inner):
                    at = pl.ds(pl.multiple_of(i * 128, 128), 128)
                    scores = lax.dot_general(
                        lifted_ref[at, :], tok_ref[disk], NT, preferred_element_type=F32
                    )
                    best = jnp.max(scores, axis=1, keepdims=True)
                    shift_ref[at, :] = jnp.maximum(shift_ref[at, :], best)
                    return inner

                lax.fori_loop(0, rows // 128, body, 0)

            return carry

        lax.fori_loop(0, disks, top_disk, 0)
        add_disks(128, 1, False)

    for copy in late:
        copy.wait()
    lane = lax.broadcasted_iota(jnp.int32, (n, 128), 1)
    for pair in range(HEADS // 2):
        lo = pair * 128
        sides = []
        for odd in range(2):
            head = 2 * pair + odd
            at = pl.ds(head * n, n)
            shift = shift_ref[at, :1]
            top = top_ref[:, head : head + 1]
            best = jnp.maximum(shift, top)
            disk_scale = jnp.exp2(shift - best)
            near_scale = jnp.exp2(top - best)
            total = (
                jnp.sum(den_ref[at, :], axis=1, keepdims=True) * disk_scale
                + sum_ref[:, head : head + 1] * near_scale
            )
            inv = 1.0 / total
            mixed = (acc_ref[at, :] * (disk_scale * inv)).astype(BF16)
            part = jnp.dot(mixed, wd_ref[:, d + lo : d + lo + 128], preferred_element_type=F32)
            sides.append(part + near_ref[:, lo : lo + 128] * (near_scale * inv))
        att_ref[:, lo : lo + 128] = jnp.where(lane < 64, sides[0], sides[1]).astype(BF16)
    out = jnp.dot(att_ref[...], wout_ref[...], preferred_element_type=F32)
    out_ref[...] = (x_ref[...].astype(F32) + out).astype(BF16)


def disk_attend(start, extent, everything, pieces, own, top, total, near, wd, wout, x):
    n, d = x.shape
    disks = pieces[0].shape[0]
    tokens = sum(piece.shape[1] for piece in pieces)
    rows, width = HEADS * n, wd.shape[0]
    late = (top, total, near, wd, wout, x)
    return pl.pallas_call(
        functools.partial(disk_kernel, pieces=len(pieces)),
        out_shape=shape((n, d), BF16),
        in_specs=[SMEM, SMEM] + [HBM] * (8 + len(pieces)),
        out_specs=VMEM,
        scratch_shapes=[
            pltpu.VMEM(own.shape, F32),
            pltpu.VMEM((rows, width), BF16),
            pltpu.VMEM((disks, tokens, width), BF16),
        ]
        + [pltpu.VMEM(v.shape, v.dtype) for v in late]
        + [
            pltpu.VMEM((rows, 128), F32),
            pltpu.VMEM((rows, width), F32),
            pltpu.VMEM((rows, 128), F32),
            pltpu.VMEM((n, d), BF16),
            pltpu.SemaphoreType.DMA((8,)),
            pltpu.SemaphoreType.DMA((disks, len(pieces))),
        ],
        compiler_params=params(67043328),
        cost_estimate=pl.CostEstimate(flops=16 * 10**9, bytes_accessed=10**7, transcendentals=10**6),
        name="disk_attend",
    )(start, extent, everything, *pieces, own, *late)


def device_at(z, y, x, core):
    return (z * 2 + y // 2) * 16 + (y % 2) * 8 + x * 2 + core


def ring(*steps):
    pairs = []
    for z in range(4):
        for y in range(4):
            for x in range(4):
                for core in range(2):
                    axis, by = steps[core]
                    to = [z, y, x]
                    to[axis] = (to[axis] + by) % 4
                    pairs.append((device_at(z, y, x, core), device_at(*to, core)))
    return pairs


def other_core():
    return [(s, s ^ 1) for s in range(128)]


def spread(block, first, second):
    got = []
    for by in (1, 3, 2):
        got.append(lax.ppermute(block, AXES, ring((first, by), (second, by))))
    return got


def gather_tokens(disk_tokens):
    block = jnp.transpose(disk_tokens, (1, 0, 2))
    block = jnp.concatenate([block] + spread(block, 0, 1), axis=1)
    block = lax.optimization_barrier(block)
    block = jnp.concatenate([block] + spread(block, 1, 2), axis=1)
    block = lax.optimization_barrier(block)
    pieces = [block] + spread(block, 2, 0)
    swapped = []
    for piece in pieces:
        swapped.append(lax.ppermute(piece, AXES, other_core()))
    return pieces + swapped


def local(
    mesh_nodes,
    norm_gain,
    w_query,
    w_node_kv,
    obs_rows,
    w_obs_kv,
    obs_owner,
    neighbours,
    neighbour_mask,
    disk_tokens,
    w_disk_kv,
    disk_start,
    disk_extent,
    w_out,
):
    devices = lax.axis_size("lat") * lax.axis_size("lon")
    width = obs_rows.shape[1]
    slots = devices * 8
    send = place(obs_owner.reshape(1, -1), obs_rows, slots)
    got = lax.all_to_all(
        send.reshape(devices, 8, width), AXES, split_axis=0, concat_axis=0, tiled=True
    ).reshape(slots, width)
    everything, own = prep(
        neighbours.T,
        neighbour_mask.T,
        mesh_nodes,
        norm_gain.reshape(1, -1),
        w_query,
        w_node_kv,
        w_disk_kv,
    )
    pieces = gather_tokens(disk_tokens)
    top, total, near = near_attend(got, w_obs_kv, everything, own)
    return disk_attend(
        disk_start, disk_extent, everything, pieces, own, top, total, near, w_disk_kv, w_out, mesh_nodes
    )


def solution(mesh):
    split = P(AXES, None)
    return jax.shard_map(
        local,
        mesh=mesh,
        in_specs=(
            split,
            P(),
            P(),
            P(),
            split,
            P(),
            split,
            split,
            split,
            P(AXES, None, None),
            P(),
            P(),
            P(),
            P(),
        ),
        out_specs=split,
        check_vma=False,
    )
```

```python
import functools

import jax
import jax.numpy as jnp
from jax import lax
from jax.experimental import pallas as pl
from jax.experimental.pallas import tpu as pltpu
from jax.sharding import PartitionSpec as P


HEADS = 8
AXES = ("lat", "lon")
LOG2E = 1.4426950408889634
EMPTY = 65536.0
NEG = -1e30
BIG = 2.0**100
F32 = jnp.float32
BF16 = jnp.bfloat16
NT = (((1,), (1,)), ((), ()))


def shape(dims, dtype):
    return jax.ShapeDtypeStruct(dims, dtype)


FULL = 67043328


def params(grant):
    return pltpu.CompilerParams(vmem_limit_bytes=grant)


HBM = pl.BlockSpec(memory_space=pltpu.HBM)
VMEM = pl.BlockSpec(memory_space=pltpu.VMEM)
SMEM = pl.BlockSpec(memory_space=pltpu.SMEM)


def start_copy(source, target, sem):
    copy = pltpu.make_async_copy(source, target, sem)
    copy.start()
    return copy


def place_kernel(owner_ref, rows_ref, send_ref, held_ref, sems):
    count = rows_ref.shape[0]
    slots = send_ref.shape[0]
    owners = slots // 8
    owner = owner_ref[...]
    hot = jnp.where(lax.broadcasted_iota(jnp.int32, (owners, count), 0) == owner, 1.0, 0.0)
    row = lax.broadcasted_iota(jnp.int32, (count, count), 0)
    col = lax.broadcasted_iota(jnp.int32, (count, count), 1)
    earlier = jnp.where(row < col, 1.0, 0.0).astype(BF16)
    before = jnp.dot(hot.astype(BF16), earlier, preferred_element_type=F32)
    rank = jnp.sum(before * hot, axis=0, keepdims=True)
    slot = owner * 8 + rank.astype(jnp.int32)
    rows = rows_ref[...]
    ones_rows = jnp.ones((count, 128), BF16)
    step = slots // 4
    copies = []
    for i in range(4):
        at = pl.ds(i * step, step)
        ids_col = lax.broadcasted_iota(jnp.int32, (step, count), 0) + i * step
        placing = jnp.where(ids_col == slot, 1.0, 0.0).astype(BF16)
        placed = jnp.dot(placing, rows, preferred_element_type=F32)
        filled = jnp.dot(placing, ones_rows, preferred_element_type=F32)
        filled = jnp.concatenate([filled, filled], axis=1)
        held_ref[at, :] = jnp.where(filled > 0.5, placed, EMPTY).astype(BF16)
        copies.append(start_copy(held_ref.at[at, :], send_ref.at[at, :], sems.at[i]))
    for copy in copies:
        copy.wait()


def place(owner, rows, slots):
    return pl.pallas_call(
        place_kernel,
        out_shape=shape((slots, rows.shape[1]), BF16),
        in_specs=[VMEM, VMEM],
        out_specs=HBM,
        scratch_shapes=[pltpu.VMEM((slots, rows.shape[1]), BF16), pltpu.SemaphoreType.DMA((4,))],
        compiler_params=params(FULL),
        cost_estimate=pl.CostEstimate(flops=10**9, bytes_accessed=10**6, transcendentals=0),
        name="place",
    )(owner, rows)


def one_head(pair, odd):
    lane = lax.broadcasted_iota(jnp.int32, pair.shape, 1)
    keep = lane >= 64 if odd else lane < 64
    return jnp.where(keep, pair.astype(F32), 0.0).astype(pair.dtype)


def node_kernel(
    x_hbm, gain_ref, wq_hbm, wkv_hbm, query_hbm, value_hbm, own_hbm,
    x_ref, wq_ref, wkv_ref, query_ref, value_ref, own_ref, sems,
):
    n, d = x_ref.shape
    get_x = start_copy(x_hbm, x_ref, sems.at[0])
    get_wq = start_copy(wq_hbm, wq_ref, sems.at[1])
    get_wkv = start_copy(wkv_hbm, wkv_ref, sems.at[2])
    get_x.wait()
    x = x_ref[...].astype(F32)
    inverse = lax.rsqrt(jnp.mean(x * x, axis=1, keepdims=True) + 1e-06)
    normed = (x * inverse * gain_ref[...]).astype(BF16)
    get_wq.wait()
    query = (jnp.dot(normed, wq_ref[...], preferred_element_type=F32) * 0.125).astype(BF16)
    query_ref[...] = query
    puts = [start_copy(query_ref, query_hbm, sems.at[3])]
    get_wkv.wait()
    kv = jnp.dot(normed, wkv_ref[...], preferred_element_type=F32).astype(BF16)
    value_ref[...] = kv[:, d:]
    puts.append(start_copy(value_ref, value_hbm, sems.at[4]))
    prod = query.astype(F32) * kv[:, :d].astype(F32)
    lane = lax.broadcasted_iota(jnp.int32, (n, 128), 1)
    own = jnp.zeros((n, 128), F32)
    for head in range(HEADS):
        part = jnp.sum(prod[:, head * 64 : head * 64 + 64], axis=1, keepdims=True) * LOG2E
        own = jnp.where(lane == head, part, own)
    own_ref[...] = own
    puts.append(start_copy(own_ref, own_hbm, sems.at[5]))
    for copy in puts:
        copy.wait()


def node(x, gain, wq, wkv):
    n, d = x.shape
    outs = [((n, d), BF16), ((n, d), BF16), ((n, 128), F32)]
    ins = [(v.shape, v.dtype) for v in (x, wq, wkv)]
    return pl.pallas_call(
        node_kernel,
        out_shape=tuple(shape(*o) for o in outs),
        in_specs=[HBM, VMEM, HBM, HBM],
        out_specs=(HBM,) * 3,
        scratch_shapes=[pltpu.VMEM(*v) for v in ins + outs] + [pltpu.SemaphoreType.DMA((6,))],
        compiler_params=params(FULL),
        cost_estimate=pl.CostEstimate(flops=2 * 10**9, bytes_accessed=3 * 10**6, transcendentals=0),
        name="node",
    )(x, gain, wq, wkv)


def lift_kernel(query_ref, wd_ref, lifted_hbm, lifted_ref, sems):
    n = query_ref.shape[0]
    puts = []
    for head in range(HEADS):
        lo = head // 2 * 128
        lifted = lax.dot_general(
            one_head(query_ref[:, lo : lo + 128], head % 2),
            wd_ref[:, lo : lo + 128],
            NT,
            preferred_element_type=F32,
        )
        at = pl.ds(head * n, n)
        lifted_ref[at, :] = (lifted * LOG2E).astype(BF16)
        puts.append(start_copy(lifted_ref.at[at, :], lifted_hbm.at[at, :], sems.at[head]))
    for copy in puts:
        copy.wait()


def lift(query, wd):
    n = query.shape[0]
    out = ((HEADS * n, wd.shape[0]), BF16)
    return pl.pallas_call(
        lift_kernel,
        out_shape=shape(*out),
        in_specs=[VMEM, VMEM],
        out_specs=HBM,
        scratch_shapes=[pltpu.VMEM(*out), pltpu.SemaphoreType.DMA((HEADS,))],
        compiler_params=params(FULL),
        cost_estimate=pl.CostEstimate(flops=2 * 10**9, bytes_accessed=3 * 10**6, transcendentals=0),
        name="lift",
    )(query, wd)


def count_kernel(near_ref, mark_ref, count_hbm, count_ref, list_ref, sems):
    n, slots = count_ref.shape
    step = 64
    parts = n // step
    list_ref[...] = jnp.transpose(jnp.where(mark_ref[...] > 0, near_ref[...], -1), (1, 0))

    def piece(i):
        at = pl.ds(pl.multiple_of(i * step, step), step)
        return pltpu.make_async_copy(count_ref.at[at, :], count_hbm.at[at, :], sems.at[i])

    def body(i, carry):
        start = pl.multiple_of(i * step, step)
        near = list_ref[pl.ds(start, step), :].astype(jnp.int16)
        ids = lax.broadcasted_iota(jnp.int16, (step, slots), 1)
        total = jnp.zeros((step, slots), jnp.int16)
        one = jnp.ones((step, slots), jnp.int16)
        for entry in range(near.shape[1]):
            total = jnp.where(ids == near[:, entry : entry + 1], total + one, total)
        count_ref[pl.ds(start, step), :] = total.astype(F32).astype(BF16)
        piece(i).start()
        return carry

    lax.fori_loop(0, parts, body, 0)
    for i in range(parts):
        piece(i).wait()


def count_listed(near, mark, slots):
    n = near.shape[1]
    return pl.pallas_call(
        count_kernel,
        out_shape=shape((n, slots), BF16),
        in_specs=[VMEM, VMEM],
        out_specs=HBM,
        scratch_shapes=[
            pltpu.VMEM((n, slots), BF16),
            pltpu.VMEM(near.shape[::-1], jnp.int32),
            pltpu.SemaphoreType.DMA((n // 64,)),
        ],
        compiler_params=params(FULL),
        cost_estimate=pl.CostEstimate(flops=4 * 10**9, bytes_accessed=2 * 10**6, transcendentals=0),
        name="count_listed",
    )(near, mark)


def near_kernel(
    got_hbm, w_hbm, query_hbm, count_hbm, own_hbm, value_hbm, top_hbm, sum_hbm, acc_hbm,
    got_ref, w_ref, query_ref, count_ref, own_ref, value_ref, top_ref, sum_ref, acc_ref,
    key_ref, val_ref, bias_ref, sems,
):
    slots = got_ref.shape[0]
    n, d = query_ref.shape
    get_got = start_copy(got_hbm, got_ref, sems.at[0])
    get_w = start_copy(w_hbm, w_ref, sems.at[1])
    get_got.wait()
    get_count = start_copy(count_hbm, count_ref, sems.at[2])
    gets = [
        start_copy(query_hbm, query_ref, sems.at[3]),
        start_copy(own_hbm, own_ref, sems.at[4]),
        start_copy(value_hbm, value_ref, sems.at[5]),
    ]
    got = got_ref[...]
    absent = got.astype(F32) > 1024.0
    rows = jnp.where(absent, 0.0, got.astype(F32)).astype(BF16)
    ones = jnp.ones((8, 128), BF16)
    empty = lax.dot_general(
        ones, jnp.where(absent[:, :128], 1.0, 0.0).astype(BF16), NT, preferred_element_type=F32
    )[0:1, :]
    get_w.wait()
    kv = jnp.dot(rows, w_ref[...], preferred_element_type=F32).astype(BF16)
    key_ref[...] = kv[:, :d]
    for pair in range(HEADS // 2):
        lo = d + pair * 128
        val_ref[pair, :, :128] = kv[:, lo : lo + 128]
        val_ref[pair, :, 128:] = jnp.ones((slots, 128), BF16)
    get_count.wait()
    count = count_ref[...].astype(F32)
    bias_ref[...] = jnp.where((count > 0.0) & (empty < 0.5), jnp.log2(jnp.maximum(count, 1.0)), NEG)
    for copy in gets:
        copy.wait()

    def attend(step, exact):
        lane = lax.broadcasted_iota(jnp.int32, (step, 128), 1)

        def body(i, carry):
            at = pl.ds(pl.multiple_of(i * step, step), step)
            own = own_ref[at, :]
            tops = own
            sums = jnp.ones((step, 128), F32)
            for pair in range(HEADS // 2):
                lo = pair * 128
                sides = []
                for odd in range(2):
                    head = 2 * pair + odd
                    scores = lax.dot_general(
                        one_head(query_ref[at, lo : lo + 128], odd),
                        key_ref[:, lo : lo + 128],
                        NT,
                        preferred_element_type=F32,
                    )
                    scores = scores * LOG2E + bias_ref[at, :]
                    shift = own[:, head : head + 1]
                    if exact:
                        mine = shift
                        shift = jnp.maximum(jnp.max(scores, axis=1, keepdims=True), mine)
                        self_weight = jnp.exp2(mine - shift).astype(BF16).astype(F32)
                        tops = jnp.where(lane == head, shift, tops)
                    else:
                        self_weight = 1.0
                    weights = jnp.exp2(scores - shift).astype(BF16)
                    part = jnp.dot(weights, val_ref[pair], preferred_element_type=F32)
                    sums = jnp.where(lane == head, part[:, 128:] + self_weight, sums)
                    sides.append(part[:, :128] + self_weight * value_ref[at, lo : lo + 128].astype(F32))
                acc_ref[at, lo : lo + 128] = jnp.where(lane < 64, sides[0], sides[1])
            top_ref[at, :] = tops
            sum_ref[at, :] = sums
            return carry

        lax.fori_loop(0, n // step, body, 0)

    attend(256, False)
    worst = jnp.max(jnp.max(sum_ref[...], axis=0, keepdims=True))

    @pl.when(jnp.logical_not(worst < BIG))
    def _():
        attend(64, True)

    puts = [
        start_copy(top_ref, top_hbm, sems.at[6]),
        start_copy(sum_ref, sum_hbm, sems.at[7]),
        start_copy(acc_ref, acc_hbm, sems.at[8]),
    ]
    for copy in puts:
        copy.wait()


def near_attend(got, w, query, count, own, value):
    n, d = own.shape[0], w.shape[1] // 2
    slots = got.shape[0]
    ins = [(got.shape, BF16), (w.shape, BF16), ((n, d), BF16), ((n, slots), BF16)]
    ins += [(own.shape, F32), ((n, d), BF16)]
    outs = [((n, 128), F32), ((n, 128), F32), ((n, d), F32)]
    return pl.pallas_call(
        near_kernel,
        out_shape=tuple(shape(*o) for o in outs),
        in_specs=[HBM] * 6,
        out_specs=(HBM,) * 3,
        scratch_shapes=[pltpu.VMEM(*v) for v in ins + outs]
        + [
            pltpu.VMEM((slots, d), BF16),
            pltpu.VMEM((HEADS // 2, slots, 256), BF16),
            pltpu.VMEM((n, slots), F32),
            pltpu.SemaphoreType.DMA((9,)),
        ],
        compiler_params=params(FULL),
        cost_estimate=pl.CostEstimate(flops=5 * 10**9, bytes_accessed=5 * 10**6, transcendentals=10**6),
        name="near_attend",
    )(got, w, query, count, own, value)


def disk_kernel(*refs, pieces):
    (start_ref, extent_ref, lifted_hbm), refs = refs[:3], refs[3:]
    piece_hbm, refs = refs[:pieces], refs[pieces:]
    late_hbm, refs = refs[:7], refs[7:]
    out_ref, own_ref, lifted_ref, tok_ref = refs[:4]
    top_ref, sum_ref, near_ref, wd_ref, wout_ref, x_ref = late_refs = refs[4:10]
    shift_ref, acc_ref, den_ref, att_ref, sems, tok_sems = refs[10:]
    own_hbm = late_hbm[0]
    n, d = x_ref.shape
    rows = lifted_ref.shape[0]
    disks, size = piece_hbm[0].shape[:2]

    get_own = start_copy(own_hbm, own_ref, sems.at[0])
    get_lifted = start_copy(lifted_hbm, lifted_ref, sems.at[1])
    here = lax.axis_index("lon")
    sectors = lax.axis_size("lon")

    def seen(disk):
        return lax.rem(here - start_ref[disk] + sectors, sectors) < extent_ref[disk]

    def token_copies(disk):
        return [
            pltpu.make_async_copy(
                piece_hbm[i].at[disk],
                tok_ref.at[disk, pl.ds(i * size, size), :],
                tok_sems.at[disk, i],
            )
            for i in range(pieces)
        ]

    for disk in range(disks):

        @pl.when(seen(disk))
        def _():
            for copy in token_copies(disk):
                copy.start()

    late = [
        start_copy(source, target, sems.at[2 + i])
        for i, (source, target) in enumerate(zip(late_hbm[1:], late_refs))
    ]

    def add_disks(step, unroll, first):
        den_ref[...] = jnp.zeros_like(den_ref)
        acc_ref[...] = jnp.zeros_like(acc_ref)
        if first:
            get_own.wait()
            for head in range(HEADS):
                shift_ref[pl.ds(head * n, n), :] = jnp.broadcast_to(own_ref[:, head : head + 1], (n, 128))
            get_lifted.wait()

        def add_disk(disk, carry):
            @pl.when(seen(disk))
            def _():
                if first:
                    for copy in token_copies(disk):
                        copy.wait()

                def body(i, inner):
                    for u in range(unroll):
                        at = pl.ds(pl.multiple_of((i * unroll + u) * step, step), step)
                        scores = lax.dot_general(
                            lifted_ref[at, :], tok_ref[disk], NT, preferred_element_type=F32
                        )
                        weights = jnp.exp2(scores - shift_ref[at, :1])
                        part = weights[:, :128]
                        for j in range(1, weights.shape[1] // 128):
                            part = part + weights[:, j * 128 : j * 128 + 128]
                        den_ref[at, :] += part
                        acc_ref[at, :] += jnp.dot(
                            weights.astype(BF16), tok_ref[disk], preferred_element_type=F32
                        )
                    return inner

                lax.fori_loop(0, rows // (step * unroll), body, 0)

            return carry

        lax.fori_loop(0, disks, add_disk, 0)

    add_disks(512, 8, True)

    worst = jnp.max(jnp.max(den_ref[...], axis=0, keepdims=True))

    @pl.when(jnp.logical_not(worst < BIG))
    def _():
        def top_disk(disk, carry):
            @pl.when(seen(disk))
            def _():
                def body(i, inner):
                    at = pl.ds(pl.multiple_of(i * 128, 128), 128)
                    scores = lax.dot_general(
                        lifted_ref[at, :], tok_ref[disk], NT, preferred_element_type=F32
                    )
                    best = jnp.max(scores, axis=1, keepdims=True)
                    shift_ref[at, :] = jnp.maximum(shift_ref[at, :], best)
                    return inner

                lax.fori_loop(0, rows // 128, body, 0)

            return carry

        lax.fori_loop(0, disks, top_disk, 0)
        add_disks(128, 1, False)

    for copy in late:
        copy.wait()
    lane = lax.broadcasted_iota(jnp.int32, (n, 128), 1)
    for pair in range(HEADS // 2):
        lo = pair * 128
        sides = []
        for odd in range(2):
            head = 2 * pair + odd
            at = pl.ds(head * n, n)
            shift = shift_ref[at, :1]
            top = top_ref[:, head : head + 1]
            best = jnp.maximum(shift, top)
            disk_scale = jnp.exp2(shift - best)
            near_scale = jnp.exp2(top - best)
            total = (
                jnp.sum(den_ref[at, :], axis=1, keepdims=True) * disk_scale
                + sum_ref[:, head : head + 1] * near_scale
            )
            inv = 1.0 / total
            mixed = (acc_ref[at, :] * (disk_scale * inv)).astype(BF16)
            part = jnp.dot(mixed, wd_ref[:, d + lo : d + lo + 128], preferred_element_type=F32)
            sides.append(part + near_ref[:, lo : lo + 128] * (near_scale * inv))
        att_ref[:, lo : lo + 128] = jnp.where(lane < 64, sides[0], sides[1]).astype(BF16)
    out = jnp.dot(att_ref[...], wout_ref[...], preferred_element_type=F32)
    out_ref[...] = (x_ref[...].astype(F32) + out).astype(BF16)


def disk_attend(start, extent, lifted, pieces, own, top, total, near, wd, wout, x):
    n, d = x.shape
    disks = pieces[0].shape[0]
    tokens = sum(piece.shape[1] for piece in pieces)
    rows, width = HEADS * n, wd.shape[0]
    late = (top, total, near, wd, wout, x)
    return pl.pallas_call(
        functools.partial(disk_kernel, pieces=len(pieces)),
        out_shape=shape((n, d), BF16),
        in_specs=[SMEM, SMEM] + [HBM] * (8 + len(pieces)),
        out_specs=VMEM,
        scratch_shapes=[
            pltpu.VMEM(own.shape, F32),
            pltpu.VMEM((rows, width), BF16),
            pltpu.VMEM((disks, tokens, width), BF16),
        ]
        + [pltpu.VMEM(v.shape, v.dtype) for v in late]
        + [
            pltpu.VMEM((rows, 128), F32),
            pltpu.VMEM((rows, width), F32),
            pltpu.VMEM((rows, 128), F32),
            pltpu.VMEM((n, d), BF16),
            pltpu.SemaphoreType.DMA((8,)),
            pltpu.SemaphoreType.DMA((disks, len(pieces))),
        ],
        compiler_params=params(FULL),
        cost_estimate=pl.CostEstimate(flops=16 * 10**9, bytes_accessed=10**7, transcendentals=10**6),
        name="disk_attend",
    )(start, extent, lifted, *pieces, own, *late)


def device_at(z, y, x, core):
    return (z * 2 + y // 2) * 16 + (y % 2) * 8 + x * 2 + core


def ring(*steps):
    pairs = []
    for z in range(4):
        for y in range(4):
            for x in range(4):
                for core in range(2):
                    axis, by = steps[core]
                    to = [z, y, x]
                    to[axis] = (to[axis] + by) % 4
                    pairs.append((device_at(z, y, x, core), device_at(*to, core)))
    return pairs


def other_core():
    return [(s, s ^ 1) for s in range(128)]


def spread(block, first, second):
    got = []
    for by in (1, 3, 2):
        got.append(lax.ppermute(block, AXES, ring((first, by), (second, by))))
    return got


def gather_tokens(disk_tokens):
    block = jnp.transpose(disk_tokens, (1, 0, 2))
    block = jnp.concatenate([block] + spread(block, 0, 1), axis=1)
    block = lax.optimization_barrier(block)
    block = jnp.concatenate([block] + spread(block, 1, 2), axis=1)
    block = lax.optimization_barrier(block)
    pieces = [block] + spread(block, 2, 0)
    swapped = []
    for piece in pieces:
        swapped.append(lax.ppermute(piece, AXES, other_core()))
    return pieces + swapped


def local(
    mesh_nodes,
    norm_gain,
    w_query,
    w_node_kv,
    obs_rows,
    w_obs_kv,
    obs_owner,
    neighbours,
    neighbour_mask,
    disk_tokens,
    w_disk_kv,
    disk_start,
    disk_extent,
    w_out,
):
    devices = lax.axis_size("lat") * lax.axis_size("lon")
    width = obs_rows.shape[1]
    slots = devices * 8
    send = place(obs_owner.reshape(1, -1), obs_rows, slots)
    got = lax.all_to_all(
        send.reshape(devices, 8, width), AXES, split_axis=0, concat_axis=0, tiled=True
    ).reshape(slots, width)
    query, value, own = node(mesh_nodes, norm_gain.reshape(1, -1), w_query, w_node_kv)
    count = count_listed(neighbours.T, neighbour_mask.T, slots)
    pieces = gather_tokens(disk_tokens)
    top, total, near = near_attend(got, w_obs_kv, query, count, own, value)
    lifted = lift(query, w_disk_kv)
    return disk_attend(
        disk_start, disk_extent, lifted, pieces, own, top, total, near, w_disk_kv, w_out, mesh_nodes
    )


def solution(mesh):
    split = P(AXES, None)
    return jax.shard_map(
        local,
        mesh=mesh,
        in_specs=(
            split,
            P(),
            P(),
            P(),
            split,
            P(),
            split,
            split,
            split,
            P(AXES, None, None),
            P(),
            P(),
            P(),
            P(),
        ),
        out_specs=split,
        check_vma=False,
    )
```

```python
import functools

import jax
import jax.numpy as jnp
from jax import lax
from jax.experimental import pallas as pl
from jax.experimental.pallas import tpu as pltpu
from jax.sharding import PartitionSpec as P


HEADS = 8
AXES = ("lat", "lon")
LOG2E = 1.4426950408889634
EMPTY = 65536.0
NEG = -1e30
BIG = 2.0**100
F32 = jnp.float32
BF16 = jnp.bfloat16
NT = (((1,), (1,)), ((), ()))


def shape(dims, dtype):
    return jax.ShapeDtypeStruct(dims, dtype)


def params(grant=60 * 1024 * 1024):
    return pltpu.CompilerParams(vmem_limit_bytes=grant)


HBM = pl.BlockSpec(memory_space=pltpu.HBM)
VMEM = pl.BlockSpec(memory_space=pltpu.VMEM)
SMEM = pl.BlockSpec(memory_space=pltpu.SMEM)


def start_copy(source, target, sem):
    copy = pltpu.make_async_copy(source, target, sem)
    copy.start()
    return copy


def place_kernel(owner_ref, rows_ref, send_ref, held_ref, sems):
    count = rows_ref.shape[0]
    slots = send_ref.shape[0]
    owners = slots // 8
    owner = owner_ref[...]
    hot = jnp.where(lax.broadcasted_iota(jnp.int32, (owners, count), 0) == owner, 1.0, 0.0)
    row = lax.broadcasted_iota(jnp.int32, (count, count), 0)
    col = lax.broadcasted_iota(jnp.int32, (count, count), 1)
    earlier = jnp.where(row < col, 1.0, 0.0).astype(BF16)
    before = jnp.dot(hot.astype(BF16), earlier, preferred_element_type=F32)
    rank = jnp.sum(before * hot, axis=0, keepdims=True)
    slot = owner * 8 + rank.astype(jnp.int32)
    rows = rows_ref[...]
    ones_rows = jnp.ones((count, 128), BF16)
    step = slots // 4
    copies = []
    for i in range(4):
        at = pl.ds(i * step, step)
        ids_col = lax.broadcasted_iota(jnp.int32, (step, count), 0) + i * step
        placing = jnp.where(ids_col == slot, 1.0, 0.0).astype(BF16)
        placed = jnp.dot(placing, rows, preferred_element_type=F32)
        filled = jnp.dot(placing, ones_rows, preferred_element_type=F32)
        filled = jnp.concatenate([filled, filled], axis=1)
        held_ref[at, :] = jnp.where(filled > 0.5, placed, EMPTY).astype(BF16)
        copies.append(start_copy(held_ref.at[at, :], send_ref.at[at, :], sems.at[i]))
    for copy in copies:
        copy.wait()


def place(owner, rows, slots):
    return pl.pallas_call(
        place_kernel,
        out_shape=shape((slots, rows.shape[1]), BF16),
        in_specs=[VMEM, VMEM],
        out_specs=HBM,
        scratch_shapes=[pltpu.VMEM((slots, rows.shape[1]), BF16), pltpu.SemaphoreType.DMA((4,))],
        compiler_params=params(67043328),
        cost_estimate=pl.CostEstimate(flops=10**9, bytes_accessed=10**6, transcendentals=0),
        name="place",
    )(owner, rows)


def one_head(pair, odd):
    lane = lax.broadcasted_iota(jnp.int32, pair.shape, 1)
    keep = lane >= 64 if odd else lane < 64
    return jnp.where(keep, pair.astype(F32), 0.0).astype(pair.dtype)


def prep_kernel(
    near_ref, mark_ref, x_hbm, gain_ref, wq_hbm, wkv_hbm, wd_hbm, all_hbm, own_hbm,
    x_ref, wq_ref, wkv_ref, wd_ref, all_ref, own_ref, list_ref, sems, out_sems,
):
    n, d = x_ref.shape
    slots = 1024
    get_x = start_copy(x_hbm, x_ref, sems.at[0])
    get_wq = start_copy(wq_hbm, wq_ref, sems.at[1])
    get_wkv = start_copy(wkv_hbm, wkv_ref, sems.at[2])
    get_wd = start_copy(wd_hbm, wd_ref, sems.at[3])
    list_ref[...] = jnp.transpose(jnp.where(mark_ref[...] > 0, near_ref[...], -1), (1, 0))
    step = 64

    def body(i, carry):
        start = pl.multiple_of(i * step, step)
        near = list_ref[pl.ds(start, step), :].astype(jnp.int16)
        ids = lax.broadcasted_iota(jnp.int16, (step, slots), 1)
        total = jnp.zeros((step, slots), jnp.int16)
        one = jnp.ones((step, slots), jnp.int16)
        for entry in range(near.shape[1]):
            total = jnp.where(ids == near[:, entry : entry + 1], total + one, total)
        count = total.astype(F32).astype(BF16)
        for j in range(4):
            at = pl.ds(pl.multiple_of((12 + j) * n + start, step), step)
            all_ref[at, :] = count[:, j * 256 : j * 256 + 256]
        return carry

    lax.fori_loop(0, n // step, body, 0)

    def put(block, blocks, sem):
        at = pl.ds(block * n, blocks * n)
        return start_copy(all_ref.at[at, :], all_hbm.at[at, :], out_sems.at[sem])

    puts = [put(12, 4, 0)]
    get_x.wait()
    x = x_ref[...].astype(F32)
    inverse = lax.rsqrt(jnp.mean(x * x, axis=1, keepdims=True) + 1e-06)
    normed = (x * inverse * gain_ref[...]).astype(BF16)
    get_wq.wait()
    query = (jnp.dot(normed, wq_ref[...], preferred_element_type=F32) * 0.125).astype(BF16)
    get_wkv.wait()
    kv = jnp.dot(normed, wkv_ref[...], preferred_element_type=F32).astype(BF16)
    for j in range(2):
        all_ref[pl.ds((8 + j) * n, n), :] = query[:, j * 256 : j * 256 + 256]
        all_ref[pl.ds((10 + j) * n, n), :] = kv[:, d + j * 256 : d + j * 256 + 256]
    puts.append(put(8, 4, 1))
    prod = query.astype(F32) * kv[:, :d].astype(F32)
    lane = lax.broadcasted_iota(jnp.int32, (n, 128), 1)
    own = jnp.zeros((n, 128), F32)
    get_wd.wait()
    for head in range(HEADS):
        lo = head // 2 * 128
        part = jnp.sum(prod[:, head * 64 : head * 64 + 64], axis=1, keepdims=True) * LOG2E
        own = jnp.where(lane == head, part, own)
        lifted = lax.dot_general(
            one_head(query[:, lo : lo + 128], head % 2),
            wd_ref[:, lo : lo + 128],
            NT,
            preferred_element_type=F32,
        )
        all_ref[pl.ds(head * n, n), :] = (lifted * LOG2E).astype(BF16)
        puts.append(put(head, 1, 2 + head))
    own_ref[...] = own
    puts.append(start_copy(own_ref, own_hbm, out_sems.at[2 + HEADS]))
    for copy in puts:
        copy.wait()


def prep(near, mark, x, gain, wq, wkv, wd):
    n, _ = x.shape
    outs = [((16 * n, 256), BF16), ((n, 128), F32)]
    ins = [(v.shape, v.dtype) for v in (x, wq, wkv, wd)]
    return pl.pallas_call(
        prep_kernel,
        out_shape=tuple(shape(*o) for o in outs),
        in_specs=[VMEM, VMEM, HBM, VMEM, HBM, HBM, HBM],
        out_specs=(HBM,) * 2,
        scratch_shapes=[pltpu.VMEM(*v) for v in ins + outs]
        + [
            pltpu.VMEM(near.shape[::-1], jnp.int32),
            pltpu.SemaphoreType.DMA((4,)),
            pltpu.SemaphoreType.DMA((3 + HEADS,)),
        ],
        compiler_params=params(),
        cost_estimate=pl.CostEstimate(flops=8 * 10**9, bytes_accessed=8 * 10**6, transcendentals=0),
        name="prep",
    )(near, mark, x, gain, wq, wkv, wd)


def near_kernel(
    got_hbm, w_hbm, all_hbm, own_hbm, top_hbm, sum_hbm, acc_hbm,
    got_ref, w_ref, query_ref, count_ref, own_ref, value_ref, top_ref, sum_ref, acc_ref,
    key_ref, val_ref, bias_ref, sems,
):
    slots = got_ref.shape[0]
    n, d = query_ref.shape
    get_got = start_copy(got_hbm, got_ref, sems.at[0])
    get_w = start_copy(w_hbm, w_ref, sems.at[1])

    def get_block(block, target, j, sem):
        return start_copy(
            all_hbm.at[pl.ds(block * n, n), :], target.at[:, pl.ds(j * 256, 256)], sems.at[sem]
        )

    get_got.wait()
    get_count = [get_block(12 + j, count_ref, j, 8 + j) for j in range(4)]
    gets = [get_block(8 + j, query_ref, j, 2 + j) for j in range(2)]
    gets += [get_block(10 + j, value_ref, j, 4 + j) for j in range(2)]
    gets.append(start_copy(own_hbm, own_ref, sems.at[6]))
    got = got_ref[...]
    absent = got.astype(F32) > 1024.0
    rows = jnp.where(absent, 0.0, got.astype(F32)).astype(BF16)
    ones = jnp.ones((8, 128), BF16)
    empty = lax.dot_general(
        ones, jnp.where(absent[:, :128], 1.0, 0.0).astype(BF16), NT, preferred_element_type=F32
    )[0:1, :]
    get_w.wait()
    kv = jnp.dot(rows, w_ref[...], preferred_element_type=F32).astype(BF16)
    key_ref[...] = kv[:, :d]
    for pair in range(HEADS // 2):
        lo = d + pair * 128
        val_ref[pair, :, :128] = kv[:, lo : lo + 128]
        val_ref[pair, :, 128:] = jnp.ones((slots, 128), BF16)
    for copy in get_count:
        copy.wait()
    count = count_ref[...].astype(F32)
    bias_ref[...] = jnp.where((count > 0.0) & (empty < 0.5), jnp.log2(jnp.maximum(count, 1.0)), NEG)
    for copy in gets:
        copy.wait()

    def attend(step, exact):
        lane = lax.broadcasted_iota(jnp.int32, (step, 128), 1)

        def body(i, carry):
            at = pl.ds(pl.multiple_of(i * step, step), step)
            own = own_ref[at, :]
            tops = own
            sums = jnp.ones((step, 128), F32)
            for pair in range(HEADS // 2):
                lo = pair * 128
                sides = []
                for odd in range(2):
                    head = 2 * pair + odd
                    scores = lax.dot_general(
                        one_head(query_ref[at, lo : lo + 128], odd),
                        key_ref[:, lo : lo + 128],
                        NT,
                        preferred_element_type=F32,
                    )
                    scores = scores * LOG2E + bias_ref[at, :]
                    shift = own[:, head : head + 1]
                    if exact:
                        mine = shift
                        shift = jnp.maximum(jnp.max(scores, axis=1, keepdims=True), mine)
                        self_weight = jnp.exp2(mine - shift).astype(BF16).astype(F32)
                        tops = jnp.where(lane == head, shift, tops)
                    else:
                        self_weight = 1.0
                    weights = jnp.exp2(scores - shift).astype(BF16)
                    part = jnp.dot(weights, val_ref[pair], preferred_element_type=F32)
                    sums = jnp.where(lane == head, part[:, 128:] + self_weight, sums)
                    sides.append(part[:, :128] + self_weight * value_ref[at, lo : lo + 128].astype(F32))
                acc_ref[at, lo : lo + 128] = jnp.where(lane < 64, sides[0], sides[1])
            top_ref[at, :] = tops
            sum_ref[at, :] = sums
            return carry

        lax.fori_loop(0, n // step, body, 0)

    attend(256, False)
    worst = jnp.max(jnp.max(sum_ref[...], axis=0, keepdims=True))

    @pl.when(jnp.logical_not(worst < BIG))
    def _():
        attend(64, True)

    puts = [
        start_copy(top_ref, top_hbm, sems.at[12]),
        start_copy(sum_ref, sum_hbm, sems.at[13]),
        start_copy(acc_ref, acc_hbm, sems.at[14]),
    ]
    for copy in puts:
        copy.wait()


def near_attend(got, w, everything, own):
    n, d = own.shape[0], w.shape[1] // 2
    slots = got.shape[0]
    ins = [(got.shape, BF16), (w.shape, BF16), ((n, d), BF16), ((n, slots), BF16)]
    ins += [(own.shape, F32), ((n, d), BF16)]
    outs = [((n, 128), F32), ((n, 128), F32), ((n, d), F32)]
    return pl.pallas_call(
        near_kernel,
        out_shape=tuple(shape(*o) for o in outs),
        in_specs=[HBM] * 4,
        out_specs=(HBM,) * 3,
        scratch_shapes=[pltpu.VMEM(*v) for v in ins + outs]
        + [
            pltpu.VMEM((slots, d), BF16),
            pltpu.VMEM((HEADS // 2, slots, 256), BF16),
            pltpu.VMEM((n, slots), F32),
            pltpu.SemaphoreType.DMA((15,)),
        ],
        compiler_params=params(67043328),
        cost_estimate=pl.CostEstimate(flops=5 * 10**9, bytes_accessed=5 * 10**6, transcendentals=10**6),
        name="near_attend",
    )(got, w, everything, own)


def disk_kernel(*refs, pieces):
    (start_ref, extent_ref, lifted_hbm), refs = refs[:3], refs[3:]
    piece_hbm, refs = refs[:pieces], refs[pieces:]
    late_hbm, refs = refs[:7], refs[7:]
    out_ref, own_ref, lifted_ref, tok_ref = refs[:4]
    top_ref, sum_ref, near_ref, wd_ref, wout_ref, x_ref = late_refs = refs[4:10]
    shift_ref, acc_ref, den_ref, att_ref, sems, tok_sems = refs[10:]
    own_hbm = late_hbm[0]
    n, d = x_ref.shape
    rows = lifted_ref.shape[0]
    disks, size = piece_hbm[0].shape[:2]

    get_own = start_copy(own_hbm, own_ref, sems.at[0])
    get_lifted = start_copy(lifted_hbm.at[pl.ds(0, rows), :], lifted_ref, sems.at[1])
    here = lax.axis_index("lon")
    sectors = lax.axis_size("lon")

    def seen(disk):
        return lax.rem(here - start_ref[disk] + sectors, sectors) < extent_ref[disk]

    def token_copies(disk):
        return [
            pltpu.make_async_copy(
                piece_hbm[i].at[disk],
                tok_ref.at[disk, pl.ds(i * size, size), :],
                tok_sems.at[disk, i],
            )
            for i in range(pieces)
        ]

    for disk in range(disks):

        @pl.when(seen(disk))
        def _():
            for copy in token_copies(disk):
                copy.start()

    late = [
        start_copy(source, target, sems.at[2 + i])
        for i, (source, target) in enumerate(zip(late_hbm[1:], late_refs))
    ]

    def add_disks(step, unroll, first):
        den_ref[...] = jnp.zeros_like(den_ref)
        acc_ref[...] = jnp.zeros_like(acc_ref)
        if first:
            get_own.wait()
            for head in range(HEADS):
                shift_ref[pl.ds(head * n, n), :] = jnp.broadcast_to(own_ref[:, head : head + 1], (n, 128))
            get_lifted.wait()

        def add_disk(disk, carry):
            @pl.when(seen(disk))
            def _():
                if first:
                    for copy in token_copies(disk):
                        copy.wait()

                def body(i, inner):
                    for u in range(unroll):
                        at = pl.ds(pl.multiple_of((i * unroll + u) * step, step), step)
                        scores = lax.dot_general(
                            lifted_ref[at, :], tok_ref[disk], NT, preferred_element_type=F32
                        )
                        weights = jnp.exp2(scores - shift_ref[at, :1])
                        part = weights[:, :128]
                        for j in range(1, weights.shape[1] // 128):
                            part = part + weights[:, j * 128 : j * 128 + 128]
                        den_ref[at, :] += part
                        acc_ref[at, :] += jnp.dot(
                            weights.astype(BF16), tok_ref[disk], preferred_element_type=F32
                        )
                    return inner

                lax.fori_loop(0, rows // (step * unroll), body, 0)

            return carry

        lax.fori_loop(0, disks, add_disk, 0)

    add_disks(512, 8, True)

    worst = jnp.max(jnp.max(den_ref[...], axis=0, keepdims=True))

    @pl.when(jnp.logical_not(worst < BIG))
    def _():
        def top_disk(disk, carry):
            @pl.when(seen(disk))
            def _():
                def body(i, inner):
                    at = pl.ds(pl.multiple_of(i * 128, 128), 128)
                    scores = lax.dot_general(
                        lifted_ref[at, :], tok_ref[disk], NT, preferred_element_type=F32
                    )
                    best = jnp.max(scores, axis=1, keepdims=True)
                    shift_ref[at, :] = jnp.maximum(shift_ref[at, :], best)
                    return inner

                lax.fori_loop(0, rows // 128, body, 0)

            return carry

        lax.fori_loop(0, disks, top_disk, 0)
        add_disks(128, 1, False)

    for copy in late:
        copy.wait()
    lane = lax.broadcasted_iota(jnp.int32, (n, 128), 1)
    for pair in range(HEADS // 2):
        lo = pair * 128
        sides = []
        for odd in range(2):
            head = 2 * pair + odd
            at = pl.ds(head * n, n)
            shift = shift_ref[at, :1]
            top = top_ref[:, head : head + 1]
            best = jnp.maximum(shift, top)
            disk_scale = jnp.exp2(shift - best)
            near_scale = jnp.exp2(top - best)
            total = (
                jnp.sum(den_ref[at, :], axis=1, keepdims=True) * disk_scale
                + sum_ref[:, head : head + 1] * near_scale
            )
            inv = 1.0 / total
            mixed = (acc_ref[at, :] * (disk_scale * inv)).astype(BF16)
            part = jnp.dot(mixed, wd_ref[:, d + lo : d + lo + 128], preferred_element_type=F32)
            sides.append(part + near_ref[:, lo : lo + 128] * (near_scale * inv))
        att_ref[:, lo : lo + 128] = jnp.where(lane < 64, sides[0], sides[1]).astype(BF16)
    out = jnp.dot(att_ref[...], wout_ref[...], preferred_element_type=F32)
    out_ref[...] = (x_ref[...].astype(F32) + out).astype(BF16)


def disk_attend(start, extent, everything, pieces, own, top, total, near, wd, wout, x):
    n, d = x.shape
    disks = pieces[0].shape[0]
    tokens = sum(piece.shape[1] for piece in pieces)
    rows, width = HEADS * n, wd.shape[0]
    late = (top, total, near, wd, wout, x)
    return pl.pallas_call(
        functools.partial(disk_kernel, pieces=len(pieces)),
        out_shape=shape((n, d), BF16),
        in_specs=[SMEM, SMEM] + [HBM] * (8 + len(pieces)),
        out_specs=VMEM,
        scratch_shapes=[
            pltpu.VMEM(own.shape, F32),
            pltpu.VMEM((rows, width), BF16),
            pltpu.VMEM((disks, tokens, width), BF16),
        ]
        + [pltpu.VMEM(v.shape, v.dtype) for v in late]
        + [
            pltpu.VMEM((rows, 128), F32),
            pltpu.VMEM((rows, width), F32),
            pltpu.VMEM((rows, 128), F32),
            pltpu.VMEM((n, d), BF16),
            pltpu.SemaphoreType.DMA((8,)),
            pltpu.SemaphoreType.DMA((disks, len(pieces))),
        ],
        compiler_params=params(67043328),
        cost_estimate=pl.CostEstimate(flops=16 * 10**9, bytes_accessed=10**7, transcendentals=10**6),
        name="disk_attend",
    )(start, extent, everything, *pieces, own, *late)


def device_at(z, y, x, core):
    return (z * 2 + y // 2) * 16 + (y % 2) * 8 + x * 2 + core


def ring(*steps):
    pairs = []
    for z in range(4):
        for y in range(4):
            for x in range(4):
                for core in range(2):
                    axis, by = steps[core]
                    to = [z, y, x]
                    to[axis] = (to[axis] + by) % 4
                    pairs.append((device_at(z, y, x, core), device_at(*to, core)))
    return pairs


def other_core():
    return [(s, s ^ 1) for s in range(128)]


def spread(block, first, second):
    got = []
    for by in (1, 3, 2):
        got.append(lax.ppermute(block, AXES, ring((first, by), (second, by))))
    return got


def planes():
    groups = []
    for core in range(2):
        for fixed in range(4):
            group = []
            for a in range(4):
                for b in range(4):
                    at = (a, b, fixed) if core == 0 else (fixed, a, b)
                    group.append(device_at(*at, core))
            groups.append(group)
    return groups


def gather_tokens(disk_tokens):
    block = jnp.transpose(disk_tokens, (1, 0, 2))
    disks, size, width = block.shape
    block = lax.all_to_all(
        jnp.broadcast_to(block, (16, disks, size, width)),
        AXES,
        split_axis=0,
        concat_axis=0,
        tiled=True,
        axis_index_groups=planes(),
    )
    block = jnp.transpose(block, (1, 0, 2, 3)).reshape(disks, 16 * size, width)
    pieces = [block] + spread(block, 2, 0)
    swapped = []
    for piece in pieces:
        swapped.append(lax.ppermute(piece, AXES, other_core()))
    return pieces + swapped


def local(
    mesh_nodes,
    norm_gain,
    w_query,
    w_node_kv,
    obs_rows,
    w_obs_kv,
    obs_owner,
    neighbours,
    neighbour_mask,
    disk_tokens,
    w_disk_kv,
    disk_start,
    disk_extent,
    w_out,
):
    devices = lax.axis_size("lat") * lax.axis_size("lon")
    width = obs_rows.shape[1]
    slots = devices * 8
    send = place(obs_owner.reshape(1, -1), obs_rows, slots)
    got = lax.all_to_all(
        send.reshape(devices, 8, width), AXES, split_axis=0, concat_axis=0, tiled=True
    ).reshape(slots, width)
    everything, own = prep(
        neighbours.T,
        neighbour_mask.T,
        mesh_nodes,
        norm_gain.reshape(1, -1),
        w_query,
        w_node_kv,
        w_disk_kv,
    )
    pieces = gather_tokens(disk_tokens)
    top, total, near = near_attend(got, w_obs_kv, everything, own)
    return disk_attend(
        disk_start, disk_extent, everything, pieces, own, top, total, near, w_disk_kv, w_out, mesh_nodes
    )


def solution(mesh):
    split = P(AXES, None)
    return jax.shard_map(
        local,
        mesh=mesh,
        in_specs=(
            split,
            P(),
            P(),
            P(),
            split,
            P(),
            split,
            split,
            split,
            P(AXES, None, None),
            P(),
            P(),
            P(),
            P(),
        ),
        out_specs=split,
        check_vma=False,
    )
```

```python
import functools

import jax
import jax.numpy as jnp
from jax import lax
from jax.experimental import pallas as pl
from jax.experimental.pallas import tpu as pltpu
from jax.sharding import PartitionSpec as P


HEADS = 8
AXES = ("lat", "lon")
LOG2E = 1.4426950408889634
EMPTY = 65536.0
NEG = -1e30
BIG = 2.0**100
F32 = jnp.float32
BF16 = jnp.bfloat16
NT = (((1,), (1,)), ((), ()))


def shape(dims, dtype):
    return jax.ShapeDtypeStruct(dims, dtype)


def params(grant=60 * 1024 * 1024):
    return pltpu.CompilerParams(vmem_limit_bytes=grant)


HBM = pl.BlockSpec(memory_space=pltpu.HBM)
VMEM = pl.BlockSpec(memory_space=pltpu.VMEM)
SMEM = pl.BlockSpec(memory_space=pltpu.SMEM)


def start_copy(source, target, sem):
    copy = pltpu.make_async_copy(source, target, sem)
    copy.start()
    return copy


def place_kernel(owner_ref, rows_ref, send_ref, held_ref, sems):
    count = rows_ref.shape[0]
    slots = send_ref.shape[0]
    owners = slots // 8
    owner = owner_ref[...]
    hot = jnp.where(lax.broadcasted_iota(jnp.int32, (owners, count), 0) == owner, 1.0, 0.0)
    row = lax.broadcasted_iota(jnp.int32, (count, count), 0)
    col = lax.broadcasted_iota(jnp.int32, (count, count), 1)
    earlier = jnp.where(row < col, 1.0, 0.0).astype(BF16)
    before = jnp.dot(hot.astype(BF16), earlier, preferred_element_type=F32)
    rank = jnp.sum(before * hot, axis=0, keepdims=True)
    slot = owner * 8 + rank.astype(jnp.int32)
    rows = rows_ref[...]
    ones_rows = jnp.ones((count, 128), BF16)
    step = slots // 4
    copies = []
    for i in range(4):
        at = pl.ds(i * step, step)
        ids_col = lax.broadcasted_iota(jnp.int32, (step, count), 0) + i * step
        placing = jnp.where(ids_col == slot, 1.0, 0.0).astype(BF16)
        placed = jnp.dot(placing, rows, preferred_element_type=F32)
        filled = jnp.dot(placing, ones_rows, preferred_element_type=F32)
        filled = jnp.concatenate([filled, filled], axis=1)
        held_ref[at, :] = jnp.where(filled > 0.5, placed, EMPTY).astype(BF16)
        copies.append(start_copy(held_ref.at[at, :], send_ref.at[at, :], sems.at[i]))
    for copy in copies:
        copy.wait()


def place(owner, rows, slots):
    return pl.pallas_call(
        place_kernel,
        out_shape=shape((slots, rows.shape[1]), BF16),
        in_specs=[VMEM, VMEM],
        out_specs=HBM,
        scratch_shapes=[pltpu.VMEM((slots, rows.shape[1]), BF16), pltpu.SemaphoreType.DMA((4,))],
        compiler_params=params(67043328),
        cost_estimate=pl.CostEstimate(flops=10**9, bytes_accessed=10**6, transcendentals=0),
        name="place",
    )(owner, rows)


def one_head(pair, odd):
    lane = lax.broadcasted_iota(jnp.int32, pair.shape, 1)
    keep = lane >= 64 if odd else lane < 64
    return jnp.where(keep, pair.astype(F32), 0.0).astype(pair.dtype)


def prep_kernel(
    near_ref, mark_ref, x_hbm, gain_ref, wq_hbm, wkv_hbm, wd_hbm, all_hbm, own_hbm,
    x_ref, wq_ref, wkv_ref, wd_ref, all_ref, own_ref, list_ref, sems, out_sems,
):
    n, d = x_ref.shape
    slots = 1024
    get_x = start_copy(x_hbm, x_ref, sems.at[0])
    get_wq = start_copy(wq_hbm, wq_ref, sems.at[1])
    get_wkv = start_copy(wkv_hbm, wkv_ref, sems.at[2])
    get_wd = start_copy(wd_hbm, wd_ref, sems.at[3])
    list_ref[...] = jnp.transpose(jnp.where(mark_ref[...] > 0, near_ref[...], -1), (1, 0))
    step = 64

    def body(i, carry):
        start = pl.multiple_of(i * step, step)
        near = list_ref[pl.ds(start, step), :].astype(jnp.int16)
        ids = lax.broadcasted_iota(jnp.int16, (step, slots), 1)
        total = jnp.zeros((step, slots), jnp.int16)
        one = jnp.ones((step, slots), jnp.int16)
        for entry in range(near.shape[1]):
            total = jnp.where(ids == near[:, entry : entry + 1], total + one, total)
        count = total.astype(F32).astype(BF16)
        for j in range(4):
            at = pl.ds(pl.multiple_of((12 + j) * n + start, step), step)
            all_ref[at, :] = count[:, j * 256 : j * 256 + 256]
        return carry

    lax.fori_loop(0, n // step, body, 0)

    def put(block, blocks, sem):
        at = pl.ds(block * n, blocks * n)
        return start_copy(all_ref.at[at, :], all_hbm.at[at, :], out_sems.at[sem])

    puts = [put(12, 4, 0)]
    get_x.wait()
    x = x_ref[...].astype(F32)
    inverse = lax.rsqrt(jnp.mean(x * x, axis=1, keepdims=True) + 1e-06)
    normed = (x * inverse * gain_ref[...]).astype(BF16)
    get_wq.wait()
    query = (jnp.dot(normed, wq_ref[...], preferred_element_type=F32) * 0.125).astype(BF16)
    get_wkv.wait()
    kv = jnp.dot(normed, wkv_ref[...], preferred_element_type=F32).astype(BF16)
    for j in range(2):
        all_ref[pl.ds((8 + j) * n, n), :] = query[:, j * 256 : j * 256 + 256]
        all_ref[pl.ds((10 + j) * n, n), :] = kv[:, d + j * 256 : d + j * 256 + 256]
    puts.append(put(8, 4, 1))
    prod = query.astype(F32) * kv[:, :d].astype(F32)
    lane = lax.broadcasted_iota(jnp.int32, (n, 128), 1)
    own = jnp.zeros((n, 128), F32)
    get_wd.wait()
    for head in range(HEADS):
        lo = head // 2 * 128
        part = jnp.sum(prod[:, head * 64 : head * 64 + 64], axis=1, keepdims=True) * LOG2E
        own = jnp.where(lane == head, part, own)
        lifted = lax.dot_general(
            one_head(query[:, lo : lo + 128], head % 2),
            wd_ref[:, lo : lo + 128],
            NT,
            preferred_element_type=F32,
        )
        all_ref[pl.ds(head * n, n), :] = (lifted * LOG2E).astype(BF16)
        puts.append(put(head, 1, 2 + head))
    own_ref[...] = own
    puts.append(start_copy(own_ref, own_hbm, out_sems.at[2 + HEADS]))
    for copy in puts:
        copy.wait()


def prep(near, mark, x, gain, wq, wkv, wd):
    n, _ = x.shape
    outs = [((16 * n, 256), BF16), ((n, 128), F32)]
    ins = [(v.shape, v.dtype) for v in (x, wq, wkv, wd)]
    return pl.pallas_call(
        prep_kernel,
        out_shape=tuple(shape(*o) for o in outs),
        in_specs=[VMEM, VMEM, HBM, VMEM, HBM, HBM, HBM],
        out_specs=(HBM,) * 2,
        scratch_shapes=[pltpu.VMEM(*v) for v in ins + outs]
        + [
            pltpu.VMEM(near.shape[::-1], jnp.int32),
            pltpu.SemaphoreType.DMA((4,)),
            pltpu.SemaphoreType.DMA((3 + HEADS,)),
        ],
        compiler_params=params(),
        cost_estimate=pl.CostEstimate(flops=8 * 10**9, bytes_accessed=8 * 10**6, transcendentals=0),
        name="prep",
    )(near, mark, x, gain, wq, wkv, wd)


def near_kernel(
    got_hbm, w_hbm, all_hbm, own_hbm, top_hbm, sum_hbm, acc_hbm,
    got_ref, w_ref, query_ref, count_ref, own_ref, value_ref, top_ref, sum_ref, acc_ref,
    key_ref, val_ref, bias_ref, sems,
):
    slots = got_ref.shape[0]
    n, d = query_ref.shape
    get_got = start_copy(got_hbm, got_ref, sems.at[0])
    get_w = start_copy(w_hbm, w_ref, sems.at[1])

    def get_block(block, target, j, sem):
        return start_copy(
            all_hbm.at[pl.ds(block * n, n), :], target.at[:, pl.ds(j * 256, 256)], sems.at[sem]
        )

    get_got.wait()
    get_count = [get_block(12 + j, count_ref, j, 8 + j) for j in range(4)]
    gets = [get_block(8 + j, query_ref, j, 2 + j) for j in range(2)]
    gets += [get_block(10 + j, value_ref, j, 4 + j) for j in range(2)]
    gets.append(start_copy(own_hbm, own_ref, sems.at[6]))
    got = got_ref[...]
    absent = got.astype(F32) > 1024.0
    rows = jnp.where(absent, 0.0, got.astype(F32)).astype(BF16)
    ones = jnp.ones((8, 128), BF16)
    empty = lax.dot_general(
        ones, jnp.where(absent[:, :128], 1.0, 0.0).astype(BF16), NT, preferred_element_type=F32
    )[0:1, :]
    get_w.wait()
    kv = jnp.dot(rows, w_ref[...], preferred_element_type=F32).astype(BF16)
    key_ref[...] = kv[:, :d]
    for pair in range(HEADS // 2):
        lo = d + pair * 128
        val_ref[pair, :, :128] = kv[:, lo : lo + 128]
        val_ref[pair, :, 128:] = jnp.ones((slots, 128), BF16)
    for copy in get_count:
        copy.wait()
    count = count_ref[...].astype(F32)
    bias_ref[...] = jnp.where((count > 0.0) & (empty < 0.5), jnp.log2(jnp.maximum(count, 1.0)), NEG)
    for copy in gets:
        copy.wait()

    def attend(step, exact):
        lane = lax.broadcasted_iota(jnp.int32, (step, 128), 1)

        def body(i, carry):
            at = pl.ds(pl.multiple_of(i * step, step), step)
            own = own_ref[at, :]
            tops = own
            sums = jnp.ones((step, 128), F32)
            for pair in range(HEADS // 2):
                lo = pair * 128
                sides = []
                for odd in range(2):
                    head = 2 * pair + odd
                    scores = lax.dot_general(
                        one_head(query_ref[at, lo : lo + 128], odd),
                        key_ref[:, lo : lo + 128],
                        NT,
                        preferred_element_type=F32,
                    )
                    scores = scores * LOG2E + bias_ref[at, :]
                    shift = own[:, head : head + 1]
                    if exact:
                        mine = shift
                        shift = jnp.maximum(jnp.max(scores, axis=1, keepdims=True), mine)
                        self_weight = jnp.exp2(mine - shift).astype(BF16).astype(F32)
                        tops = jnp.where(lane == head, shift, tops)
                    else:
                        self_weight = 1.0
                    weights = jnp.exp2(scores - shift).astype(BF16)
                    part = jnp.dot(weights, val_ref[pair], preferred_element_type=F32)
                    sums = jnp.where(lane == head, part[:, 128:] + self_weight, sums)
                    sides.append(part[:, :128] + self_weight * value_ref[at, lo : lo + 128].astype(F32))
                acc_ref[at, lo : lo + 128] = jnp.where(lane < 64, sides[0], sides[1])
            top_ref[at, :] = tops
            sum_ref[at, :] = sums
            return carry

        lax.fori_loop(0, n // step, body, 0)

    attend(256, False)
    worst = jnp.max(jnp.max(sum_ref[...], axis=0, keepdims=True))

    @pl.when(jnp.logical_not(worst < BIG))
    def _():
        attend(64, True)

    puts = [
        start_copy(top_ref, top_hbm, sems.at[12]),
        start_copy(sum_ref, sum_hbm, sems.at[13]),
        start_copy(acc_ref, acc_hbm, sems.at[14]),
    ]
    for copy in puts:
        copy.wait()


def near_attend(got, w, everything, own):
    n, d = own.shape[0], w.shape[1] // 2
    slots = got.shape[0]
    ins = [(got.shape, BF16), (w.shape, BF16), ((n, d), BF16), ((n, slots), BF16)]
    ins += [(own.shape, F32), ((n, d), BF16)]
    outs = [((n, 128), F32), ((n, 128), F32), ((n, d), F32)]
    return pl.pallas_call(
        near_kernel,
        out_shape=tuple(shape(*o) for o in outs),
        in_specs=[HBM] * 4,
        out_specs=(HBM,) * 3,
        scratch_shapes=[pltpu.VMEM(*v) for v in ins + outs]
        + [
            pltpu.VMEM((slots, d), BF16),
            pltpu.VMEM((HEADS // 2, slots, 256), BF16),
            pltpu.VMEM((n, slots), F32),
            pltpu.SemaphoreType.DMA((15,)),
        ],
        compiler_params=params(67043328),
        cost_estimate=pl.CostEstimate(flops=5 * 10**9, bytes_accessed=5 * 10**6, transcendentals=10**6),
        name="near_attend",
    )(got, w, everything, own)


def disk_kernel(*refs, pieces):
    (start_ref, extent_ref, lifted_hbm), refs = refs[:3], refs[3:]
    piece_hbm, refs = refs[:pieces], refs[pieces:]
    late_hbm, refs = refs[:7], refs[7:]
    out_ref, own_ref, lifted_ref, tok_ref = refs[:4]
    top_ref, sum_ref, near_ref, wd_ref, wout_ref, x_ref = late_refs = refs[4:10]
    shift_ref, acc_ref, den_ref, att_ref, sems, tok_sems = refs[10:]
    own_hbm = late_hbm[0]
    n, d = x_ref.shape
    rows = lifted_ref.shape[0]
    disks, size = piece_hbm[0].shape[:2]

    get_own = start_copy(own_hbm, own_ref, sems.at[0])
    get_lifted = start_copy(lifted_hbm.at[pl.ds(0, rows), :], lifted_ref, sems.at[1])
    here = lax.axis_index("lon")
    sectors = lax.axis_size("lon")

    def seen(disk):
        return lax.rem(here - start_ref[disk] + sectors, sectors) < extent_ref[disk]

    def token_copies(disk):
        return [
            pltpu.make_async_copy(
                piece_hbm[i].at[disk],
                tok_ref.at[disk, pl.ds(i * size, size), :],
                tok_sems.at[disk, i],
            )
            for i in range(pieces)
        ]

    for disk in range(disks):

        @pl.when(seen(disk))
        def _():
            for copy in token_copies(disk):
                copy.start()

    late = [
        start_copy(source, target, sems.at[2 + i])
        for i, (source, target) in enumerate(zip(late_hbm[1:], late_refs))
    ]

    def add_disks(step, unroll, first):
        den_ref[...] = jnp.zeros_like(den_ref)
        acc_ref[...] = jnp.zeros_like(acc_ref)
        if first:
            get_own.wait()
            for head in range(HEADS):
                shift_ref[pl.ds(head * n, n), :] = jnp.broadcast_to(own_ref[:, head : head + 1], (n, 128))
            get_lifted.wait()

        def add_disk(disk, carry):
            @pl.when(seen(disk))
            def _():
                if first:
                    for copy in token_copies(disk):
                        copy.wait()

                def body(i, inner):
                    for u in range(unroll):
                        at = pl.ds(pl.multiple_of((i * unroll + u) * step, step), step)
                        scores = lax.dot_general(
                            lifted_ref[at, :], tok_ref[disk], NT, preferred_element_type=F32
                        )
                        weights = jnp.exp2(scores - shift_ref[at, :1])
                        part = weights[:, :128]
                        for j in range(1, weights.shape[1] // 128):
                            part = part + weights[:, j * 128 : j * 128 + 128]
                        den_ref[at, :] += part
                        acc_ref[at, :] += jnp.dot(
                            weights.astype(BF16), tok_ref[disk], preferred_element_type=F32
                        )
                    return inner

                lax.fori_loop(0, rows // (step * unroll), body, 0)

            return carry

        lax.fori_loop(0, disks, add_disk, 0)

    add_disks(512, 8, True)

    worst = jnp.max(jnp.max(den_ref[...], axis=0, keepdims=True))

    @pl.when(jnp.logical_not(worst < BIG))
    def _():
        def top_disk(disk, carry):
            @pl.when(seen(disk))
            def _():
                def body(i, inner):
                    at = pl.ds(pl.multiple_of(i * 128, 128), 128)
                    scores = lax.dot_general(
                        lifted_ref[at, :], tok_ref[disk], NT, preferred_element_type=F32
                    )
                    best = jnp.max(scores, axis=1, keepdims=True)
                    shift_ref[at, :] = jnp.maximum(shift_ref[at, :], best)
                    return inner

                lax.fori_loop(0, rows // 128, body, 0)

            return carry

        lax.fori_loop(0, disks, top_disk, 0)
        add_disks(128, 1, False)

    for copy in late:
        copy.wait()
    lane = lax.broadcasted_iota(jnp.int32, (n, 128), 1)
    for pair in range(HEADS // 2):
        lo = pair * 128
        sides = []
        for odd in range(2):
            head = 2 * pair + odd
            at = pl.ds(head * n, n)
            shift = shift_ref[at, :1]
            top = top_ref[:, head : head + 1]
            best = jnp.maximum(shift, top)
            disk_scale = jnp.exp2(shift - best)
            near_scale = jnp.exp2(top - best)
            total = (
                jnp.sum(den_ref[at, :], axis=1, keepdims=True) * disk_scale
                + sum_ref[:, head : head + 1] * near_scale
            )
            inv = 1.0 / total
            mixed = (acc_ref[at, :] * (disk_scale * inv)).astype(BF16)
            part = jnp.dot(mixed, wd_ref[:, d + lo : d + lo + 128], preferred_element_type=F32)
            sides.append(part + near_ref[:, lo : lo + 128] * (near_scale * inv))
        att_ref[:, lo : lo + 128] = jnp.where(lane < 64, sides[0], sides[1]).astype(BF16)
    out = jnp.dot(att_ref[...], wout_ref[...], preferred_element_type=F32)
    out_ref[...] = (x_ref[...].astype(F32) + out).astype(BF16)


def disk_attend(start, extent, everything, pieces, own, top, total, near, wd, wout, x):
    n, d = x.shape
    disks = pieces[0].shape[0]
    tokens = sum(piece.shape[1] for piece in pieces)
    rows, width = HEADS * n, wd.shape[0]
    late = (top, total, near, wd, wout, x)
    return pl.pallas_call(
        functools.partial(disk_kernel, pieces=len(pieces)),
        out_shape=shape((n, d), BF16),
        in_specs=[SMEM, SMEM] + [HBM] * (8 + len(pieces)),
        out_specs=VMEM,
        scratch_shapes=[
            pltpu.VMEM(own.shape, F32),
            pltpu.VMEM((rows, width), BF16),
            pltpu.VMEM((disks, tokens, width), BF16),
        ]
        + [pltpu.VMEM(v.shape, v.dtype) for v in late]
        + [
            pltpu.VMEM((rows, 128), F32),
            pltpu.VMEM((rows, width), F32),
            pltpu.VMEM((rows, 128), F32),
            pltpu.VMEM((n, d), BF16),
            pltpu.SemaphoreType.DMA((8,)),
            pltpu.SemaphoreType.DMA((disks, len(pieces))),
        ],
        compiler_params=params(67043328),
        cost_estimate=pl.CostEstimate(flops=16 * 10**9, bytes_accessed=10**7, transcendentals=10**6),
        name="disk_attend",
    )(start, extent, everything, *pieces, own, *late)


def device_at(z, y, x, core):
    return (z * 2 + y // 2) * 16 + (y % 2) * 8 + x * 2 + core


def ring(*steps):
    pairs = []
    for z in range(4):
        for y in range(4):
            for x in range(4):
                for core in range(2):
                    axis, by = steps[core]
                    to = [z, y, x]
                    to[axis] = (to[axis] + by) % 4
                    pairs.append((device_at(z, y, x, core), device_at(*to, core)))
    return pairs


def other_core():
    return [(s, s ^ 1) for s in range(128)]


def spread(block, first, second):
    got = []
    for by in (1, 3, 2):
        got.append(lax.ppermute(block, AXES, ring((first, by), (second, by))))
    return got


def gather_tokens(disk_tokens):
    block = jnp.transpose(disk_tokens, (1, 0, 2))
    block = jnp.concatenate([block] + spread(block, 0, 1), axis=1)
    block = lax.optimization_barrier(block)
    block = jnp.concatenate([block] + spread(block, 1, 2), axis=1)
    block = lax.optimization_barrier(block)
    pieces = [block] + spread(block, 2, 0)
    swapped = []
    for piece in pieces:
        swapped.append(lax.ppermute(piece, AXES, other_core()))
    return pieces + swapped


def local(
    mesh_nodes,
    norm_gain,
    w_query,
    w_node_kv,
    obs_rows,
    w_obs_kv,
    obs_owner,
    neighbours,
    neighbour_mask,
    disk_tokens,
    w_disk_kv,
    disk_start,
    disk_extent,
    w_out,
):
    devices = lax.axis_size("lat") * lax.axis_size("lon")
    width = obs_rows.shape[1]
    slots = devices * 8
    send = place(obs_owner.reshape(1, -1), obs_rows, slots)
    got = lax.all_to_all(
        send.reshape(devices, 8, width), AXES, split_axis=0, concat_axis=0, tiled=True
    ).reshape(slots, width)
    everything, own = prep(
        neighbours.T,
        neighbour_mask.T,
        mesh_nodes,
        norm_gain.reshape(1, -1),
        w_query,
        w_node_kv,
        w_disk_kv,
    )
    pieces = gather_tokens(disk_tokens)
    top, total, near = near_attend(got, w_obs_kv, everything, own)
    return disk_attend(
        disk_start, disk_extent, everything, pieces, own, top, total, near, w_disk_kv, w_out, mesh_nodes
    )


def solution(mesh):
    split = P(AXES, None)
    return jax.shard_map(
        local,
        mesh=mesh,
        in_specs=(
            split,
            P(),
            P(),
            P(),
            split,
            P(),
            split,
            split,
            split,
            P(AXES, None, None),
            P(),
            P(),
            P(),
            P(),
        ),
        out_specs=split,
        check_vma=False,
    )
```

```python
import functools

import jax
import jax.numpy as jnp
from jax import lax
from jax.experimental import pallas as pl
from jax.experimental.pallas import tpu as pltpu
from jax.sharding import PartitionSpec as P


HEADS = 8
AXES = ("lat", "lon")
LOG2E = 1.4426950408889634
EMPTY = 65536.0
NEG = -1e30
BIG = 2.0**100
F32 = jnp.float32
BF16 = jnp.bfloat16
NT = (((1,), (1,)), ((), ()))


def shape(dims, dtype):
    return jax.ShapeDtypeStruct(dims, dtype)


def params(grant=60 * 1024 * 1024):
    return pltpu.CompilerParams(vmem_limit_bytes=grant)


HBM = pl.BlockSpec(memory_space=pltpu.HBM)
VMEM = pl.BlockSpec(memory_space=pltpu.VMEM)
SMEM = pl.BlockSpec(memory_space=pltpu.SMEM)


def start_copy(source, target, sem):
    copy = pltpu.make_async_copy(source, target, sem)
    copy.start()
    return copy


def place_kernel(owner_ref, rows_ref, send_ref, held_ref, sems):
    count = rows_ref.shape[0]
    slots = send_ref.shape[0]
    owners = slots // 8
    owner = owner_ref[...]
    hot = jnp.where(lax.broadcasted_iota(jnp.int32, (owners, count), 0) == owner, 1.0, 0.0)
    row = lax.broadcasted_iota(jnp.int32, (count, count), 0)
    col = lax.broadcasted_iota(jnp.int32, (count, count), 1)
    earlier = jnp.where(row < col, 1.0, 0.0).astype(BF16)
    before = jnp.dot(hot.astype(BF16), earlier, preferred_element_type=F32)
    rank = jnp.sum(before * hot, axis=0, keepdims=True)
    slot = owner * 8 + rank.astype(jnp.int32)
    rows = rows_ref[...]
    ones_rows = jnp.ones((count, 128), BF16)
    step = slots // 4
    copies = []
    for i in range(4):
        at = pl.ds(i * step, step)
        ids_col = lax.broadcasted_iota(jnp.int32, (step, count), 0) + i * step
        placing = jnp.where(ids_col == slot, 1.0, 0.0).astype(BF16)
        placed = jnp.dot(placing, rows, preferred_element_type=F32)
        filled = jnp.dot(placing, ones_rows, preferred_element_type=F32)
        filled = jnp.concatenate([filled, filled], axis=1)
        held_ref[at, :] = jnp.where(filled > 0.5, placed, EMPTY).astype(BF16)
        copies.append(start_copy(held_ref.at[at, :], send_ref.at[at, :], sems.at[i]))
    for copy in copies:
        copy.wait()


def place(owner, rows, slots):
    return pl.pallas_call(
        place_kernel,
        out_shape=shape((slots, rows.shape[1]), BF16),
        in_specs=[VMEM, VMEM],
        out_specs=HBM,
        scratch_shapes=[pltpu.VMEM((slots, rows.shape[1]), BF16), pltpu.SemaphoreType.DMA((4,))],
        compiler_params=params(67043328),
        cost_estimate=pl.CostEstimate(flops=10**9, bytes_accessed=10**6, transcendentals=0),
        name="place",
    )(owner, rows)


def one_head(pair, odd):
    lane = lax.broadcasted_iota(jnp.int32, pair.shape, 1)
    keep = lane >= 64 if odd else lane < 64
    return jnp.where(keep, pair.astype(F32), 0.0).astype(pair.dtype)


def prep_kernel(
    near_ref, mark_ref, x_hbm, gain_ref, wq_hbm, wkv_hbm, wd_hbm, all_hbm, own_hbm,
    x_ref, wq_ref, wkv_ref, wd_ref, all_ref, own_ref, list_ref, sems, out_sems,
):
    n, d = x_ref.shape
    slots = 1024
    get_x = start_copy(x_hbm, x_ref, sems.at[0])
    get_wq = start_copy(wq_hbm, wq_ref, sems.at[1])
    get_wkv = start_copy(wkv_hbm, wkv_ref, sems.at[2])
    get_wd = start_copy(wd_hbm, wd_ref, sems.at[3])
    list_ref[...] = jnp.transpose(jnp.where(mark_ref[...] > 0, near_ref[...], -1), (1, 0))
    step = 64

    def body(i, carry):
        start = pl.multiple_of(i * step, step)
        near = list_ref[pl.ds(start, step), :].astype(jnp.int16)
        ids = lax.broadcasted_iota(jnp.int16, (step, slots), 1)
        total = jnp.zeros((step, slots), jnp.int16)
        one = jnp.ones((step, slots), jnp.int16)
        for entry in range(near.shape[1]):
            total = jnp.where(ids == near[:, entry : entry + 1], total + one, total)
        count = total.astype(F32).astype(BF16)
        for j in range(4):
            at = pl.ds(pl.multiple_of((12 + j) * n + start, step), step)
            all_ref[at, :] = count[:, j * 256 : j * 256 + 256]
        return carry

    lax.fori_loop(0, n // step, body, 0)

    def put(block, blocks, sem):
        at = pl.ds(block * n, blocks * n)
        return start_copy(all_ref.at[at, :], all_hbm.at[at, :], out_sems.at[sem])

    puts = [put(12, 4, 0)]
    get_x.wait()
    x = x_ref[...].astype(F32)
    inverse = lax.rsqrt(jnp.mean(x * x, axis=1, keepdims=True) + 1e-06)
    normed = (x * inverse * gain_ref[...]).astype(BF16)
    get_wq.wait()
    query = (jnp.dot(normed, wq_ref[...], preferred_element_type=F32) * 0.125).astype(BF16)
    get_wkv.wait()
    kv = jnp.dot(normed, wkv_ref[...], preferred_element_type=F32).astype(BF16)
    for j in range(2):
        all_ref[pl.ds((8 + j) * n, n), :] = query[:, j * 256 : j * 256 + 256]
        all_ref[pl.ds((10 + j) * n, n), :] = kv[:, d + j * 256 : d + j * 256 + 256]
    puts.append(put(8, 4, 1))
    prod = query.astype(F32) * kv[:, :d].astype(F32)
    lane = lax.broadcasted_iota(jnp.int32, (n, 128), 1)
    own = jnp.zeros((n, 128), F32)
    get_wd.wait()
    for head in range(HEADS):
        lo = head // 2 * 128
        part = jnp.sum(prod[:, head * 64 : head * 64 + 64], axis=1, keepdims=True) * LOG2E
        own = jnp.where(lane == head, part, own)
        lifted = lax.dot_general(
            one_head(query[:, lo : lo + 128], head % 2),
            wd_ref[:, lo : lo + 128],
            NT,
            preferred_element_type=F32,
        )
        all_ref[pl.ds(head * n, n), :] = (lifted * LOG2E).astype(BF16)
        puts.append(put(head, 1, 2 + head))
    own_ref[...] = own
    puts.append(start_copy(own_ref, own_hbm, out_sems.at[2 + HEADS]))
    for copy in puts:
        copy.wait()


def prep(near, mark, x, gain, wq, wkv, wd):
    n, _ = x.shape
    outs = [((16 * n, 256), BF16), ((n, 128), F32)]
    ins = [(v.shape, v.dtype) for v in (x, wq, wkv, wd)]
    return pl.pallas_call(
        prep_kernel,
        out_shape=tuple(shape(*o) for o in outs),
        in_specs=[VMEM, VMEM, HBM, VMEM, HBM, HBM, HBM],
        out_specs=(HBM,) * 2,
        scratch_shapes=[pltpu.VMEM(*v) for v in ins + outs]
        + [
            pltpu.VMEM(near.shape[::-1], jnp.int32),
            pltpu.SemaphoreType.DMA((4,)),
            pltpu.SemaphoreType.DMA((3 + HEADS,)),
        ],
        compiler_params=params(),
        cost_estimate=pl.CostEstimate(flops=8 * 10**9, bytes_accessed=8 * 10**6, transcendentals=0),
        name="prep",
    )(near, mark, x, gain, wq, wkv, wd)


def near_kernel(
    got_hbm, w_hbm, all_hbm, own_hbm, top_hbm, sum_hbm, acc_hbm,
    got_ref, w_ref, query_ref, count_ref, own_ref, value_ref, top_ref, sum_ref, acc_ref,
    key_ref, val_ref, bias_ref, sems,
):
    slots = got_ref.shape[0]
    n, d = query_ref.shape
    get_got = start_copy(got_hbm, got_ref, sems.at[0])
    get_w = start_copy(w_hbm, w_ref, sems.at[1])

    def get_block(block, target, j, sem):
        return start_copy(
            all_hbm.at[pl.ds(block * n, n), :], target.at[:, pl.ds(j * 256, 256)], sems.at[sem]
        )

    for pair in range(HEADS // 2):
        val_ref[pair, :, 128:] = jnp.ones((slots, 128), BF16)
    get_got.wait()
    get_count = [get_block(12 + j, count_ref, j, 8 + j) for j in range(4)]
    gets = [get_block(8 + j, query_ref, j, 2 + j) for j in range(2)]
    gets += [get_block(10 + j, value_ref, j, 4 + j) for j in range(2)]
    gets.append(start_copy(own_hbm, own_ref, sems.at[6]))
    got = got_ref[...]
    absent = got.astype(F32) > 1024.0
    rows = jnp.where(absent, 0.0, got.astype(F32)).astype(BF16)
    ones = jnp.ones((8, 128), BF16)
    empty = lax.dot_general(
        ones, jnp.where(absent[:, :128], 1.0, 0.0).astype(BF16), NT, preferred_element_type=F32
    )[0:1, :]
    get_w.wait()
    kv = jnp.dot(rows, w_ref[...], preferred_element_type=F32).astype(BF16)
    key_ref[...] = kv[:, :d]
    for pair in range(HEADS // 2):
        lo = d + pair * 128
        val_ref[pair, :, :128] = kv[:, lo : lo + 128]
    for copy in get_count:
        copy.wait()
    for copy in gets:
        copy.wait()

    def attend(i, step, exact):
        lane = lax.broadcasted_iota(jnp.int32, (step, 128), 1)
        at = pl.ds(pl.multiple_of(i * step, step), step)
        count = count_ref[at, :].astype(F32)
        listed = (count > 0.0) & (empty < 0.5)
        bias_ref[at, :] = jnp.where(listed, jnp.log2(jnp.maximum(count, 1.0)), NEG)
        own = own_ref[at, :]
        tops = own
        sums = jnp.ones((step, 128), F32)
        for pair in range(HEADS // 2):
            lo = pair * 128
            sides = []
            for odd in range(2):
                head = 2 * pair + odd
                scores = lax.dot_general(
                    one_head(query_ref[at, lo : lo + 128], odd),
                    key_ref[:, lo : lo + 128],
                    NT,
                    preferred_element_type=F32,
                )
                scores = scores * LOG2E + bias_ref[at, :]
                shift = own[:, head : head + 1]
                if exact:
                    mine = shift
                    shift = jnp.maximum(jnp.max(scores, axis=1, keepdims=True), mine)
                    self_weight = jnp.exp2(mine - shift).astype(BF16).astype(F32)
                    tops = jnp.where(lane == head, shift, tops)
                else:
                    self_weight = 1.0
                weights = jnp.exp2(scores - shift).astype(BF16)
                part = jnp.dot(weights, val_ref[pair], preferred_element_type=F32)
                sums = jnp.where(lane == head, part[:, 128:] + self_weight, sums)
                sides.append(part[:, :128] + self_weight * value_ref[at, lo : lo + 128].astype(F32))
            acc_ref[at, lo : lo + 128] = jnp.where(lane < 64, sides[0], sides[1])
        top_ref[at, :] = tops
        sum_ref[at, :] = sums

    half = n // 2

    def results(i):
        at = pl.ds(pl.multiple_of(i * half, half), half)
        return [
            pltpu.make_async_copy(source.at[at, :], target.at[at, :], sems.at[12 + 3 * i + j])
            for j, (source, target) in enumerate(
                ((top_ref, top_hbm), (sum_ref, sum_hbm), (acc_ref, acc_hbm))
            )
        ]

    for i in range(2):
        attend(i, half, False)
        for copy in results(i):
            copy.start()
    for i in range(2):
        for copy in results(i):
            copy.wait()
    worst = jnp.max(jnp.max(sum_ref[...], axis=0, keepdims=True))

    @pl.when(jnp.logical_not(worst < BIG))
    def _():
        lax.fori_loop(0, n // 64, lambda i, carry: attend(i, 64, True) or carry, 0)
        for i in range(2):
            for copy in results(i):
                copy.start()
                copy.wait()


def near_attend(got, w, everything, own):
    n, d = own.shape[0], w.shape[1] // 2
    slots = got.shape[0]
    ins = [(got.shape, BF16), (w.shape, BF16), ((n, d), BF16), ((n, slots), BF16)]
    ins += [(own.shape, F32), ((n, d), BF16)]
    outs = [((n, 128), F32), ((n, 128), F32), ((n, d), F32)]
    return pl.pallas_call(
        near_kernel,
        out_shape=tuple(shape(*o) for o in outs),
        in_specs=[HBM] * 4,
        out_specs=(HBM,) * 3,
        scratch_shapes=[pltpu.VMEM(*v) for v in ins + outs]
        + [
            pltpu.VMEM((slots, d), BF16),
            pltpu.VMEM((HEADS // 2, slots, 256), BF16),
            pltpu.VMEM((n, slots), F32),
            pltpu.SemaphoreType.DMA((18,)),
        ],
        compiler_params=params(67043328),
        cost_estimate=pl.CostEstimate(flops=5 * 10**9, bytes_accessed=5 * 10**6, transcendentals=10**6),
        name="near_attend",
    )(got, w, everything, own)


def disk_kernel(*refs, pieces):
    (start_ref, extent_ref, lifted_hbm), refs = refs[:3], refs[3:]
    piece_hbm, refs = refs[:pieces], refs[pieces:]
    late_hbm, refs = refs[:7], refs[7:]
    out_ref, own_ref, lifted_ref, tok_ref = refs[:4]
    top_ref, sum_ref, near_ref, wd_ref, wout_ref, x_ref = late_refs = refs[4:10]
    shift_ref, acc_ref, den_ref, att_ref, sems, tok_sems = refs[10:]
    own_hbm = late_hbm[0]
    n, d = x_ref.shape
    rows = lifted_ref.shape[0]
    disks, size = piece_hbm[0].shape[:2]

    get_own = start_copy(own_hbm, own_ref, sems.at[0])
    get_lifted = start_copy(lifted_hbm.at[pl.ds(0, rows), :], lifted_ref, sems.at[1])
    here = lax.axis_index("lon")
    sectors = lax.axis_size("lon")

    def seen(disk):
        return lax.rem(here - start_ref[disk] + sectors, sectors) < extent_ref[disk]

    def token_copies(disk):
        return [
            pltpu.make_async_copy(
                piece_hbm[i].at[disk],
                tok_ref.at[disk, pl.ds(i * size, size), :],
                tok_sems.at[disk, i],
            )
            for i in range(pieces)
        ]

    for disk in range(disks):

        @pl.when(seen(disk))
        def _():
            for copy in token_copies(disk):
                copy.start()

    late = [
        start_copy(source, target, sems.at[2 + i])
        for i, (source, target) in enumerate(zip(late_hbm[1:], late_refs))
    ]

    def add_disks(step, unroll, first):
        den_ref[...] = jnp.zeros_like(den_ref)
        acc_ref[...] = jnp.zeros_like(acc_ref)
        if first:
            get_own.wait()
            for head in range(HEADS):
                shift_ref[pl.ds(head * n, n), :] = jnp.broadcast_to(own_ref[:, head : head + 1], (n, 128))
            get_lifted.wait()

        def add_disk(disk, carry):
            @pl.when(seen(disk))
            def _():
                if first:
                    for copy in token_copies(disk):
                        copy.wait()

                def body(i, inner):
                    for u in range(unroll):
                        at = pl.ds(pl.multiple_of((i * unroll + u) * step, step), step)
                        scores = lax.dot_general(
                            lifted_ref[at, :], tok_ref[disk], NT, preferred_element_type=F32
                        )
                        weights = jnp.exp2(scores - shift_ref[at, :1])
                        part = weights[:, :128]
                        for j in range(1, weights.shape[1] // 128):
                            part = part + weights[:, j * 128 : j * 128 + 128]
                        den_ref[at, :] += part
                        acc_ref[at, :] += jnp.dot(
                            weights.astype(BF16), tok_ref[disk], preferred_element_type=F32
                        )
                    return inner

                lax.fori_loop(0, rows // (step * unroll), body, 0)

            return carry

        lax.fori_loop(0, disks, add_disk, 0)

    add_disks(512, 8, True)

    worst = jnp.max(jnp.max(den_ref[...], axis=0, keepdims=True))

    @pl.when(jnp.logical_not(worst < BIG))
    def _():
        def top_disk(disk, carry):
            @pl.when(seen(disk))
            def _():
                def body(i, inner):
                    at = pl.ds(pl.multiple_of(i * 128, 128), 128)
                    scores = lax.dot_general(
                        lifted_ref[at, :], tok_ref[disk], NT, preferred_element_type=F32
                    )
                    best = jnp.max(scores, axis=1, keepdims=True)
                    shift_ref[at, :] = jnp.maximum(shift_ref[at, :], best)
                    return inner

                lax.fori_loop(0, rows // 128, body, 0)

            return carry

        lax.fori_loop(0, disks, top_disk, 0)
        add_disks(128, 1, False)

    for copy in late:
        copy.wait()
    lane = lax.broadcasted_iota(jnp.int32, (n, 128), 1)

    def join(scaled):
        for pair in range(HEADS // 2):
            lo = pair * 128
            sides = []
            for odd in range(2):
                head = 2 * pair + odd
                at = pl.ds(head * n, n)
                wide = acc_ref[at, :]
                part_sum = den_ref[at, :]
                near = near_ref[:, lo : lo + 128]
                near_sum = sum_ref[...]
                if scaled:
                    shift = shift_ref[at, :1]
                    top = top_ref[:, head : head + 1]
                    best = jnp.maximum(shift, top)
                    disk_scale = jnp.exp2(shift - best)
                    near_scale = jnp.exp2(top - best)
                    wide = wide * disk_scale
                    part_sum = part_sum * disk_scale
                    near = near * near_scale
                    near_sum = near_sum * near_scale
                total = jnp.sum(
                    part_sum + jnp.where(lane == head, near_sum, 0.0), axis=1, keepdims=True
                )
                part = jnp.dot(
                    wide.astype(BF16), wd_ref[:, d + lo : d + lo + 128], preferred_element_type=F32
                )
                sides.append((part + near) * (1.0 / total))
            att_ref[:, lo : lo + 128] = jnp.where(lane < 64, sides[0], sides[1]).astype(BF16)

    moved = jnp.max(jnp.max(jnp.abs(top_ref[...] - own_ref[...]), axis=0, keepdims=True))
    same = (worst < BIG) & (moved == 0.0)

    @pl.when(same)
    def _():
        join(False)

    @pl.when(jnp.logical_not(same))
    def _():
        join(True)

    out = jnp.dot(att_ref[...], wout_ref[...], preferred_element_type=F32)
    out_ref[...] = (x_ref[...].astype(F32) + out).astype(BF16)


def disk_attend(start, extent, everything, pieces, own, top, total, near, wd, wout, x):
    n, d = x.shape
    disks = pieces[0].shape[0]
    tokens = sum(piece.shape[1] for piece in pieces)
    rows, width = HEADS * n, wd.shape[0]
    late = (top, total, near, wd, wout, x)
    return pl.pallas_call(
        functools.partial(disk_kernel, pieces=len(pieces)),
        out_shape=shape((n, d), BF16),
        in_specs=[SMEM, SMEM] + [HBM] * (8 + len(pieces)),
        out_specs=VMEM,
        scratch_shapes=[
            pltpu.VMEM(own.shape, F32),
            pltpu.VMEM((rows, width), BF16),
            pltpu.VMEM((disks, tokens, width), BF16),
        ]
        + [pltpu.VMEM(v.shape, v.dtype) for v in late]
        + [
            pltpu.VMEM((rows, 128), F32),
            pltpu.VMEM((rows, width), F32),
            pltpu.VMEM((rows, 128), F32),
            pltpu.VMEM((n, d), BF16),
            pltpu.SemaphoreType.DMA((8,)),
            pltpu.SemaphoreType.DMA((disks, len(pieces))),
        ],
        compiler_params=params(67043328),
        cost_estimate=pl.CostEstimate(flops=16 * 10**9, bytes_accessed=10**7, transcendentals=10**6),
        name="disk_attend",
    )(start, extent, everything, *pieces, own, *late)


def device_at(z, y, x, core):
    return (z * 2 + y // 2) * 16 + (y % 2) * 8 + x * 2 + core


def ring(*steps):
    pairs = []
    for z in range(4):
        for y in range(4):
            for x in range(4):
                for core in range(2):
                    axis, by = steps[core]
                    to = [z, y, x]
                    to[axis] = (to[axis] + by) % 4
                    pairs.append((device_at(z, y, x, core), device_at(*to, core)))
    return pairs


def other_core():
    return [(s, s ^ 1) for s in range(128)]


def spread(block, first, second):
    got = []
    for by in (1, 3, 2):
        got.append(lax.ppermute(block, AXES, ring((first, by), (second, by))))
    return got


def gather_tokens(disk_tokens):
    block = jnp.transpose(disk_tokens, (1, 0, 2))
    block = jnp.concatenate([block] + spread(block, 0, 1), axis=1)
    block = lax.optimization_barrier(block)
    block = jnp.concatenate([block] + spread(block, 1, 2), axis=1)
    block = lax.optimization_barrier(block)
    pieces = [block] + spread(block, 2, 0)
    swapped = []
    for piece in pieces:
        swapped.append(lax.ppermute(piece, AXES, other_core()))
    return pieces + swapped


def local(
    mesh_nodes,
    norm_gain,
    w_query,
    w_node_kv,
    obs_rows,
    w_obs_kv,
    obs_owner,
    neighbours,
    neighbour_mask,
    disk_tokens,
    w_disk_kv,
    disk_start,
    disk_extent,
    w_out,
):
    devices = lax.axis_size("lat") * lax.axis_size("lon")
    width = obs_rows.shape[1]
    slots = devices * 8
    send = place(obs_owner.reshape(1, -1), obs_rows, slots)
    got = lax.all_to_all(
        send.reshape(devices, 8, width), AXES, split_axis=0, concat_axis=0, tiled=True
    ).reshape(slots, width)
    everything, own = prep(
        neighbours.T,
        neighbour_mask.T,
        mesh_nodes,
        norm_gain.reshape(1, -1),
        w_query,
        w_node_kv,
        w_disk_kv,
    )
    pieces = gather_tokens(disk_tokens)
    top, total, near = near_attend(got, w_obs_kv, everything, own)
    return disk_attend(
        disk_start, disk_extent, everything, pieces, own, top, total, near, w_disk_kv, w_out, mesh_nodes
    )


def solution(mesh):
    split = P(AXES, None)
    return jax.shard_map(
        local,
        mesh=mesh,
        in_specs=(
            split,
            P(),
            P(),
            P(),
            split,
            P(),
            split,
            split,
            split,
            P(AXES, None, None),
            P(),
            P(),
            P(),
            P(),
        ),
        out_specs=split,
        check_vma=False,
    )
```

```python
import functools

import jax
import jax.numpy as jnp
from jax import lax
from jax.experimental import pallas as pl
from jax.experimental.pallas import tpu as pltpu
from jax.sharding import PartitionSpec as P


HEADS = 8
AXES = ("lat", "lon")
LOG2E = 1.4426950408889634
EMPTY = 65536.0
NEG = -1e30
BIG = 2.0**100
F32 = jnp.float32
BF16 = jnp.bfloat16
NT = (((1,), (1,)), ((), ()))


def shape(dims, dtype):
    return jax.ShapeDtypeStruct(dims, dtype)


def params(grant=60 * 1024 * 1024):
    return pltpu.CompilerParams(vmem_limit_bytes=grant)


HBM = pl.BlockSpec(memory_space=pltpu.HBM)
VMEM = pl.BlockSpec(memory_space=pltpu.VMEM)
SMEM = pl.BlockSpec(memory_space=pltpu.SMEM)


def start_copy(source, target, sem):
    copy = pltpu.make_async_copy(source, target, sem)
    copy.start()
    return copy


def place_kernel(owner_ref, rows_ref, send_ref, held_ref, sems):
    count = rows_ref.shape[0]
    slots = send_ref.shape[0]
    owners = slots // 8
    owner = owner_ref[...]
    hot = jnp.where(lax.broadcasted_iota(jnp.int32, (owners, count), 0) == owner, 1.0, 0.0)
    row = lax.broadcasted_iota(jnp.int32, (count, count), 0)
    col = lax.broadcasted_iota(jnp.int32, (count, count), 1)
    earlier = jnp.where(row < col, 1.0, 0.0).astype(BF16)
    before = jnp.dot(hot.astype(BF16), earlier, preferred_element_type=F32)
    rank = jnp.sum(before * hot, axis=0, keepdims=True)
    slot = owner * 8 + rank.astype(jnp.int32)
    rows = rows_ref[...]
    ones_rows = jnp.ones((count, 128), BF16)
    step = slots // 4
    copies = []
    for i in range(4):
        at = pl.ds(i * step, step)
        ids_col = lax.broadcasted_iota(jnp.int32, (step, count), 0) + i * step
        placing = jnp.where(ids_col == slot, 1.0, 0.0).astype(BF16)
        placed = jnp.dot(placing, rows, preferred_element_type=F32)
        filled = jnp.dot(placing, ones_rows, preferred_element_type=F32)
        filled = jnp.concatenate([filled, filled], axis=1)
        held_ref[at, :] = jnp.where(filled > 0.5, placed, EMPTY).astype(BF16)
        copies.append(start_copy(held_ref.at[at, :], send_ref.at[at, :], sems.at[i]))
    for copy in copies:
        copy.wait()


def place(owner, rows, slots):
    return pl.pallas_call(
        place_kernel,
        out_shape=shape((slots, rows.shape[1]), BF16),
        in_specs=[VMEM, VMEM],
        out_specs=HBM,
        scratch_shapes=[pltpu.VMEM((slots, rows.shape[1]), BF16), pltpu.SemaphoreType.DMA((4,))],
        compiler_params=params(),
        cost_estimate=pl.CostEstimate(flops=10**9, bytes_accessed=10**6, transcendentals=0),
        name="place",
    )(owner, rows)


def one_head(pair, odd):
    lane = lax.broadcasted_iota(jnp.int32, pair.shape, 1)
    keep = lane >= 64 if odd else lane < 64
    return jnp.where(keep, pair.astype(F32), 0.0).astype(pair.dtype)


def prep_kernel(
    near_ref, mark_ref, x_hbm, gain_ref, wq_hbm, wkv_hbm, wd_hbm, all_hbm, own_hbm,
    x_ref, wq_ref, wkv_ref, wd_ref, all_ref, own_ref, list_ref, sems, out_sems,
):
    n, d = x_ref.shape
    slots = 1024
    get_x = start_copy(x_hbm, x_ref, sems.at[0])
    get_wq = start_copy(wq_hbm, wq_ref, sems.at[1])
    get_wkv = start_copy(wkv_hbm, wkv_ref, sems.at[2])
    get_wd = start_copy(wd_hbm, wd_ref, sems.at[3])
    list_ref[...] = jnp.transpose(jnp.where(mark_ref[...] > 0, near_ref[...], -1), (1, 0))
    step = 64

    def body(i, carry):
        start = pl.multiple_of(i * step, step)
        near = list_ref[pl.ds(start, step), :].astype(jnp.int16)
        ids = lax.broadcasted_iota(jnp.int16, (step, slots), 1)
        total = jnp.zeros((step, slots), jnp.int16)
        one = jnp.ones((step, slots), jnp.int16)
        for entry in range(near.shape[1]):
            total = jnp.where(ids == near[:, entry : entry + 1], total + one, total)
        count = total.astype(F32).astype(BF16)
        for j in range(4):
            at = pl.ds(pl.multiple_of((12 + j) * n + start, step), step)
            all_ref[at, :] = count[:, j * 256 : j * 256 + 256]
        return carry

    lax.fori_loop(0, n // step, body, 0)

    def put(block, blocks, sem):
        at = pl.ds(block * n, blocks * n)
        return start_copy(all_ref.at[at, :], all_hbm.at[at, :], out_sems.at[sem])

    puts = [put(12, 4, 0)]
    get_x.wait()
    x = x_ref[...].astype(F32)
    inverse = lax.rsqrt(jnp.mean(x * x, axis=1, keepdims=True) + 1e-06)
    normed = (x * inverse * gain_ref[...]).astype(BF16)
    get_wq.wait()
    query = (jnp.dot(normed, wq_ref[...], preferred_element_type=F32) * 0.125).astype(BF16)
    get_wkv.wait()
    kv = jnp.dot(normed, wkv_ref[...], preferred_element_type=F32).astype(BF16)
    for j in range(2):
        all_ref[pl.ds((8 + j) * n, n), :] = query[:, j * 256 : j * 256 + 256]
        all_ref[pl.ds((10 + j) * n, n), :] = kv[:, d + j * 256 : d + j * 256 + 256]
    puts.append(put(8, 4, 1))
    prod = query.astype(F32) * kv[:, :d].astype(F32)
    lane = lax.broadcasted_iota(jnp.int32, (n, 128), 1)
    own = jnp.zeros((n, 128), F32)
    get_wd.wait()
    for head in range(HEADS):
        lo = head // 2 * 128
        part = jnp.sum(prod[:, head * 64 : head * 64 + 64], axis=1, keepdims=True) * LOG2E
        own = jnp.where(lane == head, part, own)
        lifted = lax.dot_general(
            one_head(query[:, lo : lo + 128], head % 2),
            wd_ref[:, lo : lo + 128],
            NT,
            preferred_element_type=F32,
        )
        all_ref[pl.ds(head * n, n), :] = (lifted * LOG2E).astype(BF16)
        puts.append(put(head, 1, 2 + head))
    own_ref[...] = own
    puts.append(start_copy(own_ref, own_hbm, out_sems.at[2 + HEADS]))
    for copy in puts:
        copy.wait()


def prep(near, mark, x, gain, wq, wkv, wd):
    n, _ = x.shape
    outs = [((16 * n, 256), BF16), ((n, 128), F32)]
    ins = [(v.shape, v.dtype) for v in (x, wq, wkv, wd)]
    return pl.pallas_call(
        prep_kernel,
        out_shape=tuple(shape(*o) for o in outs),
        in_specs=[VMEM, VMEM, HBM, VMEM, HBM, HBM, HBM],
        out_specs=(HBM,) * 2,
        scratch_shapes=[pltpu.VMEM(*v) for v in ins + outs]
        + [
            pltpu.VMEM(near.shape[::-1], jnp.int32),
            pltpu.SemaphoreType.DMA((4,)),
            pltpu.SemaphoreType.DMA((3 + HEADS,)),
        ],
        compiler_params=params(),
        cost_estimate=pl.CostEstimate(flops=8 * 10**9, bytes_accessed=8 * 10**6, transcendentals=0),
        name="prep",
    )(near, mark, x, gain, wq, wkv, wd)


def near_kernel(
    got_hbm, w_hbm, all_hbm, own_hbm, top_hbm, sum_hbm, acc_hbm,
    got_ref, w_ref, query_ref, count_ref, own_ref, value_ref, top_ref, sum_ref, acc_ref,
    key_ref, val_ref, bias_ref, sems,
):
    slots = got_ref.shape[0]
    n, d = query_ref.shape
    get_got = start_copy(got_hbm, got_ref, sems.at[0])
    get_w = start_copy(w_hbm, w_ref, sems.at[1])

    def get_block(block, target, j, sem):
        return start_copy(
            all_hbm.at[pl.ds(block * n, n), :], target.at[:, pl.ds(j * 256, 256)], sems.at[sem]
        )

    for pair in range(HEADS // 2):
        val_ref[pair, :, 128:] = jnp.ones((slots, 128), BF16)
    get_got.wait()
    get_count = [get_block(12 + j, count_ref, j, 8 + j) for j in range(4)]
    gets = [get_block(8 + j, query_ref, j, 2 + j) for j in range(2)]
    gets += [get_block(10 + j, value_ref, j, 4 + j) for j in range(2)]
    gets.append(start_copy(own_hbm, own_ref, sems.at[6]))
    got = got_ref[...]
    absent = got.astype(F32) > 1024.0
    rows = jnp.where(absent, 0.0, got.astype(F32)).astype(BF16)
    ones = jnp.ones((8, 128), BF16)
    empty = lax.dot_general(
        ones, jnp.where(absent[:, :128], 1.0, 0.0).astype(BF16), NT, preferred_element_type=F32
    )[0:1, :]
    get_w.wait()
    kv = jnp.dot(rows, w_ref[...], preferred_element_type=F32).astype(BF16)
    key_ref[...] = kv[:, :d]
    for pair in range(HEADS // 2):
        lo = d + pair * 128
        val_ref[pair, :, :128] = kv[:, lo : lo + 128]
    for copy in get_count:
        copy.wait()
    count = count_ref[...].astype(F32)
    bias_ref[...] = jnp.where((count > 0.0) & (empty < 0.5), jnp.log2(jnp.maximum(count, 1.0)), NEG)
    for copy in gets:
        copy.wait()

    def attend(i, step, exact):
        lane = lax.broadcasted_iota(jnp.int32, (step, 128), 1)
        at = pl.ds(pl.multiple_of(i * step, step), step)
        own = own_ref[at, :]
        tops = own
        sums = jnp.ones((step, 128), F32)
        for pair in range(HEADS // 2):
            lo = pair * 128
            sides = []
            for odd in range(2):
                head = 2 * pair + odd
                scores = lax.dot_general(
                    one_head(query_ref[at, lo : lo + 128], odd),
                    key_ref[:, lo : lo + 128],
                    NT,
                    preferred_element_type=F32,
                )
                scores = scores * LOG2E + bias_ref[at, :]
                shift = own[:, head : head + 1]
                if exact:
                    mine = shift
                    shift = jnp.maximum(jnp.max(scores, axis=1, keepdims=True), mine)
                    self_weight = jnp.exp2(mine - shift).astype(BF16).astype(F32)
                    tops = jnp.where(lane == head, shift, tops)
                else:
                    self_weight = 1.0
                weights = jnp.exp2(scores - shift).astype(BF16)
                part = jnp.dot(weights, val_ref[pair], preferred_element_type=F32)
                sums = jnp.where(lane == head, part[:, 128:] + self_weight, sums)
                sides.append(part[:, :128] + self_weight * value_ref[at, lo : lo + 128].astype(F32))
            acc_ref[at, lo : lo + 128] = jnp.where(lane < 64, sides[0], sides[1])
        top_ref[at, :] = tops
        sum_ref[at, :] = sums

    half = n // 2

    def results(i):
        at = pl.ds(pl.multiple_of(i * half, half), half)
        return [
            pltpu.make_async_copy(source.at[at, :], target.at[at, :], sems.at[12 + 3 * i + j])
            for j, (source, target) in enumerate(
                ((top_ref, top_hbm), (sum_ref, sum_hbm), (acc_ref, acc_hbm))
            )
        ]

    def one_half(i, carry):
        attend(i, half, False)
        for copy in results(i):
            copy.start()
        return carry

    lax.fori_loop(0, 2, one_half, 0)
    for i in range(2):
        for copy in results(i):
            copy.wait()
    worst = jnp.max(jnp.max(sum_ref[...], axis=0, keepdims=True))

    @pl.when(jnp.logical_not(worst < BIG))
    def _():
        lax.fori_loop(0, n // 64, lambda i, carry: attend(i, 64, True) or carry, 0)
        for i in range(2):
            for copy in results(i):
                copy.start()
                copy.wait()


def near_attend(got, w, everything, own):
    n, d = own.shape[0], w.shape[1] // 2
    slots = got.shape[0]
    ins = [(got.shape, BF16), (w.shape, BF16), ((n, d), BF16), ((n, slots), BF16)]
    ins += [(own.shape, F32), ((n, d), BF16)]
    outs = [((n, 128), F32), ((n, 128), F32), ((n, d), F32)]
    return pl.pallas_call(
        near_kernel,
        out_shape=tuple(shape(*o) for o in outs),
        in_specs=[HBM] * 4,
        out_specs=(HBM,) * 3,
        scratch_shapes=[pltpu.VMEM(*v) for v in ins + outs]
        + [
            pltpu.VMEM((slots, d), BF16),
            pltpu.VMEM((HEADS // 2, slots, 256), BF16),
            pltpu.VMEM((n, slots), F32),
            pltpu.SemaphoreType.DMA((18,)),
        ],
        compiler_params=params(67043328),
        cost_estimate=pl.CostEstimate(flops=5 * 10**9, bytes_accessed=5 * 10**6, transcendentals=10**6),
        name="near_attend",
    )(got, w, everything, own)


def disk_kernel(*refs, pieces):
    (start_ref, extent_ref, lifted_hbm), refs = refs[:3], refs[3:]
    piece_hbm, refs = refs[:pieces], refs[pieces:]
    late_hbm, refs = refs[:7], refs[7:]
    out_ref, own_ref, lifted_ref, tok_ref = refs[:4]
    top_ref, sum_ref, near_ref, wd_ref, wout_ref, x_ref = late_refs = refs[4:10]
    shift_ref, acc_ref, den_ref, att_ref, sems, tok_sems = refs[10:]
    own_hbm = late_hbm[0]
    n, d = x_ref.shape
    rows = lifted_ref.shape[0]
    disks, size = piece_hbm[0].shape[:2]

    get_own = start_copy(own_hbm, own_ref, sems.at[0])
    get_lifted = start_copy(lifted_hbm.at[pl.ds(0, rows), :], lifted_ref, sems.at[1])
    here = lax.axis_index("lon")
    sectors = lax.axis_size("lon")

    def seen(disk):
        return lax.rem(here - start_ref[disk] + sectors, sectors) < extent_ref[disk]

    def token_copies(disk):
        return [
            pltpu.make_async_copy(
                piece_hbm[i].at[disk],
                tok_ref.at[disk, pl.ds(i * size, size), :],
                tok_sems.at[disk, i],
            )
            for i in range(pieces)
        ]

    for disk in range(disks):

        @pl.when(seen(disk))
        def _():
            for copy in token_copies(disk):
                copy.start()

    late = [
        start_copy(source, target, sems.at[2 + i])
        for i, (source, target) in enumerate(zip(late_hbm[1:], late_refs))
    ]

    def add_disks(step, unroll, first):
        den_ref[...] = jnp.zeros_like(den_ref)
        acc_ref[...] = jnp.zeros_like(acc_ref)
        if first:
            get_own.wait()
            for head in range(HEADS):
                shift_ref[pl.ds(head * n, n), :] = jnp.broadcast_to(own_ref[:, head : head + 1], (n, 128))
            get_lifted.wait()

        def add_disk(disk, carry):
            @pl.when(seen(disk))
            def _():
                if first:
                    for copy in token_copies(disk):
                        copy.wait()

                def body(i, inner):
                    for u in range(unroll):
                        at = pl.ds(pl.multiple_of((i * unroll + u) * step, step), step)
                        scores = lax.dot_general(
                            lifted_ref[at, :], tok_ref[disk], NT, preferred_element_type=F32
                        )
                        weights = jnp.exp2(scores - shift_ref[at, :1])
                        part = weights[:, :128]
                        for j in range(1, weights.shape[1] // 128):
                            part = part + weights[:, j * 128 : j * 128 + 128]
                        den_ref[at, :] += part
                        acc_ref[at, :] += jnp.dot(
                            weights.astype(BF16), tok_ref[disk], preferred_element_type=F32
                        )
                    return inner

                lax.fori_loop(0, rows // (step * unroll), body, 0)

            return carry

        lax.fori_loop(0, disks, add_disk, 0)

    add_disks(512, 8, True)

    worst = jnp.max(jnp.max(den_ref[...], axis=0, keepdims=True))

    @pl.when(jnp.logical_not(worst < BIG))
    def _():
        def top_disk(disk, carry):
            @pl.when(seen(disk))
            def _():
                def body(i, inner):
                    at = pl.ds(pl.multiple_of(i * 128, 128), 128)
                    scores = lax.dot_general(
                        lifted_ref[at, :], tok_ref[disk], NT, preferred_element_type=F32
                    )
                    best = jnp.max(scores, axis=1, keepdims=True)
                    shift_ref[at, :] = jnp.maximum(shift_ref[at, :], best)
                    return inner

                lax.fori_loop(0, rows // 128, body, 0)

            return carry

        lax.fori_loop(0, disks, top_disk, 0)
        add_disks(128, 1, False)

    for copy in late:
        copy.wait()
    lane = lax.broadcasted_iota(jnp.int32, (n, 128), 1)

    def join(scaled):
        for pair in range(HEADS // 2):
            lo = pair * 128
            sides = []
            for odd in range(2):
                head = 2 * pair + odd
                at = pl.ds(head * n, n)
                wide = acc_ref[at, :]
                part_sum = den_ref[at, :]
                near = near_ref[:, lo : lo + 128]
                near_sum = sum_ref[...]
                if scaled:
                    shift = shift_ref[at, :1]
                    top = top_ref[:, head : head + 1]
                    best = jnp.maximum(shift, top)
                    disk_scale = jnp.exp2(shift - best)
                    near_scale = jnp.exp2(top - best)
                    wide = wide * disk_scale
                    part_sum = part_sum * disk_scale
                    near = near * near_scale
                    near_sum = near_sum * near_scale
                total = jnp.sum(
                    part_sum + jnp.where(lane == head, near_sum, 0.0), axis=1, keepdims=True
                )
                part = jnp.dot(
                    wide.astype(BF16), wd_ref[:, d + lo : d + lo + 128], preferred_element_type=F32
                )
                sides.append((part + near) * (1.0 / total))
            att_ref[:, lo : lo + 128] = jnp.where(lane < 64, sides[0], sides[1]).astype(BF16)

    moved = jnp.max(jnp.max(jnp.abs(top_ref[...] - own_ref[...]), axis=0, keepdims=True))
    same = (worst < BIG) & (moved == 0.0)

    @pl.when(same)
    def _():
        join(False)

    @pl.when(jnp.logical_not(same))
    def _():
        join(True)

    out = jnp.dot(att_ref[...], wout_ref[...], preferred_element_type=F32)
    out_ref[...] = (x_ref[...].astype(F32) + out).astype(BF16)


def disk_attend(start, extent, everything, pieces, own, top, total, near, wd, wout, x):
    n, d = x.shape
    disks = pieces[0].shape[0]
    tokens = sum(piece.shape[1] for piece in pieces)
    rows, width = HEADS * n, wd.shape[0]
    late = (top, total, near, wd, wout, x)
    return pl.pallas_call(
        functools.partial(disk_kernel, pieces=len(pieces)),
        out_shape=shape((n, d), BF16),
        in_specs=[SMEM, SMEM] + [HBM] * (8 + len(pieces)),
        out_specs=VMEM,
        scratch_shapes=[
            pltpu.VMEM(own.shape, F32),
            pltpu.VMEM((rows, width), BF16),
            pltpu.VMEM((disks, tokens, width), BF16),
        ]
        + [pltpu.VMEM(v.shape, v.dtype) for v in late]
        + [
            pltpu.VMEM((rows, 128), F32),
            pltpu.VMEM((rows, width), F32),
            pltpu.VMEM((rows, 128), F32),
            pltpu.VMEM((n, d), BF16),
            pltpu.SemaphoreType.DMA((8,)),
            pltpu.SemaphoreType.DMA((disks, len(pieces))),
        ],
        compiler_params=params(67043328),
        cost_estimate=pl.CostEstimate(flops=16 * 10**9, bytes_accessed=10**7, transcendentals=10**6),
        name="disk_attend",
    )(start, extent, everything, *pieces, own, *late)


def device_at(z, y, x, core):
    return (z * 2 + y // 2) * 16 + (y % 2) * 8 + x * 2 + core


def ring(*steps):
    pairs = []
    for z in range(4):
        for y in range(4):
            for x in range(4):
                for core in range(2):
                    axis, by = steps[core]
                    to = [z, y, x]
                    to[axis] = (to[axis] + by) % 4
                    pairs.append((device_at(z, y, x, core), device_at(*to, core)))
    return pairs


def other_core():
    return [(s, s ^ 1) for s in range(128)]


def spread(block, first, second):
    got = []
    for by in (1, 3, 2):
        got.append(lax.ppermute(block, AXES, ring((first, by), (second, by))))
    return got


def gather_tokens(disk_tokens):
    block = jnp.transpose(disk_tokens, (1, 0, 2))
    block = jnp.concatenate([block] + spread(block, 2, 0), axis=1)
    block = lax.optimization_barrier(block)
    block = jnp.concatenate([block] + spread(block, 0, 1), axis=1)
    block = lax.optimization_barrier(block)
    pieces = [block] + spread(block, 1, 2)
    swapped = []
    for piece in pieces:
        swapped.append(lax.ppermute(piece, AXES, other_core()))
    return pieces + swapped


def local(
    mesh_nodes,
    norm_gain,
    w_query,
    w_node_kv,
    obs_rows,
    w_obs_kv,
    obs_owner,
    neighbours,
    neighbour_mask,
    disk_tokens,
    w_disk_kv,
    disk_start,
    disk_extent,
    w_out,
):
    devices = lax.axis_size("lat") * lax.axis_size("lon")
    width = obs_rows.shape[1]
    slots = devices * 8
    send = place(obs_owner.reshape(1, -1), obs_rows, slots)
    got = lax.all_to_all(
        send.reshape(devices, 8, width), AXES, split_axis=0, concat_axis=0, tiled=True
    ).reshape(slots, width)
    everything, own = prep(
        neighbours.T,
        neighbour_mask.T,
        mesh_nodes,
        norm_gain.reshape(1, -1),
        w_query,
        w_node_kv,
        w_disk_kv,
    )
    pieces = gather_tokens(disk_tokens)
    top, total, near = near_attend(got, w_obs_kv, everything, own)
    return disk_attend(
        disk_start, disk_extent, everything, pieces, own, top, total, near, w_disk_kv, w_out, mesh_nodes
    )


def solution(mesh):
    split = P(AXES, None)
    return jax.shard_map(
        local,
        mesh=mesh,
        in_specs=(
            split,
            P(),
            P(),
            P(),
            split,
            P(),
            split,
            split,
            split,
            P(AXES, None, None),
            P(),
            P(),
            P(),
            P(),
        ),
        out_specs=split,
        check_vma=False,
    )
```

```python
import functools

import jax
import jax.numpy as jnp
from jax import lax
from jax.experimental import pallas as pl
from jax.experimental.pallas import tpu as pltpu
from jax.sharding import PartitionSpec as P


HEADS = 8
AXES = ("lat", "lon")
LOG2E = 1.4426950408889634
EMPTY = 65536.0
NEG = -1e30
BIG = 2.0**100
F32 = jnp.float32
BF16 = jnp.bfloat16
NT = (((1,), (1,)), ((), ()))


def shape(dims, dtype):
    return jax.ShapeDtypeStruct(dims, dtype)


def params(grant=60 * 1024 * 1024):
    return pltpu.CompilerParams(vmem_limit_bytes=grant)


HBM = pl.BlockSpec(memory_space=pltpu.HBM)
VMEM = pl.BlockSpec(memory_space=pltpu.VMEM)
SMEM = pl.BlockSpec(memory_space=pltpu.SMEM)


def start_copy(source, target, sem):
    copy = pltpu.make_async_copy(source, target, sem)
    copy.start()
    return copy


def place_kernel(owner_ref, rows_ref, send_ref, held_ref, sems):
    count = rows_ref.shape[0]
    slots = send_ref.shape[0]
    owners = slots // 8
    owner = owner_ref[...]
    hot = jnp.where(lax.broadcasted_iota(jnp.int32, (owners, count), 0) == owner, 1.0, 0.0)
    row = lax.broadcasted_iota(jnp.int32, (count, count), 0)
    col = lax.broadcasted_iota(jnp.int32, (count, count), 1)
    earlier = jnp.where(row < col, 1.0, 0.0).astype(BF16)
    before = jnp.dot(hot.astype(BF16), earlier, preferred_element_type=F32)
    rank = jnp.sum(before * hot, axis=0, keepdims=True)
    slot = owner * 8 + rank.astype(jnp.int32)
    rows = rows_ref[...]
    ones_rows = jnp.ones((count, 128), BF16)
    step = slots // 4
    copies = []
    for i in range(4):
        at = pl.ds(i * step, step)
        ids_col = lax.broadcasted_iota(jnp.int32, (step, count), 0) + i * step
        placing = jnp.where(ids_col == slot, 1.0, 0.0).astype(BF16)
        placed = jnp.dot(placing, rows, preferred_element_type=F32)
        filled = jnp.dot(placing, ones_rows, preferred_element_type=F32)
        filled = jnp.concatenate([filled, filled], axis=1)
        held_ref[at, :] = jnp.where(filled > 0.5, placed, EMPTY).astype(BF16)
        copies.append(start_copy(held_ref.at[at, :], send_ref.at[at, :], sems.at[i]))
    for copy in copies:
        copy.wait()


def place(owner, rows, slots):
    return pl.pallas_call(
        place_kernel,
        out_shape=shape((slots, rows.shape[1]), BF16),
        in_specs=[VMEM, VMEM],
        out_specs=HBM,
        scratch_shapes=[pltpu.VMEM((slots, rows.shape[1]), BF16), pltpu.SemaphoreType.DMA((4,))],
        compiler_params=params(),
        cost_estimate=pl.CostEstimate(flops=10**9, bytes_accessed=10**6, transcendentals=0),
        name="place",
    )(owner, rows)


def one_head(pair, odd):
    lane = lax.broadcasted_iota(jnp.int32, pair.shape, 1)
    keep = lane >= 64 if odd else lane < 64
    return jnp.where(keep, pair.astype(F32), 0.0).astype(pair.dtype)


def prep_kernel(
    near_ref, mark_ref, x_hbm, gain_ref, wq_hbm, wkv_hbm, wd_hbm, all_hbm, own_hbm,
    x_ref, wq_ref, wkv_ref, wd_ref, all_ref, own_ref, list_ref, sems, out_sems,
):
    n, d = x_ref.shape
    slots = 1024
    get_x = start_copy(x_hbm, x_ref, sems.at[0])
    get_wq = start_copy(wq_hbm, wq_ref, sems.at[1])
    get_wkv = start_copy(wkv_hbm, wkv_ref, sems.at[2])
    get_wd = start_copy(wd_hbm, wd_ref, sems.at[3])
    list_ref[...] = jnp.transpose(jnp.where(mark_ref[...] > 0, near_ref[...], -1), (1, 0))
    step = 64

    def body(i, carry):
        start = pl.multiple_of(i * step, step)
        near = list_ref[pl.ds(start, step), :].astype(jnp.int16)
        ids = lax.broadcasted_iota(jnp.int16, (step, slots), 1)
        total = jnp.zeros((step, slots), jnp.int16)
        one = jnp.ones((step, slots), jnp.int16)
        for entry in range(near.shape[1]):
            total = jnp.where(ids == near[:, entry : entry + 1], total + one, total)
        count = total.astype(F32).astype(BF16)
        for j in range(4):
            at = pl.ds(pl.multiple_of((12 + j) * n + start, step), step)
            all_ref[at, :] = count[:, j * 256 : j * 256 + 256]
        return carry

    lax.fori_loop(0, n // step, body, 0)

    def put(block, blocks, sem):
        at = pl.ds(block * n, blocks * n)
        return start_copy(all_ref.at[at, :], all_hbm.at[at, :], out_sems.at[sem])

    puts = [put(12, 4, 0)]
    get_x.wait()
    x = x_ref[...].astype(F32)
    inverse = lax.rsqrt(jnp.mean(x * x, axis=1, keepdims=True) + 1e-06)
    normed = (x * inverse * gain_ref[...]).astype(BF16)
    get_wq.wait()
    query = (jnp.dot(normed, wq_ref[...], preferred_element_type=F32) * 0.125).astype(BF16)
    get_wkv.wait()
    kv = jnp.dot(normed, wkv_ref[...], preferred_element_type=F32).astype(BF16)
    for j in range(2):
        all_ref[pl.ds((8 + j) * n, n), :] = query[:, j * 256 : j * 256 + 256]
        all_ref[pl.ds((10 + j) * n, n), :] = kv[:, d + j * 256 : d + j * 256 + 256]
    puts.append(put(8, 4, 1))
    prod = query.astype(F32) * kv[:, :d].astype(F32)
    lane = lax.broadcasted_iota(jnp.int32, (n, 128), 1)
    own = jnp.zeros((n, 128), F32)
    get_wd.wait()
    for head in range(HEADS):
        lo = head // 2 * 128
        part = jnp.sum(prod[:, head * 64 : head * 64 + 64], axis=1, keepdims=True) * LOG2E
        own = jnp.where(lane == head, part, own)
        lifted = lax.dot_general(
            one_head(query[:, lo : lo + 128], head % 2),
            wd_ref[:, lo : lo + 128],
            NT,
            preferred_element_type=F32,
        )
        all_ref[pl.ds(head * n, n), :] = (lifted * LOG2E).astype(BF16)
        puts.append(put(head, 1, 2 + head))
    own_ref[...] = own
    puts.append(start_copy(own_ref, own_hbm, out_sems.at[2 + HEADS]))
    for copy in puts:
        copy.wait()


def prep(near, mark, x, gain, wq, wkv, wd):
    n, _ = x.shape
    outs = [((16 * n, 256), BF16), ((n, 128), F32)]
    ins = [(v.shape, v.dtype) for v in (x, wq, wkv, wd)]
    return pl.pallas_call(
        prep_kernel,
        out_shape=tuple(shape(*o) for o in outs),
        in_specs=[VMEM, VMEM, HBM, VMEM, HBM, HBM, HBM],
        out_specs=(HBM,) * 2,
        scratch_shapes=[pltpu.VMEM(*v) for v in ins + outs]
        + [
            pltpu.VMEM(near.shape[::-1], jnp.int32),
            pltpu.SemaphoreType.DMA((4,)),
            pltpu.SemaphoreType.DMA((3 + HEADS,)),
        ],
        compiler_params=params(),
        cost_estimate=pl.CostEstimate(flops=8 * 10**9, bytes_accessed=8 * 10**6, transcendentals=0),
        name="prep",
    )(near, mark, x, gain, wq, wkv, wd)


def near_kernel(
    got_hbm, w_hbm, all_hbm, own_hbm, top_hbm, sum_hbm, acc_hbm,
    got_ref, w_ref, query_ref, count_ref, own_ref, value_ref, top_ref, sum_ref, acc_ref,
    key_ref, val_ref, bias_ref, sems,
):
    slots = got_ref.shape[0]
    n, d = query_ref.shape
    get_got = start_copy(got_hbm, got_ref, sems.at[0])
    get_w = start_copy(w_hbm, w_ref, sems.at[1])

    def get_block(block, target, j, sem):
        return start_copy(
            all_hbm.at[pl.ds(block * n, n), :], target.at[:, pl.ds(j * 256, 256)], sems.at[sem]
        )

    for pair in range(HEADS // 2):
        val_ref[pair, :, 128:] = jnp.ones((slots, 128), BF16)
    get_got.wait()
    get_count = [get_block(12 + j, count_ref, j, 8 + j) for j in range(4)]
    gets = [get_block(8 + j, query_ref, j, 2 + j) for j in range(2)]
    gets += [get_block(10 + j, value_ref, j, 4 + j) for j in range(2)]
    gets.append(start_copy(own_hbm, own_ref, sems.at[6]))
    got = got_ref[...]
    absent = got.astype(F32) > 1024.0
    rows = jnp.where(absent, 0.0, got.astype(F32)).astype(BF16)
    ones = jnp.ones((8, 128), BF16)
    empty = lax.dot_general(
        ones, jnp.where(absent[:, :128], 1.0, 0.0).astype(BF16), NT, preferred_element_type=F32
    )[0:1, :]
    get_w.wait()
    kv = jnp.dot(rows, w_ref[...], preferred_element_type=F32).astype(BF16)
    key_ref[...] = kv[:, :d]
    for pair in range(HEADS // 2):
        lo = d + pair * 128
        val_ref[pair, :, :128] = kv[:, lo : lo + 128]
    for copy in get_count:
        copy.wait()
    count = count_ref[...].astype(F32)
    bias_ref[...] = jnp.where((count > 0.0) & (empty < 0.5), jnp.log2(jnp.maximum(count, 1.0)), NEG)
    for copy in gets:
        copy.wait()

    def attend(i, step, exact):
        lane = lax.broadcasted_iota(jnp.int32, (step, 128), 1)
        at = pl.ds(pl.multiple_of(i * step, step), step)
        own = own_ref[at, :]
        tops = own
        sums = jnp.ones((step, 128), F32)
        for pair in range(HEADS // 2):
            lo = pair * 128
            sides = []
            for odd in range(2):
                head = 2 * pair + odd
                scores = lax.dot_general(
                    one_head(query_ref[at, lo : lo + 128], odd),
                    key_ref[:, lo : lo + 128],
                    NT,
                    preferred_element_type=F32,
                )
                scores = scores * LOG2E + bias_ref[at, :]
                shift = own[:, head : head + 1]
                if exact:
                    mine = shift
                    shift = jnp.maximum(jnp.max(scores, axis=1, keepdims=True), mine)
                    self_weight = jnp.exp2(mine - shift).astype(BF16).astype(F32)
                    tops = jnp.where(lane == head, shift, tops)
                else:
                    self_weight = 1.0
                weights = jnp.exp2(scores - shift).astype(BF16)
                part = jnp.dot(weights, val_ref[pair], preferred_element_type=F32)
                sums = jnp.where(lane == head, part[:, 128:] + self_weight, sums)
                sides.append(part[:, :128] + self_weight * value_ref[at, lo : lo + 128].astype(F32))
            acc_ref[at, lo : lo + 128] = jnp.where(lane < 64, sides[0], sides[1])
        top_ref[at, :] = tops
        sum_ref[at, :] = sums

    half = n // 2

    def results(i):
        at = pl.ds(pl.multiple_of(i * half, half), half)
        return [
            pltpu.make_async_copy(source.at[at, :], target.at[at, :], sems.at[12 + 3 * i + j])
            for j, (source, target) in enumerate(
                ((top_ref, top_hbm), (sum_ref, sum_hbm), (acc_ref, acc_hbm))
            )
        ]

    def one_half(i, carry):
        attend(i, half, False)
        for copy in results(i):
            copy.start()
        return carry

    lax.fori_loop(0, 2, one_half, 0)
    for i in range(2):
        for copy in results(i):
            copy.wait()
    worst = jnp.max(jnp.max(sum_ref[...], axis=0, keepdims=True))

    @pl.when(jnp.logical_not(worst < BIG))
    def _():
        lax.fori_loop(0, n // 64, lambda i, carry: attend(i, 64, True) or carry, 0)
        for i in range(2):
            for copy in results(i):
                copy.start()
                copy.wait()


def near_attend(got, w, everything, own):
    n, d = own.shape[0], w.shape[1] // 2
    slots = got.shape[0]
    ins = [(got.shape, BF16), (w.shape, BF16), ((n, d), BF16), ((n, slots), BF16)]
    ins += [(own.shape, F32), ((n, d), BF16)]
    outs = [((n, 128), F32), ((n, 128), F32), ((n, d), F32)]
    return pl.pallas_call(
        near_kernel,
        out_shape=tuple(shape(*o) for o in outs),
        in_specs=[HBM] * 4,
        out_specs=(HBM,) * 3,
        scratch_shapes=[pltpu.VMEM(*v) for v in ins + outs]
        + [
            pltpu.VMEM((slots, d), BF16),
            pltpu.VMEM((HEADS // 2, slots, 256), BF16),
            pltpu.VMEM((n, slots), F32),
            pltpu.SemaphoreType.DMA((18,)),
        ],
        compiler_params=params(67043328),
        cost_estimate=pl.CostEstimate(flops=5 * 10**9, bytes_accessed=5 * 10**6, transcendentals=10**6),
        name="near_attend",
    )(got, w, everything, own)


def disk_kernel(*refs, pieces):
    (start_ref, extent_ref, lifted_hbm), refs = refs[:3], refs[3:]
    piece_hbm, refs = refs[:pieces], refs[pieces:]
    late_hbm, refs = refs[:7], refs[7:]
    out_ref, own_ref, lifted_ref, tok_ref = refs[:4]
    top_ref, sum_ref, near_ref, wd_ref, wout_ref, x_ref = late_refs = refs[4:10]
    shift_ref, acc_ref, den_ref, att_ref, sems, tok_sems = refs[10:]
    own_hbm = late_hbm[0]
    n, d = x_ref.shape
    rows = lifted_ref.shape[0]
    disks, size = piece_hbm[0].shape[:2]

    get_own = start_copy(own_hbm, own_ref, sems.at[0])
    get_lifted = start_copy(lifted_hbm.at[pl.ds(0, rows), :], lifted_ref, sems.at[1])
    here = lax.axis_index("lon")
    sectors = lax.axis_size("lon")

    def seen(disk):
        return lax.rem(here - start_ref[disk] + sectors, sectors) < extent_ref[disk]

    def token_copies(disk):
        return [
            pltpu.make_async_copy(
                piece_hbm[i].at[disk],
                tok_ref.at[disk, pl.ds(i * size, size), :],
                tok_sems.at[disk, i],
            )
            for i in range(pieces)
        ]

    for disk in range(disks):

        @pl.when(seen(disk))
        def _():
            for copy in token_copies(disk):
                copy.start()

    late = [
        start_copy(source, target, sems.at[2 + i])
        for i, (source, target) in enumerate(zip(late_hbm[1:], late_refs))
    ]

    def add_disks(step, unroll, first):
        den_ref[...] = jnp.zeros_like(den_ref)
        acc_ref[...] = jnp.zeros_like(acc_ref)
        if first:
            get_own.wait()
            for head in range(HEADS):
                shift_ref[pl.ds(head * n, n), :] = jnp.broadcast_to(own_ref[:, head : head + 1], (n, 128))
            get_lifted.wait()

        def add_disk(disk, carry):
            @pl.when(seen(disk))
            def _():
                if first:
                    for copy in token_copies(disk):
                        copy.wait()

                def body(i, inner):
                    for u in range(unroll):
                        at = pl.ds(pl.multiple_of((i * unroll + u) * step, step), step)
                        scores = lax.dot_general(
                            lifted_ref[at, :], tok_ref[disk], NT, preferred_element_type=F32
                        )
                        weights = jnp.exp2(scores - shift_ref[at, :1])
                        part = weights[:, :128]
                        for j in range(1, weights.shape[1] // 128):
                            part = part + weights[:, j * 128 : j * 128 + 128]
                        den_ref[at, :] += part
                        acc_ref[at, :] += jnp.dot(
                            weights.astype(BF16), tok_ref[disk], preferred_element_type=F32
                        )
                    return inner

                lax.fori_loop(0, rows // (step * unroll), body, 0)

            return carry

        lax.fori_loop(0, disks, add_disk, 0)

    add_disks(512, 8, True)

    worst = jnp.max(jnp.max(den_ref[...], axis=0, keepdims=True))

    @pl.when(jnp.logical_not(worst < BIG))
    def _():
        def top_disk(disk, carry):
            @pl.when(seen(disk))
            def _():
                def body(i, inner):
                    at = pl.ds(pl.multiple_of(i * 128, 128), 128)
                    scores = lax.dot_general(
                        lifted_ref[at, :], tok_ref[disk], NT, preferred_element_type=F32
                    )
                    best = jnp.max(scores, axis=1, keepdims=True)
                    shift_ref[at, :] = jnp.maximum(shift_ref[at, :], best)
                    return inner

                lax.fori_loop(0, rows // 128, body, 0)

            return carry

        lax.fori_loop(0, disks, top_disk, 0)
        add_disks(128, 1, False)

    for copy in late:
        copy.wait()
    lane = lax.broadcasted_iota(jnp.int32, (n, 128), 1)

    def join(scaled):
        for pair in range(HEADS // 2):
            lo = pair * 128
            sides = []
            for odd in range(2):
                head = 2 * pair + odd
                at = pl.ds(head * n, n)
                wide = acc_ref[at, :]
                part_sum = den_ref[at, :]
                near = near_ref[:, lo : lo + 128]
                near_sum = sum_ref[...]
                if scaled:
                    shift = shift_ref[at, :1]
                    top = top_ref[:, head : head + 1]
                    best = jnp.maximum(shift, top)
                    disk_scale = jnp.exp2(shift - best)
                    near_scale = jnp.exp2(top - best)
                    wide = wide * disk_scale
                    part_sum = part_sum * disk_scale
                    near = near * near_scale
                    near_sum = near_sum * near_scale
                total = jnp.sum(
                    part_sum + jnp.where(lane == head, near_sum, 0.0), axis=1, keepdims=True
                )
                part = jnp.dot(
                    wide.astype(BF16), wd_ref[:, d + lo : d + lo + 128], preferred_element_type=F32
                )
                sides.append((part + near) * (1.0 / total))
            att_ref[:, lo : lo + 128] = jnp.where(lane < 64, sides[0], sides[1]).astype(BF16)

    moved = jnp.max(jnp.max(jnp.abs(top_ref[...] - own_ref[...]), axis=0, keepdims=True))
    same = (worst < BIG) & (moved == 0.0)

    @pl.when(same)
    def _():
        join(False)

    @pl.when(jnp.logical_not(same))
    def _():
        join(True)

    out = jnp.dot(att_ref[...], wout_ref[...], preferred_element_type=F32)
    out_ref[...] = (x_ref[...].astype(F32) + out).astype(BF16)


def disk_attend(start, extent, everything, pieces, own, top, total, near, wd, wout, x):
    n, d = x.shape
    disks = pieces[0].shape[0]
    tokens = sum(piece.shape[1] for piece in pieces)
    rows, width = HEADS * n, wd.shape[0]
    late = (top, total, near, wd, wout, x)
    return pl.pallas_call(
        functools.partial(disk_kernel, pieces=len(pieces)),
        out_shape=shape((n, d), BF16),
        in_specs=[SMEM, SMEM] + [HBM] * (8 + len(pieces)),
        out_specs=VMEM,
        scratch_shapes=[
            pltpu.VMEM(own.shape, F32),
            pltpu.VMEM((rows, width), BF16),
            pltpu.VMEM((disks, tokens, width), BF16),
        ]
        + [pltpu.VMEM(v.shape, v.dtype) for v in late]
        + [
            pltpu.VMEM((rows, 128), F32),
            pltpu.VMEM((rows, width), F32),
            pltpu.VMEM((rows, 128), F32),
            pltpu.VMEM((n, d), BF16),
            pltpu.SemaphoreType.DMA((8,)),
            pltpu.SemaphoreType.DMA((disks, len(pieces))),
        ],
        compiler_params=params(67043328),
        cost_estimate=pl.CostEstimate(flops=16 * 10**9, bytes_accessed=10**7, transcendentals=10**6),
        name="disk_attend",
    )(start, extent, everything, *pieces, own, *late)


def device_at(z, y, x, core):
    return (z * 2 + y // 2) * 16 + (y % 2) * 8 + x * 2 + core


def ring(*steps):
    pairs = []
    for z in range(4):
        for y in range(4):
            for x in range(4):
                for core in range(2):
                    axis, by = steps[core]
                    to = [z, y, x]
                    to[axis] = (to[axis] + by) % 4
                    pairs.append((device_at(z, y, x, core), device_at(*to, core)))
    return pairs


def other_core():
    return [(s, s ^ 1) for s in range(128)]


def spread(block, first, second, order=(1, 3, 2)):
    got = []
    for by in order:
        got.append(lax.ppermute(block, AXES, ring((first, by), (second, by))))
    return got


def gather_tokens(disk_tokens):
    block = jnp.transpose(disk_tokens, (1, 0, 2))
    block = jnp.concatenate([block] + spread(block, 0, 1), axis=1)
    block = lax.optimization_barrier(block)
    block = jnp.concatenate([block] + spread(block, 1, 2), axis=1)
    block = lax.optimization_barrier(block)
    pieces = [block] + spread(block, 2, 0, (2, 3, 1))
    swapped = []
    for piece in pieces:
        swapped.append(lax.ppermute(piece, AXES, other_core()))
    return pieces + swapped


def local(
    mesh_nodes,
    norm_gain,
    w_query,
    w_node_kv,
    obs_rows,
    w_obs_kv,
    obs_owner,
    neighbours,
    neighbour_mask,
    disk_tokens,
    w_disk_kv,
    disk_start,
    disk_extent,
    w_out,
):
    devices = lax.axis_size("lat") * lax.axis_size("lon")
    width = obs_rows.shape[1]
    slots = devices * 8
    send = place(obs_owner.reshape(1, -1), obs_rows, slots)
    got = lax.all_to_all(
        send.reshape(devices, 8, width), AXES, split_axis=0, concat_axis=0, tiled=True
    ).reshape(slots, width)
    everything, own = prep(
        neighbours.T,
        neighbour_mask.T,
        mesh_nodes,
        norm_gain.reshape(1, -1),
        w_query,
        w_node_kv,
        w_disk_kv,
    )
    pieces = gather_tokens(disk_tokens)
    top, total, near = near_attend(got, w_obs_kv, everything, own)
    return disk_attend(
        disk_start, disk_extent, everything, pieces, own, top, total, near, w_disk_kv, w_out, mesh_nodes
    )


def solution(mesh):
    split = P(AXES, None)
    return jax.shard_map(
        local,
        mesh=mesh,
        in_specs=(
            split,
            P(),
            P(),
            P(),
            split,
            P(),
            split,
            split,
            split,
            P(AXES, None, None),
            P(),
            P(),
            P(),
            P(),
        ),
        out_specs=split,
        check_vma=False,
    )
```
